32 devices in a mesh: dp: 8 (over z, y), tensor: 4 (over x, core).
Axes of the slice: x: 2, y: 2, z: 4, core: 2. Of those that a mesh axis runs over, the one named last changes fastest.
Arguments:
- hidden_in: bfloat16 [8192, 768], P('dp'), may hold values from -6 to 6
- segment_ids: int32 [8192], P('dp'), may hold values from 0 to 31, as said below
- query_weight: bfloat16 [768, 768], P(None, 'tensor'), may hold values from -0.21875 to 0.21875
- key_weight: bfloat16 [768, 768], P(None, 'tensor'), may hold values from -0.21875 to 0.21875
- value_weight: bfloat16 [768, 768], P(None, 'tensor'), may hold values from -0.21875 to 0.21875
- output_weight: bfloat16 [768, 768], P('tensor'), may hold values from -0.625 to 0.625
- position_table: float32 [12, 128], P('tensor'), may hold values from -4 to 4
- first_gain: float32 [768], replicated, may hold values from 0.5 to 1.5
- first_shift: float32 [768], replicated, may hold values from -1.5 to 1.5
- up_weight: bfloat16 [768, 3072], P(None, 'tensor'), may hold values from -0.21875 to 0.21875
- up_bias: float32 [3072], P('tensor'), may hold values from -1.5 to 1.5
- down_weight: bfloat16 [3072, 768], P('tensor'), may hold values from -0.109375 to 0.109375
- down_bias: float32 [768], replicated, may hold values from -1.5 to 1.5
- second_gain: float32 [768], replicated, may hold values from 0.5 to 1.5
- second_shift: float32 [768], replicated, may hold values from -1.5 to 1.5
- cotangent: bfloat16 [4096, 768], P('dp'), may hold values from -16 to 16
Outputs:
- pooled_out: bfloat16 [4096, 768], P('dp')
- input_grad: bfloat16 [8192, 768], P('dp', 'tensor')
- query_weight_grad: float32 [768, 768], P(None, 'tensor')
- key_weight_grad: float32 [768, 768], P(None, 'tensor')
- value_weight_grad: float32 [768, 768], P(None, 'tensor')
- output_weight_grad: float32 [768, 768], P('tensor')
- position_table_grad: float32 [12, 128], P('tensor')
- first_gain_grad: float32 [768], replicated
- first_shift_grad: float32 [768], replicated
- up_weight_grad: float32 [768, 3072], P(None, 'tensor')
- up_bias_grad: float32 [3072], P('tensor')
- down_weight_grad: float32 [3072, 768], P('tensor')
- down_bias_grad: float32 [768], replicated
- second_gain_grad: float32 [768], replicated
- second_shift_grad: float32 [768], replicated
The draws below stay inside these ranges and needn't reach their ends.
Inputs may be any that keep to these rules, and one draw needn't show every extreme that they name: `segment_ids`: within each row of 512 tokens the ids start at 0 and never fall; every document starts at an even position of its row; some row holds the largest id.
All inputs are finite; a program needn't handle non-finite values.
Results may differ from the reference program's by a relative error of at most 0.013.
Values may be sent and summed in bfloat16 or wider, within the bound.
A program may use at most 128 MiB of HBM per device.

```python
import math
from functools import partial
import jax
import jax.numpy as jnp
from jax import lax

D = 768
H = 12
DH = 64
FF = 3072
TOK_ROW = 512
REL = 64
TOKENS = 8192
NB = 128


def draw_segment_ids(key, part):
    row_count = TOKENS // TOK_ROW
    half_row = TOK_ROW // 2
    top_id = TOK_ROW // 16 - 1
    start_flags = (jax.random.randint(key, (row_count, half_row), 0, max(2, TOK_ROW // 16)) == 0).astype(jnp.int32)
    column_ids = jnp.arange(half_row, dtype=jnp.int32)[None, :]
    row_numbers = jnp.arange(row_count, dtype=jnp.int32)[:, None]
    dense_flags = (column_ids % 4 == 0).astype(jnp.int32)
    start_flags = jnp.where(row_numbers == 0, dense_flags, start_flags)
    start_flags = jnp.where(column_ids == 0, 0, start_flags)
    local_ids = jnp.minimum(jnp.cumsum(start_flags, axis=1), top_id).astype(jnp.int32)
    return jnp.repeat(local_ids, 2, axis=1).reshape(row_count * TOK_ROW)


def draw_cotangent(key, part):
    row_count = TOKENS // 2
    first_key, second_key = jax.random.split(key, 2)
    row_ramp = jnp.exp(jnp.log(3.0) * jnp.arange(row_count, dtype=jnp.float32) / max(row_count - 1, 1))
    row_rough = jax.random.uniform(second_key, (row_count, 1), jnp.float32, 0.7, 1.3)
    base_draw = jax.random.normal(first_key, (row_count, D), jnp.float32)
    base_draw = jnp.clip(base_draw, -4.0, 4.0)
    return (base_draw * row_ramp[:, None] * row_rough).astype(jnp.bfloat16)


def block_levels(key, shape, shards, smallest, largest):
    def one(dim, parts):
        steps = jax.random.uniform(jax.random.fold_in(jax.random.fold_in(key, 6), dim), (parts,), jnp.float32, smallest / len(shards), largest / len(shards))
        return jnp.repeat(jnp.exp(steps), shape[dim] // parts).reshape((-1,) + (1,) * (len(shape) - dim - 1))

    factor_of = one(*shards[0])
    for cut in shards[1:]:
        factor_of = factor_of * one(*cut)
    return factor_of


def noise(own_key, dims, deviation, limit, shards=(), kind=jnp.bfloat16):
    drawn = deviation * jax.random.normal(own_key, dims, jnp.float32)
    if shards:
        drawn = drawn * block_levels(own_key, dims, shards, -0.22, 0.18)
    return jnp.clip(drawn, -limit, limit).astype(kind)


def setup_inputs(seed: int = 0) -> dict:
    key_of = jax.random.split(jax.random.key(seed), 17)
    return {
        "hidden_in": noise(key_of[0], (TOKENS, D), 1.0, 6.0, ((0, 8),)),
        "segment_ids": draw_segment_ids(jax.random.fold_in(key_of[16], 71), 0),
        "query_weight": noise(key_of[2], (D, H * DH), D ** -0.5, 0.21875, ((1, 4),)),
        "key_weight": noise(key_of[3], (D, H * DH), D ** -0.5, 0.21875, ((1, 4),)),
        "value_weight": noise(key_of[4], (D, H * DH), D ** -0.5, 0.21875, ((1, 4),)),
        "output_weight": noise(key_of[5], (H * DH, D), (H * DH // 8) ** -0.5, 0.625, ((0, 4),)),
        "position_table": noise(key_of[6], (H, NB), 1.0, 4.0, ((0, 4),), jnp.float32),
        "first_gain": jnp.clip(1.0 + 0.1 * jax.random.normal(key_of[7], (D,), jnp.float32), 0.5, 1.5),
        "first_shift": noise(key_of[8], (D,), 0.3, 1.5, (), jnp.float32),
        "up_weight": noise(key_of[9], (D, FF), D ** -0.5, 0.21875, ((1, 4),)),
        "up_bias": noise(key_of[10], (FF,), 0.3, 1.5, ((0, 4),), jnp.float32),
        "down_weight": noise(key_of[11], (FF, D), FF ** -0.5, 0.109375, ((0, 4),)),
        "down_bias": noise(key_of[12], (D,), 0.3, 1.5, (), jnp.float32),
        "second_gain": jnp.clip(1.0 + 0.1 * jax.random.normal(key_of[13], (D,), jnp.float32), 0.5, 1.5),
        "second_shift": noise(key_of[14], (D,), 0.3, 1.5, (), jnp.float32),
        "cotangent": draw_cotangent(jax.random.fold_in(key_of[16], 71), 0),
    }


@jax.custom_vjp
def low(v):
    return lax.optimization_barrier(v.astype(jnp.bfloat16)).astype(jnp.float32)

@jax.custom_vjp
def low_back(v):
    return v

def low_keep(v):
    return (low(v), None)

def low_pass(kept, grad):
    return (grad,)

def back_keep(v):
    return (v, None)

def back_low(kept, grad):
    return (low(grad),)
low.defvjp(low_keep, low_pass)
low_back.defvjp(back_keep, back_low)
EPSILON = 1e-06
NEGATIVE = -1e+30

def matmul(left_matrix, right_matrix):
    return jnp.dot(left_matrix, right_matrix, precision=lax.Precision.HIGHEST, preferred_element_type=jnp.float32)

def layer_norm(values, gain, shift):
    centred = values - lax.optimization_barrier(jnp.mean(values, axis=-1, keepdims=True))
    inverse = lax.rsqrt(lax.optimization_barrier(jnp.mean(centred * centred, axis=-1, keepdims=True)) + EPSILON)
    return centred * inverse * gain + shift

def relative_buckets():
    half_row = TOK_ROW // 2
    offsets = lax.broadcasted_iota(jnp.int32, (half_row, TOK_ROW), 1) - 2 * lax.broadcasted_iota(jnp.int32, (half_row, TOK_ROW), 0)
    return (jnp.clip(offsets, -REL, REL - 1) + REL).astype(jnp.int32)

def forward(segment_ids, hidden_in, query_weight, key_weight, value_weight, output_weight, position_table, first_gain, first_shift, up_weight, up_bias, down_weight, down_bias, second_gain, second_shift):
    token_total = hidden_in.shape[0]
    half_row = TOK_ROW // 2
    row_total = token_total // TOK_ROW
    group_size = math.gcd(row_total, 8)
    blocks = row_total // group_size
    pooled = lax.optimization_barrier(jnp.mean(hidden_in.reshape(token_total // 2, 2, D), axis=1))
    queries = low(low_back(matmul(low(pooled), query_weight)))
    key_rows = low(low_back(matmul(hidden_in, key_weight)))
    values = low(low_back(matmul(hidden_in, value_weight)))
    position_bias = jnp.take(position_table, relative_buckets(), axis=1)
    score_scale = 1.0 / math.sqrt(DH)

    def attend(block_items):
        block_query, block_keys, block_values, block_segments = block_items
        scores = jnp.einsum('gqhd,gkhd->ghqk', block_query, block_keys, precision=lax.Precision.HIGHEST) * score_scale + position_bias[None]
        scores = low_back(scores)
        allowed = block_segments[:, None, 0::2, None] == block_segments[:, None, None, :]
        scores = jnp.where(allowed, scores, NEGATIVE)
        probs = jax.nn.softmax(scores, axis=-1)
        return jnp.einsum('ghqk,gkhd->gqhd', low(probs), block_values, precision=lax.Precision.HIGHEST)
    context = lax.map(jax.checkpoint(attend), (queries.reshape(blocks, group_size, half_row, H, DH), key_rows.reshape(blocks, group_size, TOK_ROW, H, DH), values.reshape(blocks, group_size, TOK_ROW, H, DH), segment_ids.reshape(blocks, group_size, TOK_ROW)))
    context = low(low_back(context.reshape(token_total // 2, H * DH)))
    attended = low_back(matmul(context, output_weight))
    first_out = layer_norm(pooled + attended, first_gain, first_shift)
    preact = low_back(matmul(low(first_out), up_weight) + up_bias)
    activated = low(jax.nn.gelu(preact, approximate=False))
    second = first_out + low_back(matmul(activated, down_weight)) + down_bias
    return layer_norm(second, second_gain, second_shift)

def reference(hidden_in, segment_ids, query_weight, key_weight, value_weight, output_weight, position_table, first_gain, first_shift, up_weight, up_bias, down_weight, down_bias, second_gain, second_shift, cotangent):
    primal, pullback = jax.vjp(partial(forward, segment_ids), hidden_in.astype(jnp.float32), query_weight.astype(jnp.float32), key_weight.astype(jnp.float32), value_weight.astype(jnp.float32), output_weight.astype(jnp.float32), position_table.astype(jnp.float32), first_gain.astype(jnp.float32), first_shift.astype(jnp.float32), up_weight.astype(jnp.float32), up_bias.astype(jnp.float32), down_weight.astype(jnp.float32), down_bias.astype(jnp.float32), second_gain.astype(jnp.float32), second_shift.astype(jnp.float32))
    gradients = pullback(cotangent.astype(jnp.float32))
    return (primal.astype(jnp.bfloat16), gradients[0].astype(jnp.bfloat16), gradients[1], gradients[2], gradients[3], gradients[4], gradients[5], gradients[6], gradients[7], gradients[8], gradients[9], gradients[10], gradients[11], gradients[12], gradients[13])
```

```python
import math
from functools import partial

import jax
import jax.numpy as jnp
from jax import lax
from jax.experimental import pallas as pl
from jax.experimental.pallas import tpu as pltpu
from jax.sharding import PartitionSpec as P

DH = 64
TOK_ROW = 512
HALF_ROW = TOK_ROW // 2
REL = 64
EPSILON = 1e-06
NEGATIVE = -1e30
MESH = pl.DeviceIdType.MESH
F32 = jnp.float32
BF16 = jnp.bfloat16

FIRST_GAIN, FIRST_SHIFT, DOWN_BIAS, SECOND_GAIN, SECOND_SHIFT, UP_BIAS = range(6)
UP_ROW, TABLE_ROW, SMALL_ROWS = 8, 9, 16
P_FIRST_GAIN, P_FIRST_SHIFT, P_UP_BIAS, P_DOWN_BIAS, P_SECOND_GAIN, P_SECOND_SHIFT = range(6)
BAND = 1024
ROLL = 1152


def dot(left, right, left_dim=1, right_dim=0):
    return lax.dot_general(
        left, right, (((left_dim,), (right_dim,)), ((), ())), preferred_element_type=F32
    )


def tiles(count, step, body):
    def one(index, unused):
        body(pl.multiple_of(index * step, step))
        return unused

    lax.fori_loop(0, count // step, one, 0)


def fold(value):
    total = value[0:8]
    for start in range(8, value.shape[0], 8):
        total = total + value[start : start + 8]
    return total


class Copies:
    def __init__(self, send_sems, recv_sems):
        self.send_sems, self.recv_sems, self.used = send_sems, recv_sems, 0

    def start(self, source, target, device):
        copy = pltpu.make_async_remote_copy(
            src_ref=source,
            dst_ref=target,
            send_sem=self.send_sems.at[self.used],
            recv_sem=self.recv_sems.at[self.used],
            device_id=device,
            device_id_type=MESH,
        )
        self.used += 1
        copy.start()
        return copy


class Stream:
    def __init__(
        self, copies, grads, summed, inbox, inbox_row, row, rows, order, extra, me, partner
    ):
        self.copies, self.grads, self.summed, self.inbox = copies, grads, summed, inbox
        self.inbox_row, self.rows, self.pos = inbox_row, rows, row
        self.first, self.count = row, rows
        self.me, self.partner = me, partner
        self.plan = (
            [("half", bit) for bit in order]
            + [("full", bit) for bit in extra]
            + [("back", bit) for bit in reversed(order)]
        )
        self.step, self.pending = 0, None

    def begin(self):
        kind, bit = self.plan[self.step]
        mine = self.me[bit]
        if kind == "half":
            half = self.rows // 2
            self.keep = pl.multiple_of(self.pos + mine * half, half)
            give = pl.multiple_of(self.pos + (1 - mine) * half, half)
            size, source = half, self.grads.at[pl.ds(give, half)]
            target = self.inbox.at[pl.ds(self.inbox_row, half)]
        else:
            size = self.rows
            if kind == "back":
                source = target = self.summed.at[pl.ds(self.pos, size)]
            else:
                source = self.grads.at[pl.ds(self.pos, size)]
                target = self.inbox.at[pl.ds(self.inbox_row, size)]
        self.pending = self.copies.start(source, target, self.partner[bit])
        self.size = size

    def finish(self):
        kind, bit = self.plan[self.step]
        self.pending.wait()
        if kind == "back":
            self.pos = pl.multiple_of(self.pos - self.me[bit] * self.size, self.size)
            self.rows = 2 * self.size
        else:
            if kind == "half":
                self.pos, self.rows = self.keep, self.size
            base, inbox_row, grads, inbox = self.pos, self.inbox_row, self.grads, self.inbox
            result = self.summed if self.plan[self.step + 1][0] == "back" else grads
            step = 32 if self.size % 32 == 0 else 16

            def add(row):
                rows = pl.ds(pl.multiple_of(base + row, step), step)
                arrived = inbox[pl.ds(pl.multiple_of(inbox_row + row, step), step), :]
                result[rows, :] = (grads[rows, :].astype(F32) + arrived.astype(F32)).astype(BF16)

            tiles(self.size, step, add)
            self.inbox_row += self.size
        self.step += 1

    def turn(self):
        if self.pending is not None:
            self.finish()
            self.pending = None
        if self.step < len(self.plan):
            self.begin()
            return True
        return False

    def inbox_rows(self):
        total, rows = 0, self.count
        for kind, unused in self.plan:
            if kind == "half":
                rows //= 2
            if kind != "back":
                total += rows
        return total


def fused(
    cfg,
    seg_ref,
    par_ref,
    tab_ref,
    hid_h,
    wq_h,
    wk_h,
    wv_h,
    wo_h,
    up_h,
    dn_h,
    cot_h,
    po_h,
    ig_h,
    g_h,
    small_h,
    hid,
    wq,
    wk,
    wv,
    wo,
    up,
    dn,
    cot,
    wqT,
    wkT,
    wvT,
    dup,
    segq,
    bias,
    tacc,
    plow,
    pown,
    q,
    qT,
    kT,
    vT,
    score,
    probs,
    problow,
    ds,
    ctx,
    arA,
    arR1,
    arB,
    arR2,
    f1,
    f2,
    f3,
    first_out,
    normed1,
    inv1,
    pre,
    act,
    gp,
    preg,
    sgrad,
    po,
    cg,
    cgT,
    dqT,
    kgT,
    vgT,
    f3dT,
    tp,
    inR1,
    inB,
    inR2,
    igo,
    grads,
    summed,
    inbox,
    acc,
    small,
    smallR,
    in_sems,
    out_sems,
    send_sems,
    recv_sems,
):
    n_dp, heads, rows_per, chunks, width, ff, share, stream_plan = cfg
    half = HALF_ROW // 2
    d = lax.axis_index("dp")
    t = lax.axis_index("tensor")
    core = lax.rem(t, 2)
    side = t // 2
    sib_id = (d, t + 1 - 2 * core)
    cross_id = (d, t + 2 - 4 * side)
    bits = n_dp.bit_length() - 1
    me = [lax.rem(d // (1 << bit), 2) for bit in range(bits)]
    partner = [(d + (1 - 2 * me[bit]) * (1 << bit), t) for bit in range(bits)]
    own = pl.multiple_of(core * half, half)
    away = pl.multiple_of((1 - core) * half, half)

    loads = [
        pltpu.make_async_copy(source, target, in_sems.at[index])
        for index, (source, target) in enumerate(
            [
                (hid_h, hid),
                (wk_h, wk),
                (wv_h, wv),
                (wq_h, wq),
                (wo_h, wo),
                (up_h, up),
                (dn_h, dn),
                (cot_h, cot),
            ]
        )
    ]
    for load in loads:
        load.start()
    barrier = pltpu.get_barrier_semaphore()
    for device in [sib_id, cross_id] + partner:
        pl.semaphore_signal(barrier, inc=1, device_id=device, device_id_type=MESH)

    row_i = lax.broadcasted_iota(jnp.int32, (HALF_ROW, TOK_ROW), 0)
    col_i = lax.broadcasted_iota(jnp.int32, (HALF_ROW, TOK_ROW), 1)
    dup[...] = jnp.where(col_i // 2 == row_i, 1.0, 0.0).astype(BF16)
    evens = jnp.where(col_i == 2 * row_i, 1.0, 0.0).astype(BF16)
    segk = seg_ref[...].astype(F32)
    for g in range(chunks):
        rows = jnp.broadcast_to(segk[g : g + 1], (8, TOK_ROW)).astype(BF16)
        segq[g * HALF_ROW : (g + 1) * HALF_ROW, :] = dot(evens, rows, 1, 1)[:, 0:1]
    for h in range(heads):
        table = jnp.concatenate(
            [
                jnp.broadcast_to(tab_ref[h : h + 1, 0:1], (REL, 512)),
                jnp.broadcast_to(tab_ref[h : h + 1, :], (REL, 2 * REL)),
                jnp.broadcast_to(tab_ref[h : h + 1, 2 * REL - 1 : 2 * REL], (REL, 512)),
            ],
            axis=1,
        )
        bias[h] = pltpu.roll(table, ROLL - 64, 1, stride=2, stride_axis=0)[:, :BAND]
    tacc[...] = jnp.zeros_like(tacc)
    acc[...] = jnp.zeros_like(acc)
    small[...] = jnp.zeros_like(small)

    copies = Copies(send_sems, recv_sems)

    reduce_one, reduce_two = {}, {}

    def reduce_start(which, g):
        slot = which * chunks + g
        reduce_one[slot] = copies.start(arA.at[slot, pl.ds(away, half)], arR1.at[slot], sib_id)

    def reduce_middle(which, g):
        slot = which * chunks + g
        reduce_one[slot].wait()

        def add(row):
            mine = arA[slot, pl.ds(pl.multiple_of(own + row, 32), 32), :].astype(F32)
            arB[slot, pl.ds(row, 32), :] = (
                mine + arR1[slot, pl.ds(row, 32), :].astype(F32)
            ).astype(BF16)

        tiles(half, 32, add)
        reduce_two[slot] = copies.start(arB.at[slot], arR2.at[slot], cross_id)

    def reduced(which, g, row):
        slot = which * chunks + g
        return arB[slot, pl.ds(row, 16), :].astype(F32) + arR2[slot, pl.ds(row, 16), :].astype(F32)

    shares = {}

    def share_start(name, buffer, g):
        rows = buffer.at[pl.ds(pl.multiple_of(g * HALF_ROW + own, half), half)]
        shares[name, g] = copies.start(rows, rows, sib_id)

    def qkv(g):
        tokens = hid[g * TOK_ROW : (g + 1) * TOK_ROW, :]
        pooled = slice(g * HALF_ROW, (g + 1) * HALF_ROW)
        cols = slice(g * TOK_ROW, (g + 1) * TOK_ROW)
        plow[pooled, :] = (dot(dup[...], tokens) * 0.5).astype(BF16)
        mine = hid[pl.ds(pl.multiple_of(g * TOK_ROW + core * HALF_ROW, HALF_ROW), HALF_ROW), :]
        pown[g * half : (g + 1) * half, :] = dot(dup[0:half, 0:HALF_ROW], mine) * 0.5
        kT[:, cols] = dot(wkT[...], tokens, 1, 1).astype(BF16)
        vT[:, cols] = dot(wvT[...], tokens, 1, 1).astype(BF16)
        scale = 1.0 / math.sqrt(DH)
        q[pooled, :] = (dot(plow[pooled, :], wq[...]) * scale).astype(BF16)
        qT[:, pooled] = (dot(wqT[...], plow[pooled, :], 1, 1) * scale).astype(BF16)

    def attend(g):
        pooled = slice(g * HALF_ROW, (g + 1) * HALF_ROW)
        cols = slice(g * TOK_ROW, (g + 1) * TOK_ROW)
        for h in range(heads):
            lanes = slice(h * DH, (h + 1) * DH)
            slot = g * heads + h
            score[...] = dot(q[pooled, lanes], kT[lanes, cols])

            def one(row):
                block = row // 64
                part = pl.multiple_of(lax.rem(row, 64), 32)
                band = pl.ds(pl.multiple_of(512 - 128 * block, 128), TOK_ROW)
                raw = score[pl.ds(row, 32), :] + bias[h, pl.ds(part, 32), band]
                column = segq[pl.ds(pl.multiple_of(g * HALF_ROW + row, 32), 32), :]
                raw = jnp.where(column == segk[g : g + 1], raw, NEGATIVE)
                weights = jnp.exp(raw - jnp.max(raw, axis=-1, keepdims=True))
                prob = weights * (1.0 / jnp.sum(weights, axis=-1, keepdims=True))
                probs[slot, pl.ds(row, 32), :] = prob
                problow[slot, pl.ds(row, 32), :] = prob.astype(BF16)

            tiles(HALF_ROW, 32, one)
            ctx[pooled, lanes] = dot(problow[slot], vT[lanes, cols], 1, 1).astype(BF16)
        arA[g] = dot(ctx[pooled, :], wo[...]).astype(BF16)

    def first_norm(g):
        reduce_two[g].wait()
        gain, shift = par_ref[P_FIRST_GAIN : P_FIRST_GAIN + 1], par_ref[P_FIRST_SHIFT : P_FIRST_SHIFT + 1]

        def one(row):
            here = pl.ds(pl.multiple_of(g * half + row, 16), 16)
            value = pown[here, :] + reduced(0, g, row)
            centred = value - jnp.mean(value, axis=-1, keepdims=True)
            inverse = lax.rsqrt(jnp.mean(centred * centred, axis=-1, keepdims=True) + EPSILON)
            normed = centred * inverse
            out = normed * gain + shift
            normed1[here, :] = normed
            inv1[here, :] = inverse
            first_out[here, :] = out
            f1[pl.ds(pl.multiple_of(g * HALF_ROW + own + row, 16), 16), :] = out.astype(BF16)

        tiles(half, 16, one)
        share_start("f1", f1, g)

    def feed_forward(g):
        shares["f1", g].wait()
        pooled = slice(g * HALF_ROW, (g + 1) * HALF_ROW)
        pre[...] = dot(f1[pooled, :], up[...])
        up_bias = par_ref[P_UP_BIAS : P_UP_BIAS + 1, :ff]

        def one(row):
            value = pre[pl.ds(row, 16), :] + up_bias
            cdf = 0.5 * (1.0 + lax.erf(value * (1.0 / math.sqrt(2.0))))
            density = jnp.exp(-0.5 * value * value) * (1.0 / math.sqrt(2.0 * math.pi))
            here = pl.ds(pl.multiple_of(g * HALF_ROW + row, 16), 16)
            act[here, :] = (value * cdf).astype(BF16)
            gp[here, :] = cdf + value * density

        tiles(HALF_ROW, 16, one)
        arA[chunks + g] = dot(act[pooled, :], dn[...]).astype(BF16)

    def second_norm(g):
        reduce_two[chunks + g].wait()
        gain, shift = par_ref[P_SECOND_GAIN : P_SECOND_GAIN + 1], par_ref[P_SECOND_SHIFT : P_SECOND_SHIFT + 1]
        down_bias = par_ref[P_DOWN_BIAS : P_DOWN_BIAS + 1]

        def one(row):
            here = pl.ds(pl.multiple_of(g * half + row, 16), 16)
            full = pl.ds(pl.multiple_of(g * HALF_ROW + own + row, 16), 16)
            value = first_out[here, :] + reduced(1, g, row) + down_bias
            centred = value - jnp.mean(value, axis=-1, keepdims=True)
            inverse = lax.rsqrt(jnp.mean(centred * centred, axis=-1, keepdims=True) + EPSILON)
            normed = centred * inverse
            po[full, :] = (normed * gain + shift).astype(BF16)
            upstream = cot[full, :].astype(F32)
            scaled = upstream * gain
            grad = inverse * (
                scaled
                - jnp.mean(scaled, axis=-1, keepdims=True)
                - normed * jnp.mean(scaled * normed, axis=-1, keepdims=True)
            )
            sgrad[here, :] = grad
            f2[full, :] = grad.astype(BF16)
            acc[SECOND_GAIN] += fold(upstream * normed)
            acc[SECOND_SHIFT] += fold(upstream)
            acc[DOWN_BIAS] += fold(grad)

        tiles(half, 16, one)
        share_start("f2", f2, g)
        share_start("po", po, g)

    def feed_back(g):
        shares["f2", g].wait()
        pooled = slice(g * HALF_ROW, (g + 1) * HALF_ROW)
        pre[...] = dot(f2[pooled, :], dn[...], 1, 1)

        def one(row):
            here = pl.ds(pl.multiple_of(g * HALF_ROW + row, 16), 16)
            low = (gp[here, :] * pre[pl.ds(row, 16), :]).astype(BF16)
            preg[here, :] = low
            acc[UP_BIAS, :, :ff] += fold(low.astype(F32))

        tiles(HALF_ROW, 16, one)
        arA[2 * chunks + g] = dot(preg[pooled, :], up[...], 1, 1).astype(BF16)

    def first_back(g):
        reduce_two[2 * chunks + g].wait()
        gain = par_ref[P_FIRST_GAIN : P_FIRST_GAIN + 1]

        def one(row):
            here = pl.ds(pl.multiple_of(g * half + row, 16), 16)
            full = pl.ds(pl.multiple_of(g * HALF_ROW + own + row, 16), 16)
            upstream = reduced(2, g, row) + sgrad[here, :]
            normed = normed1[here, :]
            scaled = upstream * gain
            grad = inv1[here, :] * (
                scaled
                - jnp.mean(scaled, axis=-1, keepdims=True)
                - normed * jnp.mean(scaled * normed, axis=-1, keepdims=True)
            )
            f3[full, :] = grad.astype(BF16)
            acc[FIRST_GAIN] += fold(upstream * normed)
            acc[FIRST_SHIFT] += fold(upstream)

        tiles(half, 16, one)
        share_start("f3", f3, g)

    def attend_back(g):
        shares["f3", g].wait()
        pooled = slice(g * HALF_ROW, (g + 1) * HALF_ROW)
        cols = slice(g * TOK_ROW, (g + 1) * TOK_ROW)
        cg[pooled, :] = dot(f3[pooled, :], wo[...], 1, 1).astype(BF16)
        cgT[:, pooled] = dot(wo[...], f3[pooled, :], 1, 1).astype(BF16)
        for h in range(heads):
            lanes = slice(h * DH, (h + 1) * DH)
            slot = g * heads + h
            score[...] = dot(cg[pooled, lanes], vT[lanes, cols])

            def one(row):
                block = row // 64
                part = pl.multiple_of(lax.rem(row, 64), 32)
                band = pl.ds(pl.multiple_of(512 - 128 * block, 128), TOK_ROW)
                prob = probs[slot, pl.ds(row, 32), :]
                prob_grad = score[pl.ds(row, 32), :]
                inner = jnp.sum(prob * prob_grad, axis=-1, keepdims=True)
                grad = prob * (prob_grad - inner)
                ds[pl.ds(row, 32), :] = grad.astype(BF16)
                tacc[h, pl.ds(part, 32), band] += grad

            tiles(HALF_ROW, 32, one)
            scale = 1.0 / math.sqrt(DH)
            dqT[lanes, pooled] = (dot(kT[lanes, cols], ds[...], 1, 1) * scale).astype(BF16)
            kgT[lanes, cols] = dot(qT[lanes, pooled], ds[...]).astype(BF16)
            vgT[lanes, cols] = dot(cgT[lanes, pooled], problow[slot]).astype(BF16)

    in_one, in_two = {}, {}

    def input_part(g):
        pooled = slice(g * HALF_ROW, (g + 1) * HALF_ROW)
        cols = slice(g * TOK_ROW, (g + 1) * TOK_ROW)
        doubled = (dot(dqT[:, pooled], dup[...]) * 0.5).astype(BF16)
        f3dT[...] = (dot(f3[pooled, :], dup[...], 0, 0) * 0.125).astype(BF16)
        for b in range(4):
            rows = slice(b * share, (b + 1) * share)
            total = dot(wk[rows, :], kgT[:, cols]) + dot(wv[rows, :], vgT[:, cols])
            total = total + dot(wq[rows, :], doubled) + f3dT[rows, :].astype(F32)
            tp[g, b] = total.astype(BF16)
        far = core + 2 * (1 - side)
        for index, block in enumerate((1 - core + 2 * (1 - side), 1 - core + 2 * side)):
            in_one[g, index] = copies.start(tp.at[g, block], inR1.at[g, index], sib_id)
        in_one[g, 0].wait()

        def add(row):
            here = pl.ds(row, 32)
            inB[g, here, :] = (
                tp[g, far, here, :].astype(F32) + inR1[g, 0, here, :].astype(F32)
            ).astype(BF16)

        tiles(share, 32, add)
        in_two[g] = copies.start(inB.at[g], inR2.at[g], cross_id)

    def input_end(g):
        in_one[g, 1].wait()
        in_two[g].wait()

        def add(row):
            here = pl.ds(row, 32)
            igo[here, g * TOK_ROW : (g + 1) * TOK_ROW] = (
                tp[g, t, here, :].astype(F32)
                + inR1[g, 1, here, :].astype(F32)
                + inR2[g, here, :].astype(F32)
            ).astype(BF16)

        tiles(share, 32, add)

    loads[0].wait()
    for load in loads[1:4]:
        load.wait()
    wkT[...] = wk[...].T
    wvT[...] = wv[...].T
    wqT[...] = wq[...].T
    qkv(0)
    loads[4].wait()
    attend(0)
    pl.semaphore_wait(barrier, 2 + bits)
    reduce_start(0, 0)
    qkv(1)
    reduce_middle(0, 0)
    attend(1)
    reduce_start(0, 1)
    first_norm(0)
    reduce_middle(0, 1)
    loads[5].wait()
    loads[6].wait()
    loads[7].wait()
    feed_forward(0)
    reduce_start(1, 0)
    first_norm(1)
    reduce_middle(1, 0)
    feed_forward(1)
    reduce_start(1, 1)
    second_norm(0)
    reduce_middle(1, 1)
    feed_back(0)
    reduce_start(2, 0)
    second_norm(1)
    reduce_middle(2, 0)
    feed_back(1)
    reduce_start(2, 1)

    down_rows, up_rows, qkv_rows = stream_plan
    grads[0:ff, :] = dot(act[...], f2[...], 0, 0).astype(BF16)
    inbox_row = [0]

    def open_streams(plan):
        made = []
        for row, rows, order in plan:
            extra = [bit for bit in range(bits) if bit not in order]
            stream = Stream(
                copies, grads, summed, inbox, inbox_row[0], row, rows, order, extra, me, partner
            )
            inbox_row[0] += stream.inbox_rows()
            stream.turn()
            made.append(stream)
        return made

    streams = open_streams(down_rows)
    reduce_middle(2, 1)
    grads[ff : ff + width, :] = dot(f1[...], preg[...], 0, 0).astype(BF16)
    streams += open_streams(up_rows)

    first_back(0)
    attend_back(0)
    for stream in streams:
        stream.turn()
    first_back(1)
    attend_back(1)
    for stream in streams:
        stream.turn()
    base = ff + width
    hw = heads * DH
    grads[base : base + hw, :] = dot(ctx[...], f3[...], 0, 0).astype(BF16)
    grads[base + hw : base + 2 * hw, :] = dot(dqT[...], plow[...]).astype(BF16)
    grads[base + 2 * hw : base + 3 * hw, :] = dot(kgT[...], hid[...]).astype(BF16)
    grads[base + 3 * hw : base + 4 * hw, :] = dot(vgT[...], hid[...]).astype(BF16)
    late = open_streams(qkv_rows)
    for stream in streams:
        stream.turn()

    for index in range(5):
        small[index : index + 1, :] = jnp.sum(acc[index], axis=0, keepdims=True)
    small[UP_ROW : UP_ROW + 1, :] = jnp.sum(acc[UP_BIAS], axis=0, keepdims=True)
    lane = lax.broadcasted_iota(jnp.int32, (1, BAND), 1)
    lane_out = lax.broadcasted_iota(jnp.int32, (1, 2 * REL), 1)
    sub = lax.broadcasted_iota(jnp.int32, (8, BAND), 0)
    for h in range(heads):
        part = tacc[h]
        for size in (32, 16, 8):
            part = part[0:size] + pltpu.roll(part[size : 2 * size], BAND - 2 * size, 1)
        for size in (4, 2, 1):
            part = jnp.where(
                lax.rem(sub // size, 2) == 1, pltpu.roll(part, BAND - 2 * size, 1), part
            )
        part = jnp.sum(part, axis=0, keepdims=True)
        low = jnp.sum(jnp.where(lane <= 448, part, 0.0), axis=1, keepdims=True)
        high = jnp.sum(jnp.where(lane >= 575, part, 0.0), axis=1, keepdims=True)
        middle = pltpu.roll(part, BAND - 448, 1)[:, 0 : 2 * REL]
        middle = jnp.where(lane_out == 0, low, jnp.where(lane_out == 2 * REL - 1, high, middle))
        small[TABLE_ROW + h : TABLE_ROW + h + 1, 0 : 2 * REL] = middle
    copy = copies.start(small.at[pl.ds(0, 8)], smallR.at[0, pl.ds(0, 8)], sib_id)
    input_part(0)
    copy.wait()
    small[0:8, :] = small[0:8, :] + smallR[0, 0:8, :]
    copy = copies.start(small, smallR.at[1], partner[0])
    for stream in streams + late:
        stream.turn()
    input_part(1)
    for bit in range(bits):
        copy.wait()
        small[...] = small[...] + smallR[bit + 1]
        if bit + 1 < bits:
            copy = copies.start(small, smallR.at[bit + 2], partner[bit + 1])
    for stream in streams + late:
        stream.turn()
    input_end(0)
    input_end(1)
    outs = []

    def put(source, target):
        copy = pltpu.make_async_copy(source, target, out_sems.at[len(outs)])
        copy.start()
        outs.append(copy)

    put(igo, ig_h)
    put(small, small_h)
    for g in range(chunks):
        shares["po", g].wait()
    put(po, po_h)
    running = streams + late
    while running:
        left = []
        for stream in running:
            if stream.turn():
                left.append(stream)
            else:
                rows = pl.ds(stream.first, stream.count)
                put(summed.at[rows], g_h.at[rows])
        running = left
    for copy in outs:
        copy.wait()


def local(n_dp, *args):
    (
        hidden_in,
        segment_ids,
        query_weight,
        key_weight,
        value_weight,
        output_weight,
        position_table,
        first_gain,
        first_shift,
        up_weight,
        up_bias,
        down_weight,
        down_bias,
        second_gain,
        second_shift,
        cotangent,
    ) = args
    tokens, width = hidden_in.shape
    chunks = tokens // TOK_ROW
    pooled = tokens // 2
    half = HALF_ROW // 2
    heads = position_table.shape[0]
    hw = heads * DH
    ff = up_weight.shape[1]
    share = width // 4
    order_a, order_b = ((0, 1, 2), (1, 0, 2))
    base = ff + width
    plan = (
        ((0, 512, order_a), (512, ff - 512, order_b)),
        ((ff, 512, order_a), (ff + 512, width - 512, order_a)),
        ((base, 512, order_a), (base + 512, 4 * hw - 512, order_b)),
    )
    bits = n_dp.bit_length() - 1
    total = ff + width + 4 * hw
    par = jnp.stack([first_gain, first_shift, up_bias, down_bias, second_gain, second_shift])
    cfg = (n_dp, heads, HALF_ROW, chunks, width, ff, share, plan)
    vmem = lambda *shape: pltpu.VMEM(shape, BF16)
    wide = lambda *shape: pltpu.VMEM(shape, F32)
    slots = 3 * chunks
    inbox_rows = total * 7 // 8 + (bits - 3) * total // 8
    any_spec = pl.BlockSpec(memory_space=pl.ANY)
    vmem_spec = pl.BlockSpec(memory_space=pltpu.VMEM)
    scratch = [
        vmem(tokens, width),
        vmem(width, hw),
        vmem(width, hw),
        vmem(width, hw),
        vmem(hw, width),
        vmem(width, ff),
        vmem(ff, width),
        vmem(pooled, width),
        vmem(hw, width),
        vmem(hw, width),
        vmem(hw, width),
        vmem(HALF_ROW, TOK_ROW),
        wide(pooled, 1),
        wide(heads, 64, BAND),
        wide(heads, 64, BAND),
        vmem(pooled, width),
        wide(pooled // 2, width),
        vmem(pooled, hw),
        vmem(hw, pooled),
        vmem(hw, tokens),
        vmem(hw, tokens),
        wide(HALF_ROW, TOK_ROW),
        wide(chunks * heads, HALF_ROW, TOK_ROW),
        vmem(chunks * heads, HALF_ROW, TOK_ROW),
        vmem(HALF_ROW, TOK_ROW),
        vmem(pooled, hw),
        vmem(slots, HALF_ROW, width),
        vmem(slots, half, width),
        vmem(slots, half, width),
        vmem(slots, half, width),
        vmem(pooled, width),
        vmem(pooled, width),
        vmem(pooled, width),
        wide(pooled // 2, width),
        wide(pooled // 2, width),
        wide(pooled // 2, 1),
        wide(HALF_ROW, ff),
        vmem(pooled, ff),
        wide(pooled, ff),
        vmem(pooled, ff),
        wide(pooled // 2, width),
        vmem(pooled, width),
        vmem(pooled, hw),
        vmem(hw, pooled),
        vmem(hw, pooled),
        vmem(hw, tokens),
        vmem(hw, tokens),
        vmem(width, TOK_ROW),
        vmem(chunks, 4, share, TOK_ROW),
        vmem(chunks, 2, share, TOK_ROW),
        vmem(chunks, share, TOK_ROW),
        vmem(chunks, share, TOK_ROW),
        vmem(share, tokens),
        vmem(total, width),
        vmem(total, width),
        vmem(inbox_rows, width),
        wide(6, 8, width),
        wide(SMALL_ROWS, width),
        wide(bits + 1, SMALL_ROWS, width),
        pltpu.SemaphoreType.DMA((8,)),
        pltpu.SemaphoreType.DMA((16,)),
        pltpu.SemaphoreType.DMA((120,)),
        pltpu.SemaphoreType.DMA((120,)),
    ]
    pooled_out, input_grad, grads, small = pl.pallas_call(
        partial(fused, cfg),
        name="layer",
        out_shape=(
            jax.ShapeDtypeStruct((pooled, width), BF16),
            jax.ShapeDtypeStruct((share, tokens), BF16),
            jax.ShapeDtypeStruct((total, width), BF16),
            jax.ShapeDtypeStruct((SMALL_ROWS, width), F32),
        ),
        in_specs=[vmem_spec] * 3 + [any_spec] * 8,
        out_specs=(any_spec,) * 4,
        scratch_shapes=scratch,
        compiler_params=pltpu.CompilerParams(
            collective_id=0, has_side_effects=True, vmem_limit_bytes=64_000_000
        ),
    )(
        segment_ids.reshape(chunks, TOK_ROW),
        par,
        position_table,
        hidden_in,
        query_weight,
        key_weight,
        value_weight,
        output_weight,
        up_weight,
        down_weight,
        cotangent,
    )
    wide_grads = grads.astype(F32)
    return (
        pooled_out,
        input_grad.T,
        wide_grads[base + hw : base + 2 * hw].T,
        wide_grads[base + 2 * hw : base + 3 * hw].T,
        wide_grads[base + 3 * hw : base + 4 * hw].T,
        wide_grads[base : base + hw],
        small[TABLE_ROW : TABLE_ROW + heads, : 2 * REL],
        small[FIRST_GAIN],
        small[FIRST_SHIFT],
        wide_grads[ff:base],
        small[UP_ROW, :ff],
        wide_grads[0:ff],
        small[DOWN_BIAS],
        small[SECOND_GAIN],
        small[SECOND_SHIFT],
    )


def solution(mesh):
    return jax.shard_map(
        partial(local, mesh.shape["dp"]),
        mesh=mesh,
        in_specs=(
            P("dp", None),
            P("dp"),
            P(None, "tensor"),
            P(None, "tensor"),
            P(None, "tensor"),
            P("tensor", None),
            P("tensor", None),
            P(),
            P(),
            P(None, "tensor"),
            P("tensor"),
            P("tensor", None),
            P(),
            P(),
            P(),
            P("dp", None),
        ),
        out_specs=(
            P("dp", None),
            P("dp", "tensor"),
            P(None, "tensor"),
            P(None, "tensor"),
            P(None, "tensor"),
            P("tensor", None),
            P("tensor", None),
            P(),
            P(),
            P(None, "tensor"),
            P("tensor"),
            P("tensor", None),
            P(),
            P(),
            P(),
        ),
        check_vma=False,
    )
```

```python
import math
from functools import partial

import jax
import jax.numpy as jnp
from jax import lax
from jax.experimental import pallas as pl
from jax.experimental.pallas import tpu as pltpu
from jax.sharding import PartitionSpec as P

DH = 64
TOK_ROW = 512
HALF_ROW = TOK_ROW // 2
REL = 64
EPSILON = 1e-06
NEGATIVE = -1e30
MESH = pl.DeviceIdType.MESH
F32 = jnp.float32
BF16 = jnp.bfloat16

FIRST_GAIN, FIRST_SHIFT, DOWN_BIAS, SECOND_GAIN, SECOND_SHIFT, UP_BIAS = range(6)
UP_ROW, TABLE_ROW, SMALL_ROWS = 8, 9, 16
BAND = 1024
ROLL = 1152
COPIES = 256
GROUPS = (
    ((("Y", 256), ("Z", 64), ("Z", 128), ("Y", 192), ("Y", 128)), 0),
    ((("Y", 192), ("Y", 128), ("Y", 128), ("Y", 128), ("Y", 192)), 1),
    ((("Z", 64), ("Z", 64), ("Z", 64)), 10),
    ((("Y", 192), ("Y", 192), ("Z", 64), ("Y", 128)), 12),
)
TURNS = [[], [1], [], [0, 1], [], [2, 3], [], [4], [0, 2], [5], [3, 6, 0], [4, 7], [3, 8, 5, 0], [4, 10], [9, 3, 1, 11, 2, 5], [4, 12, 0, 10], [13, 11, 6], [5, 3, 7, 12, 14]]
TAIL = [4, 6, 15, 16, 1, 7, 2, 8, 6, 5, 15, 1, 9, 7, 6, 0, 10, 11, 2, 1, 13, 8, 7, 3, 9, 12, 14, 13, 4, 8, 16, 2, 9, 5, 14, 8, 15, 13, 6, 16, 10, 9, 11, 14, 16, 7, 12, 10, 13, 11, 8, 12, 15, 14, 15, 16, 9, 10, 13, 11, 12, 14, 15, 16]
U_SOFT, U_SBACK, U_NORM, U_GELU = 2, 2, 4, 2


def dot(left, right, left_dim=1, right_dim=0):
    return lax.dot_general(
        left, right, (((left_dim,), (right_dim,)), ((), ())), preferred_element_type=F32
    )


def tiles(count, step, body, unroll=1):
    unroll = math.gcd(unroll, count // step)
    stride = step * unroll

    def one(index, unused):
        for part in range(unroll):
            body(pl.multiple_of(index * stride + part * step, step))
        return unused

    if count == stride:
        one(0, 0)
    else:
        lax.fori_loop(0, count // stride, one, 0)


def fold(value):
    total = value[0:8]
    for start in range(8, value.shape[0], 8):
        total = total + value[start : start + 8]
    return total


class Copy:
    def __init__(self, copy, send, recv):
        self.copy, self.send, self.recv = copy, send, recv

    def start(self):
        if self.send is None:
            self.copy.start()
        else:
            pl.when(self.send)(self.copy.start)

    def wait(self):
        if self.send is None:
            self.copy.wait()
        else:
            pl.when(self.send)(self.copy.wait_send)
            pl.when(self.recv)(self.copy.wait_recv)


class Copies:
    def __init__(self, send_sems, recv_sems):
        self.send_sems, self.recv_sems, self.used = send_sems, recv_sems, 0

    def start(self, source, target, device, send=None, recv=None):
        copy = Copy(
            pltpu.make_async_remote_copy(
                src_ref=source,
                dst_ref=target,
                send_sem=self.send_sems.at[self.used],
                recv_sem=self.recv_sems.at[self.used],
                device_id=device,
                device_id_type=MESH,
            ),
            send,
            recv,
        )
        self.used += 1
        copy.start()
        return copy


class Grid:
    def __init__(self, n_dp, d, t):
        self.bits = n_dp.bit_length() - 1
        self.mine = [lax.rem(d // (1 << bit), 2) for bit in range(self.bits)]
        self.across = [(d + (1 - 2 * self.mine[b]) * (1 << b), t) for b in range(self.bits)]
        self.peers = list(self.across)
        self.plans = {}
        if n_dp == 8:
            z = d // 2
            middle = jnp.logical_or(z == 1, z == 2)
            end = jnp.logical_not(middle)
            upper = z // 2
            facing = (d + (3 - 2 * z) * 2, t)
            self.peers.append(facing)
            everyone = (None, None, None)
            inner = (middle, middle, middle)
            y = ("half", self.across[0], self.mine[0])
            y_back = ("back", self.across[0], self.mine[0])
            gather = ("whole", self.across[1], 0, end, middle, middle)
            spread = ("same", self.across[1], 0, middle, end, middle)
            mid = ("half", facing, upper) + inner
            mid_back = ("back", facing, upper) + inner
            self.plans["Y"] = (
                y + everyone,
                gather,
                mid,
                mid_back,
                spread,
                y_back + everyone,
            )
            self.plans["Z"] = (gather, mid, y + inner, y_back + inner, mid_back, spread)
        else:
            everyone = (None, None, None)
            halving = list(range(min(3, self.bits)))
            plan = [("half", self.across[b], self.mine[b]) + everyone for b in halving]
            plan += [
                ("whole", self.across[b], 0) + everyone for b in range(len(halving), self.bits)
            ]
            plan += [("back", self.across[b], self.mine[b]) + everyone for b in reversed(halving)]
            self.plans["Y"] = self.plans["Z"] = tuple(plan)

    def inbox_rows(self, order, rows):
        total = 0
        for kind, *unused in self.plans[order]:
            if kind == "half":
                rows //= 2
            if kind in ("half", "whole"):
                total += rows
        return total


class Stream:
    def __init__(self, copies, buffers, inbox_row, row, rows, plan):
        self.copies, self.plan = copies, plan
        self.grads, self.summed, self.inbox = buffers
        self.inbox_row, self.rows, self.pos = inbox_row, rows, row
        self.first, self.count = row, rows
        self.step, self.pending = 0, None

    def begin(self):
        kind, device, mine, send, recv, unused = self.plan[self.step]
        size = self.rows
        at = self.pos
        if kind == "half":
            size //= 2
            self.keep = pl.multiple_of(self.pos + mine * size, 16)
            at = pl.multiple_of(self.pos + (1 - mine) * size, 16)
        if kind in ("half", "whole"):
            source = self.grads.at[pl.ds(at, size)]
            target = self.inbox.at[pl.ds(self.inbox_row, size)]
        else:
            source = target = self.summed.at[pl.ds(at, size)]
        self.pending = self.copies.start(source, target, device, send, recv)
        self.size = size

    def finish(self):
        kind, device, mine, send, recv, adds = self.plan[self.step]
        self.pending.wait()
        self.step += 1
        if kind == "back":
            self.pos = pl.multiple_of(self.pos - mine * self.size, 16)
            self.rows = 2 * self.size
        elif kind != "same":
            if kind == "half":
                self.pos, self.rows = self.keep, self.size
            base, inbox_row, grads, inbox = self.pos, self.inbox_row, self.grads, self.inbox
            result = self.summed if self.plan[self.step][0] == "back" else grads
            step = 32 if self.size % 32 == 0 else 16

            def add(row):
                rows = pl.ds(pl.multiple_of(base + row, 16), step)
                arrived = inbox[pl.ds(pl.multiple_of(inbox_row + row, 16), step), :]
                result[rows, :] = (grads[rows, :].astype(F32) + arrived.astype(F32)).astype(BF16)

            def add_all():
                tiles(self.size, step, add, 2)

            if adds is None:
                add_all()
            else:
                pl.when(adds)(add_all)
            self.inbox_row += self.size

    def turn(self):
        if self.pending is not None:
            self.finish()
            self.pending = None
        if self.step < len(self.plan):
            self.begin()
            return True
        return False


def fused(
    cfg,
    seg_ref,
    first_gain,
    first_shift,
    up_bias_in,
    down_bias_in,
    second_gain,
    second_shift,
    tab_ref,
    hid_h,
    wq_h,
    wk_h,
    wv_h,
    wo_h,
    up_h,
    dn_h,
    cot_h,
    po_h,
    ig_h,
    g_h,
    small_h,
    hid,
    wq,
    wk,
    wv,
    wo,
    up,
    dn,
    cot,
    wqT,
    wkT,
    wvT,
    dup,
    segq,
    bias,
    tacc,
    plow,
    pown,
    q,
    qT,
    kT,
    vT,
    score,
    probs,
    problow,
    ds,
    ctx,
    arA,
    arR1,
    arB,
    arR2,
    f1,
    f2,
    f3,
    first_out,
    normed1,
    inv1,
    pre,
    act,
    gp,
    preg,
    sgrad,
    po,
    cg,
    cgT,
    dqT,
    kgT,
    vgT,
    f3dT,
    tp,
    inR1,
    inB,
    inR2,
    igo,
    grads,
    summed,
    inbox,
    acc,
    small,
    smallR,
    in_sems,
    out_sems,
    send_sems,
    recv_sems,
):
    n_dp, heads, rows_per, chunks, width, ff, share, stream_plan = cfg
    half = HALF_ROW // 2
    d = lax.axis_index("dp")
    t = lax.axis_index("tensor")
    core = lax.rem(t, 2)
    side = t // 2
    sib_id = (d, t + 1 - 2 * core)
    cross_id = (d, t + 2 - 4 * side)
    grid = Grid(n_dp, d, t)
    bits = grid.bits
    own = pl.multiple_of(core * half, half)
    away = pl.multiple_of((1 - core) * half, half)

    loads = [
        pltpu.make_async_copy(source, target, in_sems.at[index])
        for index, (source, target) in enumerate(
            [
                (hid_h, hid),
                (wk_h, wkT),
                (wv_h, wvT),
                (wq_h, wqT),
                (wo_h, wo),
                (up_h, up),
                (dn_h, dn),
                (cot_h, cot),
            ]
        )
    ]
    for load in loads[:5]:
        load.start()
    barrier = pltpu.get_barrier_semaphore()
    for device in [sib_id, cross_id] + grid.peers:
        pl.semaphore_signal(barrier, inc=1, device_id=device, device_id_type=MESH)

    row_i = lax.broadcasted_iota(jnp.int32, (HALF_ROW, TOK_ROW), 0)
    col_i = lax.broadcasted_iota(jnp.int32, (HALF_ROW, TOK_ROW), 1)
    dup[...] = jnp.where(col_i // 2 == row_i, 1.0, 0.0).astype(BF16)
    evens = jnp.where(col_i == 2 * row_i, 1.0, 0.0).astype(BF16)
    segk = [
        seg_ref[g * TOK_ROW : (g + 1) * TOK_ROW].astype(F32).reshape(1, TOK_ROW)
        for g in range(chunks)
    ]
    for g in range(chunks):
        rows = jnp.broadcast_to(segk[g], (8, TOK_ROW)).astype(BF16)
        segq[g * HALF_ROW : (g + 1) * HALF_ROW, :] = dot(evens, rows, 1, 1)[:, 0:1]
    for h in range(heads):
        table = jnp.concatenate(
            [
                jnp.broadcast_to(tab_ref[h : h + 1, 0:1], (REL, 512)),
                jnp.broadcast_to(tab_ref[h : h + 1, :], (REL, 2 * REL)),
                jnp.broadcast_to(tab_ref[h : h + 1, 2 * REL - 1 : 2 * REL], (REL, 512)),
            ],
            axis=1,
        )
        bias[h] = pltpu.roll(table, ROLL - 64, 1, stride=2, stride_axis=0)[:, :BAND]
    tacc[...] = jnp.zeros_like(tacc)
    acc[...] = jnp.zeros_like(acc)
    small[...] = jnp.zeros_like(small)

    copies = Copies(send_sems, recv_sems)

    reduce_one, reduce_two = {}, {}

    def reduce_start(which, g):
        slot = which * chunks + g
        reduce_one[slot] = copies.start(arA.at[slot, pl.ds(away, half)], arR1.at[slot], sib_id)

    def reduce_middle(which, g):
        slot = which * chunks + g
        reduce_one[slot].wait()

        def add(row):
            mine = arA[slot, pl.ds(pl.multiple_of(own + row, 32), 32), :].astype(F32)
            arB[slot, pl.ds(row, 32), :] = (
                mine + arR1[slot, pl.ds(row, 32), :].astype(F32)
            ).astype(BF16)

        tiles(half, 32, add, 2)
        reduce_two[slot] = copies.start(arB.at[slot], arR2.at[slot], cross_id)

    def reduced(which, g, row):
        slot = which * chunks + g
        return arB[slot, pl.ds(row, 16), :].astype(F32) + arR2[slot, pl.ds(row, 16), :].astype(F32)

    shares = {}

    def share_start(name, buffer, g):
        rows = buffer.at[pl.ds(pl.multiple_of(g * HALF_ROW + own, half), half)]
        shares[name, g] = copies.start(rows, rows, sib_id)

    def qkv(g):
        tokens = hid[g * TOK_ROW : (g + 1) * TOK_ROW, :]
        pooled = slice(g * HALF_ROW, (g + 1) * HALF_ROW)
        cols = slice(g * TOK_ROW, (g + 1) * TOK_ROW)
        plow[pooled, :] = (dot(dup[...], tokens) * 0.5).astype(BF16)
        mine = hid[pl.ds(pl.multiple_of(g * TOK_ROW + core * HALF_ROW, HALF_ROW), HALF_ROW), :]
        pown[g * half : (g + 1) * half, :] = dot(dup[0:half, 0:HALF_ROW], mine) * 0.5
        kT[:, cols] = dot(wkT[...], tokens, 1, 1).astype(BF16)
        vT[:, cols] = dot(wvT[...], tokens, 1, 1).astype(BF16)
        scale = 1.0 / math.sqrt(DH)
        q[pooled, :] = (dot(plow[pooled, :], wqT[...], 1, 1) * scale).astype(BF16)
        qT[:, pooled] = (dot(wqT[...], plow[pooled, :], 1, 1) * scale).astype(BF16)

    def attend(g):
        pooled = slice(g * HALF_ROW, (g + 1) * HALF_ROW)
        cols = slice(g * TOK_ROW, (g + 1) * TOK_ROW)
        for h in range(heads):
            lanes = slice(h * DH, (h + 1) * DH)
            slot = g * heads + h
            score[...] = dot(q[pooled, lanes], kT[lanes, cols])

            def one(row):
                block = row // 64
                part = pl.multiple_of(lax.rem(row, 64), 32)
                band = pl.ds(pl.multiple_of(512 - 128 * block, 128), TOK_ROW)
                raw = score[pl.ds(row, 32), :] + bias[h, pl.ds(part, 32), band]
                column = segq[pl.ds(pl.multiple_of(g * HALF_ROW + row, 32), 32), :]
                raw = jnp.where(column == segk[g], raw, NEGATIVE)
                weights = jnp.exp(raw - jnp.max(raw, axis=-1, keepdims=True))
                prob = weights * (1.0 / jnp.sum(weights, axis=-1, keepdims=True))
                probs[slot, pl.ds(row, 32), :] = prob
                problow[slot, pl.ds(row, 32), :] = prob.astype(BF16)

            tiles(HALF_ROW, 32, one, U_SOFT)
            ctx[pooled, lanes] = dot(problow[slot], vT[lanes, cols], 1, 1).astype(BF16)
        arA[g] = dot(ctx[pooled, :], wo[...]).astype(BF16)

    def first_norm(g):
        reduce_two[g].wait()
        gain, shift = first_gain[...].reshape(1, width), first_shift[...].reshape(1, width)

        def one(row):
            here = pl.ds(pl.multiple_of(g * half + row, 16), 16)
            value = pown[here, :] + reduced(0, g, row)
            centred = value - jnp.mean(value, axis=-1, keepdims=True)
            inverse = lax.rsqrt(jnp.mean(centred * centred, axis=-1, keepdims=True) + EPSILON)
            normed = centred * inverse
            out = normed * gain + shift
            normed1[here, :] = normed
            inv1[here, :] = inverse
            first_out[here, :] = out
            f1[pl.ds(pl.multiple_of(g * HALF_ROW + own + row, 16), 16), :] = out.astype(BF16)

        tiles(half, 16, one, U_NORM)
        share_start("f1", f1, g)

    def feed_forward(g):
        shares["f1", g].wait()
        pooled = slice(g * HALF_ROW, (g + 1) * HALF_ROW)
        pre[...] = dot(f1[pooled, :], up[...])
        up_bias = up_bias_in[...].reshape(1, ff)

        def one(row):
            value = pre[pl.ds(row, 16), :] + up_bias
            cdf = 0.5 * (1.0 + lax.erf(value * (1.0 / math.sqrt(2.0))))
            density = jnp.exp(-0.5 * value * value) * (1.0 / math.sqrt(2.0 * math.pi))
            here = pl.ds(pl.multiple_of(g * HALF_ROW + row, 16), 16)
            act[here, :] = (value * cdf).astype(BF16)
            gp[here, :] = cdf + value * density

        tiles(HALF_ROW, 16, one, U_GELU)
        arA[chunks + g] = dot(act[pooled, :], dn[...]).astype(BF16)

    def second_norm(g):
        reduce_two[chunks + g].wait()
        gain, shift = second_gain[...].reshape(1, width), second_shift[...].reshape(1, width)
        down_bias = down_bias_in[...].reshape(1, width)

        def one(row):
            here = pl.ds(pl.multiple_of(g * half + row, 16), 16)
            full = pl.ds(pl.multiple_of(g * HALF_ROW + own + row, 16), 16)
            value = first_out[here, :] + reduced(1, g, row) + down_bias
            centred = value - jnp.mean(value, axis=-1, keepdims=True)
            inverse = lax.rsqrt(jnp.mean(centred * centred, axis=-1, keepdims=True) + EPSILON)
            normed = centred * inverse
            po[full, :] = (normed * gain + shift).astype(BF16)
            upstream = cot[full, :].astype(F32)
            scaled = upstream * gain
            grad = inverse * (
                scaled
                - jnp.mean(scaled, axis=-1, keepdims=True)
                - normed * jnp.mean(scaled * normed, axis=-1, keepdims=True)
            )
            sgrad[here, :] = grad
            f2[full, :] = grad.astype(BF16)
            acc[SECOND_GAIN] += fold(upstream * normed)
            acc[SECOND_SHIFT] += fold(upstream)
            acc[DOWN_BIAS] += fold(grad)

        tiles(half, 16, one, U_NORM)
        share_start("f2", f2, g)
        share_start("po", po, g)

    def feed_back(g):
        shares["f2", g].wait()
        pooled = slice(g * HALF_ROW, (g + 1) * HALF_ROW)
        pre[...] = dot(f2[pooled, :], dn[...], 1, 1)

        def one(row):
            here = pl.ds(pl.multiple_of(g * HALF_ROW + row, 16), 16)
            low = (gp[here, :] * pre[pl.ds(row, 16), :]).astype(BF16)
            preg[here, :] = low
            acc[UP_BIAS, :, :ff] += fold(low.astype(F32))

        tiles(HALF_ROW, 16, one, U_GELU)
        arA[2 * chunks + g] = dot(preg[pooled, :], up[...], 1, 1).astype(BF16)

    def first_back(g):
        reduce_two[2 * chunks + g].wait()
        gain = first_gain[...].reshape(1, width)

        def one(row):
            here = pl.ds(pl.multiple_of(g * half + row, 16), 16)
            full = pl.ds(pl.multiple_of(g * HALF_ROW + own + row, 16), 16)
            upstream = reduced(2, g, row) + sgrad[here, :]
            normed = normed1[here, :]
            scaled = upstream * gain
            grad = inv1[here, :] * (
                scaled
                - jnp.mean(scaled, axis=-1, keepdims=True)
                - normed * jnp.mean(scaled * normed, axis=-1, keepdims=True)
            )
            f3[full, :] = grad.astype(BF16)
            acc[FIRST_GAIN] += fold(upstream * normed)
            acc[FIRST_SHIFT] += fold(upstream)

        tiles(half, 16, one, U_NORM)
        share_start("f3", f3, g)

    def attend_back(g, after):
        shares["f3", g].wait()
        pooled = slice(g * HALF_ROW, (g + 1) * HALF_ROW)
        cols = slice(g * TOK_ROW, (g + 1) * TOK_ROW)
        cg[pooled, :] = dot(f3[pooled, :], wo[...], 1, 1).astype(BF16)
        cgT[:, pooled] = dot(wo[...], f3[pooled, :], 1, 1).astype(BF16)
        for h in range(heads):
            lanes = slice(h * DH, (h + 1) * DH)
            slot = g * heads + h
            score[...] = dot(cg[pooled, lanes], vT[lanes, cols])

            def one(row):
                block = row // 64
                part = pl.multiple_of(lax.rem(row, 64), 32)
                band = pl.ds(pl.multiple_of(512 - 128 * block, 128), TOK_ROW)
                prob = probs[slot, pl.ds(row, 32), :]
                prob_grad = score[pl.ds(row, 32), :]
                inner = jnp.sum(prob * prob_grad, axis=-1, keepdims=True)
                grad = prob * (prob_grad - inner)
                ds[pl.ds(row, 32), :] = grad.astype(BF16)
                tacc[h, pl.ds(part, 32), band] += grad

            tiles(HALF_ROW, 32, one, U_SBACK)
            scale = 1.0 / math.sqrt(DH)
            dqT[lanes, pooled] = (dot(kT[lanes, cols], ds[...], 1, 1) * scale).astype(BF16)
            kgT[lanes, cols] = dot(qT[lanes, pooled], ds[...]).astype(BF16)
            vgT[lanes, cols] = dot(cgT[lanes, pooled], problow[slot]).astype(BF16)
            after()

    in_one, in_two = {}, {}

    def input_part(g):
        pooled = slice(g * HALF_ROW, (g + 1) * HALF_ROW)
        cols = slice(g * TOK_ROW, (g + 1) * TOK_ROW)
        doubled = (dot(dqT[:, pooled], dup[...]) * 0.5).astype(BF16)
        f3dT[...] = (dot(f3[pooled, :], dup[...], 0, 0) * 0.125).astype(BF16)
        for b in range(4):
            rows = slice(b * share, (b + 1) * share)
            total = dot(wk[rows, :], kgT[:, cols]) + dot(wv[rows, :], vgT[:, cols])
            total = total + dot(wq[rows, :], doubled) + f3dT[rows, :].astype(F32)
            tp[g, b] = total.astype(BF16)
        far = core + 2 * (1 - side)
        for index, block in enumerate((1 - core + 2 * (1 - side), 1 - core + 2 * side)):
            in_one[g, index] = copies.start(tp.at[g, block], inR1.at[g, index], sib_id)
        in_one[g, 0].wait()

        def add(row):
            here = pl.ds(row, 32)
            inB[g, here, :] = (
                tp[g, far, here, :].astype(F32) + inR1[g, 0, here, :].astype(F32)
            ).astype(BF16)

        tiles(share, 32, add, 2)
        in_two[g] = copies.start(inB.at[g], inR2.at[g], cross_id)

    def input_end(g):
        in_one[g, 1].wait()
        in_two[g].wait()

        def add(row):
            here = pl.ds(row, 32)
            igo[here, g * TOK_ROW : (g + 1) * TOK_ROW] = (
                tp[g, t, here, :].astype(F32)
                + inR1[g, 1, here, :].astype(F32)
                + inR2[g, here, :].astype(F32)
            ).astype(BF16)

        tiles(share, 32, add, 2)

    def small_sums():
        for index in range(5):
            small[index : index + 1, :] = jnp.sum(acc[index], axis=0, keepdims=True)
        small[UP_ROW : UP_ROW + 1, :] = jnp.sum(acc[UP_BIAS], axis=0, keepdims=True)
        lane = lax.broadcasted_iota(jnp.int32, (1, BAND), 1)
        lane_out = lax.broadcasted_iota(jnp.int32, (1, 2 * REL), 1)
        sub = lax.broadcasted_iota(jnp.int32, (8, BAND), 0)
        for h in range(heads):
            part = tacc[h]
            for size in (32, 16, 8):
                part = part[0:size] + pltpu.roll(part[size : 2 * size], BAND - 2 * size, 1)
            for size in (4, 2, 1):
                part = jnp.where(
                    lax.rem(sub // size, 2) == 1, pltpu.roll(part, BAND - 2 * size, 1), part
                )
            part = jnp.sum(part, axis=0, keepdims=True)
            low = jnp.sum(jnp.where(lane <= 448, part, 0.0), axis=1, keepdims=True)
            high = jnp.sum(jnp.where(lane >= 575, part, 0.0), axis=1, keepdims=True)
            middle = pltpu.roll(part, BAND - 448, 1)[:, 0 : 2 * REL]
            middle = jnp.where(
                lane_out == 0, low, jnp.where(lane_out == 2 * REL - 1, high, middle)
            )
            small[TABLE_ROW + h : TABLE_ROW + h + 1, 0 : 2 * REL] = middle

    loads[0].wait()
    for load in loads[1:4]:
        load.wait()
    for load in loads[5:]:
        load.start()
    qkv(0)
    loads[4].wait()
    attend(0)
    pl.semaphore_wait(barrier, 2 + len(grid.peers))
    reduce_start(0, 0)
    qkv(1)
    reduce_middle(0, 0)
    attend(1)
    reduce_start(0, 1)
    first_norm(0)
    reduce_middle(0, 1)
    loads[5].wait()
    loads[6].wait()
    loads[7].wait()
    feed_forward(0)
    reduce_start(1, 0)
    first_norm(1)
    reduce_middle(1, 0)
    feed_forward(1)
    reduce_start(1, 1)
    second_norm(0)
    reduce_middle(1, 1)
    feed_back(0)
    reduce_start(2, 0)
    second_norm(1)
    reduce_middle(2, 0)
    feed_back(1)
    reduce_start(2, 1)

    outs = []

    def put(source, target):
        copy = pltpu.make_async_copy(source, target, out_sems.at[len(outs)])
        copy.start()
        outs.append(copy)

    specs, turns, tail = stream_plan
    streams, state = [], {"block": 0, "inbox": 0}

    def advance(stream):
        if stream.pending is not None and not stream.turn():
            rows = pl.ds(stream.first, stream.count)
            put(summed.at[rows], g_h.at[rows])

    def mark():
        block = state["block"]
        state["block"] += 1
        for row, rows, order, opens in specs:
            if opens == block:
                stream = Stream(
                    copies, (grads, summed, inbox), state["inbox"], row, rows, grid.plans[order]
                )
                state["inbox"] += grid.inbox_rows(order, rows)
                stream.turn()
                streams.append(stream)
        for index in turns[block] if block < len(turns) else ():
            advance(streams[index])

    grads[0:ff, :] = dot(act[...], f2[...], 0, 0).astype(BF16)
    mark()
    reduce_middle(2, 1)
    grads[ff : ff + width, :] = dot(f1[...], preg[...], 0, 0).astype(BF16)
    mark()
    first_back(0)
    wk[...] = wkT[...].T
    wv[...] = wvT[...].T
    wq[...] = wqT[...].T
    mark()
    attend_back(0, mark)
    first_back(1)
    mark()
    attend_back(1, mark)
    base = ff + width
    hw = heads * DH
    grads[base : base + hw, :] = dot(ctx[...], f3[...], 0, 0).astype(BF16)
    mark()
    grads[base + hw : base + 2 * hw, :] = dot(dqT[...], plow[...]).astype(BF16)
    mark()
    grads[base + 2 * hw : base + 3 * hw, :] = dot(kgT[...], hid[...]).astype(BF16)
    grads[base + 3 * hw : base + 4 * hw, :] = dot(vgT[...], hid[...]).astype(BF16)
    mark()
    small_sums()
    copy = copies.start(small.at[pl.ds(0, 8)], smallR.at[0, pl.ds(0, 8)], sib_id)
    mark()
    input_part(0)
    mark()
    copy.wait()
    small[0:8, :] = small[0:8, :] + smallR[0, 0:8, :]
    copy = copies.start(small, smallR.at[1], grid.across[0])
    input_part(1)
    mark()
    for bit in range(bits):
        copy.wait()
        small[...] = small[...] + smallR[bit + 1]
        if bit + 1 < bits:
            copy = copies.start(small, smallR.at[bit + 2], grid.across[bit + 1])
            mark()
    input_end(0)
    input_end(1)
    put(igo, ig_h)
    put(small, small_h)
    for g in range(chunks):
        shares["po", g].wait()
    put(po, po_h)
    order = list(tail)
    while any(stream.pending is not None for stream in streams):
        index = order.pop(0) if order else [s.pending is not None for s in streams].index(True)
        advance(streams[index])
    for copy in outs:
        copy.wait()


def finish_kernel(
    plan, po_h, ig_h, g_h, small_h, po_o, ig_o, q_o, k_o, v_o, wo_o, up_o, dn_o, *rest
):
    tab_o, fg_o, fs_o, ub_o, db_o, sg_o, ss_o, po, ig, low, wide, small, in_sems, out_sems = rest
    targets = (dn_o, up_o, wo_o, q_o, k_o, v_o)
    get_small = pltpu.make_async_copy(small_h, small, in_sems.at[len(plan)])
    get_po = pltpu.make_async_copy(po_h, po, in_sems.at[len(plan) + 1])
    get_ig = pltpu.make_async_copy(ig_h, ig, in_sems.at[len(plan) + 2])
    gets = [
        pltpu.make_async_copy(
            g_h.at[pl.ds(row, rows)], low.at[pl.ds(row, rows)], in_sems.at[index]
        )
        for index, (row, rows, unused, unused_row) in enumerate(plan)
    ]
    for get in gets + [get_po, get_ig, get_small]:
        get.start()
    puts = []

    def put(source, target):
        copy = pltpu.make_async_copy(source, target, out_sems.at[len(puts)])
        copy.start()
        puts.append(copy)

    for get, (row, rows, index, target_row) in zip(gets, plan):
        get.wait()

        def widen(here):
            where = pl.ds(pl.multiple_of(row + here, 32), 32)
            wide[where, :] = low[where, :].astype(F32)

        tiles(rows, 32, widen)
        put(wide.at[pl.ds(row, rows)], targets[index].at[pl.ds(target_row, rows)])
    get_po.wait()
    put(po, po_o)
    get_ig.wait()
    put(ig, ig_o)
    get_small.wait()
    for row, out in (
        (FIRST_GAIN, fg_o),
        (FIRST_SHIFT, fs_o),
        (UP_ROW, ub_o),
        (DOWN_BIAS, db_o),
        (SECOND_GAIN, sg_o),
        (SECOND_SHIFT, ss_o),
    ):
        out[...] = small[row, : out.shape[0]]
    heads = tab_o.shape[0]
    tab_o[...] = small[TABLE_ROW : TABLE_ROW + heads, : 2 * REL]
    for copy in puts:
        copy.wait()


def finish(pooled_out, input_grad, grads, small, heads, ff, width):
    hw = heads * DH
    total = grads.shape[0]
    plan, row = [], 0
    for index, rows in enumerate((ff, width, hw, hw, hw, hw)):
        for start in range(0, rows, 384):
            size = min(384, rows - start)
            plan.append((row + start, size, index, start))
        row += rows
    vector = jax.ShapeDtypeStruct((width,), F32)
    any_spec = pl.BlockSpec(memory_space=pl.ANY)
    vmem_spec = pl.BlockSpec(memory_space=pltpu.VMEM)
    outs = pl.pallas_call(
        partial(finish_kernel, tuple(plan)),
        name="finish",
        out_shape=(
            jax.ShapeDtypeStruct(pooled_out.shape, BF16),
            jax.ShapeDtypeStruct(input_grad.shape, BF16),
            jax.ShapeDtypeStruct((hw, width), F32),
            jax.ShapeDtypeStruct((hw, width), F32),
            jax.ShapeDtypeStruct((hw, width), F32),
            jax.ShapeDtypeStruct((hw, width), F32),
            jax.ShapeDtypeStruct((width, ff), F32),
            jax.ShapeDtypeStruct((ff, width), F32),
            jax.ShapeDtypeStruct((heads, 2 * REL), F32),
            vector,
            vector,
            jax.ShapeDtypeStruct((ff,), F32),
            vector,
            vector,
            vector,
        ),
        in_specs=[any_spec] * 4,
        out_specs=(any_spec,) * 8 + (vmem_spec,) * 7,
        scratch_shapes=[
            pltpu.VMEM(pooled_out.shape, BF16),
            pltpu.VMEM(input_grad.shape, BF16),
            pltpu.VMEM((total, width), BF16),
            pltpu.VMEM((total, width), F32),
            pltpu.VMEM((SMALL_ROWS, width), F32),
            pltpu.SemaphoreType.DMA((len(plan) + 3,)),
            pltpu.SemaphoreType.DMA((len(plan) + 2,)),
        ],
        compiler_params=pltpu.CompilerParams(vmem_limit_bytes=64_000_000),
    )(pooled_out, input_grad, grads, small)
    po, ig, qg, kg, vg, wo, up, dn, tab, fg, fs, ub, db, sg, ss = outs
    return po, ig.T, qg.T, kg.T, vg.T, wo, tab, fg, fs, up, ub, dn, db, sg, ss


def local(n_dp, *args):
    (
        hidden_in,
        segment_ids,
        query_weight,
        key_weight,
        value_weight,
        output_weight,
        position_table,
        first_gain,
        first_shift,
        up_weight,
        up_bias,
        down_weight,
        down_bias,
        second_gain,
        second_shift,
        cotangent,
    ) = args
    tokens, width = hidden_in.shape
    chunks = tokens // TOK_ROW
    pooled = tokens // 2
    half = HALF_ROW // 2
    heads = position_table.shape[0]
    hw = heads * DH
    ff = up_weight.shape[1]
    share = width // 4
    specs, row = [], 0
    for pieces, opens in GROUPS:
        for order, rows in pieces:
            specs.append((row, rows, order, opens))
            row += rows
    plan = (tuple(specs), TURNS, TAIL)
    bits = n_dp.bit_length() - 1
    total = ff + width + 4 * hw
    cfg = (n_dp, heads, HALF_ROW, chunks, width, ff, share, plan)
    vmem = lambda *shape: pltpu.VMEM(shape, BF16)
    wide = lambda *shape: pltpu.VMEM(shape, F32)
    slots = 3 * chunks
    inbox_rows = total * 7 // 4 + max(bits - 3, 0) * total // 8
    any_spec = pl.BlockSpec(memory_space=pl.ANY)
    vmem_spec = pl.BlockSpec(memory_space=pltpu.VMEM)
    scratch = [
        vmem(tokens, width),
        vmem(width, hw),
        vmem(width, hw),
        vmem(width, hw),
        vmem(hw, width),
        vmem(width, ff),
        vmem(ff, width),
        vmem(pooled, width),
        vmem(hw, width),
        vmem(hw, width),
        vmem(hw, width),
        vmem(HALF_ROW, TOK_ROW),
        wide(pooled, 1),
        wide(heads, 64, BAND),
        wide(heads, 64, BAND),
        vmem(pooled, width),
        wide(pooled // 2, width),
        vmem(pooled, hw),
        vmem(hw, pooled),
        vmem(hw, tokens),
        vmem(hw, tokens),
        wide(HALF_ROW, TOK_ROW),
        wide(chunks * heads, HALF_ROW, TOK_ROW),
        vmem(chunks * heads, HALF_ROW, TOK_ROW),
        vmem(HALF_ROW, TOK_ROW),
        vmem(pooled, hw),
        vmem(slots, HALF_ROW, width),
        vmem(slots, half, width),
        vmem(slots, half, width),
        vmem(slots, half, width),
        vmem(pooled, width),
        vmem(pooled, width),
        vmem(pooled, width),
        wide(pooled // 2, width),
        wide(pooled // 2, width),
        wide(pooled // 2, 1),
        wide(HALF_ROW, ff),
        vmem(pooled, ff),
        wide(pooled, ff),
        vmem(pooled, ff),
        wide(pooled // 2, width),
        vmem(pooled, width),
        vmem(pooled, hw),
        vmem(hw, pooled),
        vmem(hw, pooled),
        vmem(hw, tokens),
        vmem(hw, tokens),
        vmem(width, TOK_ROW),
        vmem(chunks, 4, share, TOK_ROW),
        vmem(chunks, 2, share, TOK_ROW),
        vmem(chunks, share, TOK_ROW),
        vmem(chunks, share, TOK_ROW),
        vmem(share, tokens),
        vmem(total, width),
        vmem(total, width),
        vmem(inbox_rows, width),
        wide(6, 8, width),
        wide(SMALL_ROWS, width),
        wide(bits + 1, SMALL_ROWS, width),
        pltpu.SemaphoreType.DMA((8,)),
        pltpu.SemaphoreType.DMA((32,)),
        pltpu.SemaphoreType.DMA((COPIES,)),
        pltpu.SemaphoreType.DMA((COPIES,)),
    ]
    pooled_out, input_grad, grads, small = pl.pallas_call(
        partial(fused, cfg),
        name="layer",
        out_shape=(
            jax.ShapeDtypeStruct((pooled, width), BF16),
            jax.ShapeDtypeStruct((share, tokens), BF16),
            jax.ShapeDtypeStruct((total, width), BF16),
            jax.ShapeDtypeStruct((SMALL_ROWS, width), F32),
        ),
        in_specs=[vmem_spec] * 8 + [any_spec] * 8,
        out_specs=(any_spec,) * 4,
        scratch_shapes=scratch,
        compiler_params=pltpu.CompilerParams(
            collective_id=0, has_side_effects=True, vmem_limit_bytes=64_000_000
        ),
    )(
        segment_ids,
        first_gain,
        first_shift,
        up_bias,
        down_bias,
        second_gain,
        second_shift,
        position_table,
        hidden_in,
        query_weight.T,
        key_weight.T,
        value_weight.T,
        output_weight,
        up_weight,
        down_weight,
        cotangent,
    )
    return finish(pooled_out, input_grad, grads, small, heads, ff, width)


def solution(mesh):
    return jax.shard_map(
        partial(local, mesh.shape["dp"]),
        mesh=mesh,
        in_specs=(
            P("dp", None),
            P("dp"),
            P(None, "tensor"),
            P(None, "tensor"),
            P(None, "tensor"),
            P("tensor", None),
            P("tensor", None),
            P(),
            P(),
            P(None, "tensor"),
            P("tensor"),
            P("tensor", None),
            P(),
            P(),
            P(),
            P("dp", None),
        ),
        out_specs=(
            P("dp", None),
            P("dp", "tensor"),
            P(None, "tensor"),
            P(None, "tensor"),
            P(None, "tensor"),
            P("tensor", None),
            P("tensor", None),
            P(),
            P(),
            P(None, "tensor"),
            P("tensor"),
            P("tensor", None),
            P(),
            P(),
            P(),
        ),
        check_vma=False,
    )
```

```python
import math
from functools import partial

import jax
import jax.numpy as jnp
from jax import lax
from jax.experimental import pallas as pl
from jax.experimental.pallas import tpu as pltpu
from jax.sharding import PartitionSpec as P

DH = 64
TOK_ROW = 512
HALF_ROW = TOK_ROW // 2
REL = 64
EPSILON = 1e-06
NEGATIVE = -1e30
MESH = pl.DeviceIdType.MESH
F32 = jnp.float32
BF16 = jnp.bfloat16

FIRST_GAIN, FIRST_SHIFT, DOWN_BIAS, SECOND_GAIN, SECOND_SHIFT, UP_BIAS = range(6)
UP_ROW, TABLE_ROW, SMALL_ROWS = 8, 9, 16
BAND = 1024
ROLL = 1152
SENDS = 28
RECEIVES = 24
GROUPS = (
    ((("Y", 256), ("Z", 64), ("Z", 128), ("Y", 192), ("Y", 128)), 0),
    ((("Y", 192), ("Y", 128), ("Y", 128), ("Y", 128), ("Y", 192)), 1),
    ((("Z", 64), ("Z", 64), ("Z", 64)), 10),
    ((("Y", 192), ("Y", 192), ("Z", 64), ("Y", 128)), 12),
)
TURNS = [[], [1], [], [0, 1], [], [2, 3], [], [4], [0, 2], [5], [3, 6, 0], [4, 7], [3, 8, 5, 0], [4, 10], [9, 3, 1, 11, 2, 5], [4, 12, 0, 10], [13, 11, 6], [5, 3, 7, 12, 14]]
TAIL = [4, 6, 15, 16, 1, 7, 2, 8, 6, 5, 15, 1, 9, 7, 6, 0, 10, 11, 2, 1, 13, 8, 7, 3, 9, 12, 14, 13, 4, 8, 16, 2, 9, 5, 14, 8, 15, 13, 6, 16, 10, 9, 11, 14, 16, 7, 12, 10, 13, 11, 8, 12, 15, 14, 15, 16, 9, 10, 13, 11, 12, 14, 15, 16]
U_SOFT, U_SBACK, U_NORM, U_GELU = 2, 2, 4, 2


def dot(left, right, left_dim=1, right_dim=0):
    return lax.dot_general(
        left, right, (((left_dim,), (right_dim,)), ((), ())), preferred_element_type=F32
    )


def tiles(count, step, body, unroll=1):
    unroll = math.gcd(unroll, count // step)
    stride = step * unroll

    def one(index, unused):
        for part in range(unroll):
            body(pl.multiple_of(index * stride + part * step, step))
        return unused

    if count == stride:
        one(0, 0)
    else:
        lax.fori_loop(0, count // stride, one, 0)


def fold(value):
    total = value[0:8]
    for start in range(8, value.shape[0], 8):
        total = total + value[start : start + 8]
    return total


class Copy:
    def __init__(self, copy, send, recv, free):
        self.copy, self.send, self.recv, self.free = copy, send, recv, free

    def start(self):
        if self.send is None:
            self.copy.start()
        else:
            pl.when(self.send)(self.copy.start)

    def wait(self):
        if self.send is None:
            self.copy.wait()
        else:
            pl.when(self.send)(self.copy.wait_send)
            pl.when(self.recv)(self.copy.wait_recv)
        self.free()


class Copies:
    def __init__(self, send_sems, recv_sems):
        self.send_sems, self.recv_sems = send_sems, recv_sems
        self.idle, self.keys = list(range(SENDS)), {}

    def start(self, key, source, target, device, send=None, recv=None):
        index = self.idle.pop(0)
        copy = Copy(
            pltpu.make_async_remote_copy(
                src_ref=source,
                dst_ref=target,
                send_sem=self.send_sems.at[index],
                recv_sem=self.recv_sems.at[self.keys.setdefault(key, len(self.keys))],
                device_id=device,
                device_id_type=MESH,
            ),
            send,
            recv,
            lambda: self.idle.append(index),
        )
        copy.start()
        return copy


class Grid:
    def __init__(self, n_dp, d, t):
        self.bits = n_dp.bit_length() - 1
        self.mine = [lax.rem(d // (1 << bit), 2) for bit in range(self.bits)]
        self.across = [(d + (1 - 2 * self.mine[b]) * (1 << b), t) for b in range(self.bits)]
        self.peers = list(self.across)
        self.plans = {}
        if n_dp == 8:
            z = d // 2
            middle = jnp.logical_or(z == 1, z == 2)
            end = jnp.logical_not(middle)
            upper = z // 2
            facing = (d + (3 - 2 * z) * 2, t)
            self.peers.append(facing)
            everyone = (None, None, None, "y")
            inner = (middle, middle, middle)
            y = ("half", self.across[0], self.mine[0])
            y_back = ("back", self.across[0], self.mine[0])
            gather = ("whole", self.across[1], 0, end, middle, middle, "z")
            spread = ("same", self.across[1], 0, middle, end, middle, "z")
            mid = ("half", facing, upper) + inner + ("mid",)
            mid_back = ("back", facing, upper) + inner + ("mid_back",)
            y_inner = inner + ("y",)
            y_out = ("y_back",)
            self.plans["Y"] = (
                y + everyone,
                gather,
                mid,
                mid_back,
                spread,
                y_back + everyone[:3] + y_out,
            )
            self.plans["Z"] = (gather, mid, y + y_inner, y_back + inner + y_out, mid_back, spread)
        else:
            everyone = (None, None, None)
            halving = list(range(min(3, self.bits)))
            plan = [("half", self.across[b], self.mine[b]) + everyone + (b,) for b in halving]
            plan += [
                ("whole", self.across[b], 0) + everyone + (b,)
                for b in range(len(halving), self.bits)
            ]
            plan += [
                ("back", self.across[b], self.mine[b]) + everyone + (self.bits + b,)
                for b in reversed(halving)
            ]
            self.plans["Y"] = self.plans["Z"] = tuple(plan)

    def inbox_rows(self, order, rows):
        total = 0
        for kind, *unused in self.plans[order]:
            if kind == "half":
                rows //= 2
            if kind in ("half", "whole"):
                total += rows
        return total


class Stream:
    def __init__(self, copies, buffers, inbox_row, row, rows, plan):
        self.copies, self.plan = copies, plan
        self.grads, self.summed, self.inbox = buffers
        self.inbox_row, self.rows, self.pos = inbox_row, rows, row
        self.first, self.count = row, rows
        self.step, self.pending = 0, None

    def begin(self):
        kind, device, mine, send, recv, unused, link = self.plan[self.step]
        size = self.rows
        at = self.pos
        if kind == "half":
            size //= 2
            self.keep = pl.multiple_of(self.pos + mine * size, 16)
            at = pl.multiple_of(self.pos + (1 - mine) * size, 16)
        if kind in ("half", "whole"):
            source = self.grads.at[pl.ds(at, size)]
            target = self.inbox.at[pl.ds(self.inbox_row, size)]
        else:
            source = target = self.summed.at[pl.ds(at, size)]
        self.pending = self.copies.start((self.first, link), source, target, device, send, recv)
        self.size = size

    def finish(self):
        kind, device, mine, send, recv, adds, link = self.plan[self.step]
        self.pending.wait()
        self.step += 1
        if kind == "back":
            self.pos = pl.multiple_of(self.pos - mine * self.size, 16)
            self.rows = 2 * self.size
        elif kind != "same":
            if kind == "half":
                self.pos, self.rows = self.keep, self.size
            base, inbox_row, grads, inbox = self.pos, self.inbox_row, self.grads, self.inbox
            result = self.summed if self.plan[self.step][0] == "back" else grads
            step = 32 if self.size % 32 == 0 else 16

            def add(row):
                rows = pl.ds(pl.multiple_of(base + row, 16), step)
                arrived = inbox[pl.ds(pl.multiple_of(inbox_row + row, 16), step), :]
                result[rows, :] = (grads[rows, :].astype(F32) + arrived.astype(F32)).astype(BF16)

            def add_all():
                tiles(self.size, step, add, 2)

            if adds is None:
                add_all()
            else:
                pl.when(adds)(add_all)
            self.inbox_row += self.size

    def turn(self):
        if self.pending is not None:
            self.finish()
            self.pending = None
        if self.step < len(self.plan):
            self.begin()
            return True
        return False


def fused(
    cfg,
    seg_h,
    first_gain_h,
    first_shift_h,
    up_bias_h,
    down_bias_h,
    second_gain_h,
    second_shift_h,
    tab_h,
    hid_h,
    wq_h,
    wk_h,
    wv_h,
    wo_h,
    up_h,
    dn_h,
    cot_h,
    po_h,
    ig_h,
    g_h,
    small_h,
    seg_ref,
    first_gain,
    first_shift,
    up_bias_in,
    down_bias_in,
    second_gain,
    second_shift,
    tab_ref,
    hid,
    wq,
    wk,
    wv,
    wo,
    up,
    dn,
    cot,
    wqT,
    wkT,
    wvT,
    dup,
    segq,
    bias,
    tacc,
    plow,
    pown,
    q,
    qT,
    kT,
    vT,
    score,
    probs,
    problow,
    ds,
    ctx,
    arA,
    arR1,
    arB,
    arR2,
    f1,
    f2,
    f3,
    first_out,
    normed1,
    inv1,
    pre,
    act,
    gp,
    preg,
    sgrad,
    po,
    cg,
    cgT,
    dqT,
    kgT,
    vgT,
    f3dT,
    tp,
    inR1,
    inB,
    inR2,
    igo,
    grads,
    summed,
    inbox,
    acc,
    small,
    smallR,
    in_sems,
    out_sems,
    send_sems,
    recv_sems,
):
    n_dp, heads, rows_per, chunks, width, ff, share, stream_plan = cfg
    half = HALF_ROW // 2
    d = lax.axis_index("dp")
    t = lax.axis_index("tensor")
    core = lax.rem(t, 2)
    side = t // 2
    sib_id = (d, t + 1 - 2 * core)
    cross_id = (d, t + 2 - 4 * side)
    grid = Grid(n_dp, d, t)
    bits = grid.bits
    own = pl.multiple_of(core * half, half)
    away = pl.multiple_of((1 - core) * half, half)

    loads = [
        pltpu.make_async_copy(source, target, in_sems.at[index])
        for index, (source, target) in enumerate(
            [
                (hid_h, hid),
                (wk_h, wkT),
                (wv_h, wvT),
                (wq_h, wqT),
                (wo_h, wo),
                (up_h, up),
                (dn_h, dn),
                (cot_h, cot),
                (seg_h, seg_ref),
                (tab_h, tab_ref),
                (first_gain_h, first_gain),
                (first_shift_h, first_shift),
                (up_bias_h, up_bias_in),
                (down_bias_h, down_bias_in),
                (second_gain_h, second_gain),
                (second_shift_h, second_shift),
            ]
        )
    ]
    early, vectors, late = loads[:5], loads[8:], loads[5:8]
    for load in vectors[:2] + early:
        load.start()
    barrier = pltpu.get_barrier_semaphore()
    for device in [sib_id, cross_id] + grid.peers:
        pl.semaphore_signal(barrier, inc=1, device_id=device, device_id_type=MESH)

    row_i = lax.broadcasted_iota(jnp.int32, (HALF_ROW, TOK_ROW), 0)
    col_i = lax.broadcasted_iota(jnp.int32, (HALF_ROW, TOK_ROW), 1)
    dup[...] = jnp.where(col_i // 2 == row_i, 1.0, 0.0).astype(BF16)
    evens = jnp.where(col_i == 2 * row_i, 1.0, 0.0).astype(BF16)
    vectors[0].wait()
    segk = [
        seg_ref[g * TOK_ROW : (g + 1) * TOK_ROW].astype(F32).reshape(1, TOK_ROW)
        for g in range(chunks)
    ]
    for g in range(chunks):
        rows = jnp.broadcast_to(segk[g], (8, TOK_ROW)).astype(BF16)
        segq[g * HALF_ROW : (g + 1) * HALF_ROW, :] = dot(evens, rows, 1, 1)[:, 0:1]
    vectors[1].wait()
    for h in range(heads):
        table = jnp.concatenate(
            [
                jnp.broadcast_to(tab_ref[h : h + 1, 0:1], (REL, 512)),
                jnp.broadcast_to(tab_ref[h : h + 1, :], (REL, 2 * REL)),
                jnp.broadcast_to(tab_ref[h : h + 1, 2 * REL - 1 : 2 * REL], (REL, 512)),
            ],
            axis=1,
        )
        bias[h] = pltpu.roll(table, ROLL - 64, 1, stride=2, stride_axis=0)[:, :BAND]
    tacc[...] = jnp.zeros_like(tacc)
    acc[...] = jnp.zeros_like(acc)
    small[...] = jnp.zeros_like(small)

    copies = Copies(send_sems, recv_sems)

    reduce_one, reduce_two = {}, {}

    def reduce_start(which, g):
        slot = which * chunks + g
        reduce_one[slot] = copies.start(("one", g), arA.at[slot, pl.ds(away, half)], arR1.at[slot], sib_id)

    def reduce_middle(which, g):
        slot = which * chunks + g
        reduce_one[slot].wait()

        def add(row):
            mine = arA[slot, pl.ds(pl.multiple_of(own + row, 32), 32), :].astype(F32)
            arB[slot, pl.ds(row, 32), :] = (
                mine + arR1[slot, pl.ds(row, 32), :].astype(F32)
            ).astype(BF16)

        tiles(half, 32, add, 2)
        reduce_two[slot] = copies.start(("two", g, which % 2), arB.at[slot], arR2.at[slot], cross_id)

    def reduced(which, g, row):
        slot = which * chunks + g
        return arB[slot, pl.ds(row, 16), :].astype(F32) + arR2[slot, pl.ds(row, 16), :].astype(F32)

    shares = {}

    def share_start(name, buffer, g):
        rows = buffer.at[pl.ds(pl.multiple_of(g * HALF_ROW + own, half), half)]
        key = ("po" if name == "po" else "share", g)
        shares[name, g] = copies.start(key, rows, rows, sib_id)

    def qkv(g):
        tokens = hid[g * TOK_ROW : (g + 1) * TOK_ROW, :]
        pooled = slice(g * HALF_ROW, (g + 1) * HALF_ROW)
        cols = slice(g * TOK_ROW, (g + 1) * TOK_ROW)
        plow[pooled, :] = (dot(dup[...], tokens) * 0.5).astype(BF16)
        mine = hid[pl.ds(pl.multiple_of(g * TOK_ROW + core * HALF_ROW, HALF_ROW), HALF_ROW), :]
        pown[g * half : (g + 1) * half, :] = dot(dup[0:half, 0:HALF_ROW], mine) * 0.5
        kT[:, cols] = dot(wkT[...], tokens, 1, 1).astype(BF16)
        vT[:, cols] = dot(wvT[...], tokens, 1, 1).astype(BF16)
        scale = 1.0 / math.sqrt(DH)
        q[pooled, :] = (dot(plow[pooled, :], wqT[...], 1, 1) * scale).astype(BF16)
        qT[:, pooled] = (dot(wqT[...], plow[pooled, :], 1, 1) * scale).astype(BF16)

    def attend(g):
        pooled = slice(g * HALF_ROW, (g + 1) * HALF_ROW)
        cols = slice(g * TOK_ROW, (g + 1) * TOK_ROW)
        for h in range(heads):
            lanes = slice(h * DH, (h + 1) * DH)
            slot = g * heads + h
            score[...] = dot(q[pooled, lanes], kT[lanes, cols])

            def one(row):
                block = row // 64
                part = pl.multiple_of(lax.rem(row, 64), 32)
                band = pl.ds(pl.multiple_of(512 - 128 * block, 128), TOK_ROW)
                raw = score[pl.ds(row, 32), :] + bias[h, pl.ds(part, 32), band]
                column = segq[pl.ds(pl.multiple_of(g * HALF_ROW + row, 32), 32), :]
                raw = jnp.where(column == segk[g], raw, NEGATIVE)
                weights = jnp.exp(raw - jnp.max(raw, axis=-1, keepdims=True))
                prob = weights * (1.0 / jnp.sum(weights, axis=-1, keepdims=True))
                probs[slot, pl.ds(row, 32), :] = prob
                problow[slot, pl.ds(row, 32), :] = prob.astype(BF16)

            tiles(HALF_ROW, 32, one, U_SOFT)
            ctx[pooled, lanes] = dot(problow[slot], vT[lanes, cols], 1, 1).astype(BF16)
        arA[g] = dot(ctx[pooled, :], wo[...]).astype(BF16)

    def first_norm(g):
        reduce_two[g].wait()
        gain, shift = first_gain[...].reshape(1, width), first_shift[...].reshape(1, width)

        def one(row):
            here = pl.ds(pl.multiple_of(g * half + row, 16), 16)
            value = pown[here, :] + reduced(0, g, row)
            centred = value - jnp.mean(value, axis=-1, keepdims=True)
            inverse = lax.rsqrt(jnp.mean(centred * centred, axis=-1, keepdims=True) + EPSILON)
            normed = centred * inverse
            out = normed * gain + shift
            normed1[here, :] = normed
            inv1[here, :] = inverse
            first_out[here, :] = out
            f1[pl.ds(pl.multiple_of(g * HALF_ROW + own + row, 16), 16), :] = out.astype(BF16)

        tiles(half, 16, one, U_NORM)
        share_start("f1", f1, g)

    def feed_forward(g):
        shares["f1", g].wait()
        pooled = slice(g * HALF_ROW, (g + 1) * HALF_ROW)
        pre[...] = dot(f1[pooled, :], up[...])
        up_bias = up_bias_in[...].reshape(1, ff)

        def one(row):
            value = pre[pl.ds(row, 16), :] + up_bias
            cdf = 0.5 * (1.0 + lax.erf(value * (1.0 / math.sqrt(2.0))))
            density = jnp.exp(-0.5 * value * value) * (1.0 / math.sqrt(2.0 * math.pi))
            here = pl.ds(pl.multiple_of(g * HALF_ROW + row, 16), 16)
            act[here, :] = (value * cdf).astype(BF16)
            gp[here, :] = cdf + value * density

        tiles(HALF_ROW, 16, one, U_GELU)
        arA[chunks + g] = dot(act[pooled, :], dn[...]).astype(BF16)

    def second_norm(g):
        reduce_two[chunks + g].wait()
        gain, shift = second_gain[...].reshape(1, width), second_shift[...].reshape(1, width)
        down_bias = down_bias_in[...].reshape(1, width)

        def one(row):
            here = pl.ds(pl.multiple_of(g * half + row, 16), 16)
            full = pl.ds(pl.multiple_of(g * HALF_ROW + own + row, 16), 16)
            value = first_out[here, :] + reduced(1, g, row) + down_bias
            centred = value - jnp.mean(value, axis=-1, keepdims=True)
            inverse = lax.rsqrt(jnp.mean(centred * centred, axis=-1, keepdims=True) + EPSILON)
            normed = centred * inverse
            po[full, :] = (normed * gain + shift).astype(BF16)
            upstream = cot[full, :].astype(F32)
            scaled = upstream * gain
            grad = inverse * (
                scaled
                - jnp.mean(scaled, axis=-1, keepdims=True)
                - normed * jnp.mean(scaled * normed, axis=-1, keepdims=True)
            )
            sgrad[here, :] = grad
            f2[full, :] = grad.astype(BF16)
            acc[SECOND_GAIN] += fold(upstream * normed)
            acc[SECOND_SHIFT] += fold(upstream)
            acc[DOWN_BIAS] += fold(grad)

        tiles(half, 16, one, U_NORM)
        share_start("f2", f2, g)
        share_start("po", po, g)

    def feed_back(g):
        shares["f2", g].wait()
        pooled = slice(g * HALF_ROW, (g + 1) * HALF_ROW)
        pre[...] = dot(f2[pooled, :], dn[...], 1, 1)

        def one(row):
            here = pl.ds(pl.multiple_of(g * HALF_ROW + row, 16), 16)
            low = (gp[here, :] * pre[pl.ds(row, 16), :]).astype(BF16)
            preg[here, :] = low
            acc[UP_BIAS, :, :ff] += fold(low.astype(F32))

        tiles(HALF_ROW, 16, one, U_GELU)
        arA[2 * chunks + g] = dot(preg[pooled, :], up[...], 1, 1).astype(BF16)

    def first_back(g):
        reduce_two[2 * chunks + g].wait()
        gain = first_gain[...].reshape(1, width)

        def one(row):
            here = pl.ds(pl.multiple_of(g * half + row, 16), 16)
            full = pl.ds(pl.multiple_of(g * HALF_ROW + own + row, 16), 16)
            upstream = reduced(2, g, row) + sgrad[here, :]
            normed = normed1[here, :]
            scaled = upstream * gain
            grad = inv1[here, :] * (
                scaled
                - jnp.mean(scaled, axis=-1, keepdims=True)
                - normed * jnp.mean(scaled * normed, axis=-1, keepdims=True)
            )
            f3[full, :] = grad.astype(BF16)
            acc[FIRST_GAIN] += fold(upstream * normed)
            acc[FIRST_SHIFT] += fold(upstream)

        tiles(half, 16, one, U_NORM)
        share_start("f3", f3, g)

    def attend_back(g, after):
        shares["f3", g].wait()
        pooled = slice(g * HALF_ROW, (g + 1) * HALF_ROW)
        cols = slice(g * TOK_ROW, (g + 1) * TOK_ROW)
        cg[pooled, :] = dot(f3[pooled, :], wo[...], 1, 1).astype(BF16)
        cgT[:, pooled] = dot(wo[...], f3[pooled, :], 1, 1).astype(BF16)
        for h in range(heads):
            lanes = slice(h * DH, (h + 1) * DH)
            slot = g * heads + h
            score[...] = dot(cg[pooled, lanes], vT[lanes, cols])

            def one(row):
                block = row // 64
                part = pl.multiple_of(lax.rem(row, 64), 32)
                band = pl.ds(pl.multiple_of(512 - 128 * block, 128), TOK_ROW)
                prob = probs[slot, pl.ds(row, 32), :]
                prob_grad = score[pl.ds(row, 32), :]
                inner = jnp.sum(prob * prob_grad, axis=-1, keepdims=True)
                grad = prob * (prob_grad - inner)
                ds[pl.ds(row, 32), :] = grad.astype(BF16)
                tacc[h, pl.ds(part, 32), band] += grad

            tiles(HALF_ROW, 32, one, U_SBACK)
            scale = 1.0 / math.sqrt(DH)
            dqT[lanes, pooled] = (dot(kT[lanes, cols], ds[...], 1, 1) * scale).astype(BF16)
            kgT[lanes, cols] = dot(qT[lanes, pooled], ds[...]).astype(BF16)
            vgT[lanes, cols] = dot(cgT[lanes, pooled], problow[slot]).astype(BF16)
            after()

    in_one, in_two = {}, {}

    def input_part(g):
        pooled = slice(g * HALF_ROW, (g + 1) * HALF_ROW)
        cols = slice(g * TOK_ROW, (g + 1) * TOK_ROW)
        doubled = (dot(dqT[:, pooled], dup[...]) * 0.5).astype(BF16)
        f3dT[...] = (dot(f3[pooled, :], dup[...], 0, 0) * 0.125).astype(BF16)
        for b in range(4):
            rows = slice(b * share, (b + 1) * share)
            total = dot(wk[rows, :], kgT[:, cols]) + dot(wv[rows, :], vgT[:, cols])
            total = total + dot(wq[rows, :], doubled) + f3dT[rows, :].astype(F32)
            tp[g, b] = total.astype(BF16)
        far = core + 2 * (1 - side)
        for index, block in enumerate((1 - core + 2 * (1 - side), 1 - core + 2 * side)):
            in_one[g, index] = copies.start(("in", g, index), tp.at[g, block], inR1.at[g, index], sib_id)
        in_one[g, 0].wait()

        def add(row):
            here = pl.ds(row, 32)
            inB[g, here, :] = (
                tp[g, far, here, :].astype(F32) + inR1[g, 0, here, :].astype(F32)
            ).astype(BF16)

        tiles(share, 32, add, 2)
        in_two[g] = copies.start(("in two", g), inB.at[g], inR2.at[g], cross_id)

    def input_end(g):
        in_one[g, 1].wait()
        in_two[g].wait()

        def add(row):
            here = pl.ds(row, 32)
            igo[here, g * TOK_ROW : (g + 1) * TOK_ROW] = (
                tp[g, t, here, :].astype(F32)
                + inR1[g, 1, here, :].astype(F32)
                + inR2[g, here, :].astype(F32)
            ).astype(BF16)

        tiles(share, 32, add, 2)

    def small_sums():
        for index in range(5):
            small[index : index + 1, :] = jnp.sum(acc[index], axis=0, keepdims=True)
        small[UP_ROW : UP_ROW + 1, :] = jnp.sum(acc[UP_BIAS], axis=0, keepdims=True)
        lane = lax.broadcasted_iota(jnp.int32, (1, BAND), 1)
        lane_out = lax.broadcasted_iota(jnp.int32, (1, 2 * REL), 1)
        sub = lax.broadcasted_iota(jnp.int32, (8, BAND), 0)
        for h in range(heads):
            part = tacc[h]
            for size in (32, 16, 8):
                part = part[0:size] + pltpu.roll(part[size : 2 * size], BAND - 2 * size, 1)
            for size in (4, 2, 1):
                part = jnp.where(
                    lax.rem(sub // size, 2) == 1, pltpu.roll(part, BAND - 2 * size, 1), part
                )
            part = jnp.sum(part, axis=0, keepdims=True)
            low = jnp.sum(jnp.where(lane <= 448, part, 0.0), axis=1, keepdims=True)
            high = jnp.sum(jnp.where(lane >= 575, part, 0.0), axis=1, keepdims=True)
            middle = pltpu.roll(part, BAND - 448, 1)[:, 0 : 2 * REL]
            middle = jnp.where(
                lane_out == 0, low, jnp.where(lane_out == 2 * REL - 1, high, middle)
            )
            small[TABLE_ROW + h : TABLE_ROW + h + 1, 0 : 2 * REL] = middle

    for load in early[:4]:
        load.wait()
    for load in vectors[2:] + late:
        load.start()
    qkv(0)
    early[4].wait()
    attend(0)
    pl.semaphore_wait(barrier, 2 + len(grid.peers))
    reduce_start(0, 0)
    qkv(1)
    reduce_middle(0, 0)
    attend(1)
    reduce_start(0, 1)
    for load in vectors[2:]:
        load.wait()
    first_norm(0)
    reduce_middle(0, 1)
    for load in late:
        load.wait()
    feed_forward(0)
    reduce_start(1, 0)
    first_norm(1)
    reduce_middle(1, 0)
    feed_forward(1)
    reduce_start(1, 1)
    second_norm(0)
    reduce_middle(1, 1)
    feed_back(0)
    reduce_start(2, 0)
    second_norm(1)
    reduce_middle(2, 0)
    feed_back(1)
    reduce_start(2, 1)

    outs = []

    def put(source, target):
        copy = pltpu.make_async_copy(source, target, out_sems.at[len(outs)])
        copy.start()
        outs.append(copy)

    specs, turns, tail = stream_plan
    streams, state = [], {"block": 0, "inbox": 0}

    def advance(stream):
        if stream.pending is not None and not stream.turn():
            rows = pl.ds(stream.first, stream.count)
            put(summed.at[rows], g_h.at[rows])

    def mark():
        block = state["block"]
        state["block"] += 1
        for row, rows, order, opens in specs:
            if opens == block:
                stream = Stream(
                    copies, (grads, summed, inbox), state["inbox"], row, rows, grid.plans[order]
                )
                state["inbox"] += grid.inbox_rows(order, rows)
                stream.turn()
                streams.append(stream)
        for index in turns[block] if block < len(turns) else ():
            advance(streams[index])

    grads[0:ff, :] = dot(act[...], f2[...], 0, 0).astype(BF16)
    mark()
    reduce_middle(2, 1)
    grads[ff : ff + width, :] = dot(f1[...], preg[...], 0, 0).astype(BF16)
    mark()
    first_back(0)
    wk[...] = wkT[...].T
    wv[...] = wvT[...].T
    wq[...] = wqT[...].T
    mark()
    attend_back(0, mark)
    first_back(1)
    mark()
    attend_back(1, mark)
    base = ff + width
    hw = heads * DH
    grads[base : base + hw, :] = dot(ctx[...], f3[...], 0, 0).astype(BF16)
    mark()
    grads[base + hw : base + 2 * hw, :] = dot(dqT[...], plow[...]).astype(BF16)
    mark()
    grads[base + 2 * hw : base + 3 * hw, :] = dot(kgT[...], hid[...]).astype(BF16)
    grads[base + 3 * hw : base + 4 * hw, :] = dot(vgT[...], hid[...]).astype(BF16)
    mark()
    small_sums()
    copy = copies.start("small", small.at[pl.ds(0, 8)], smallR.at[0, pl.ds(0, 8)], sib_id)
    mark()
    input_part(0)
    mark()
    copy.wait()
    small[0:8, :] = small[0:8, :] + smallR[0, 0:8, :]
    copy = copies.start(("small", 0), small, smallR.at[1], grid.across[0])
    input_part(1)
    mark()
    for bit in range(bits):
        copy.wait()
        small[...] = small[...] + smallR[bit + 1]
        if bit + 1 < bits:
            copy = copies.start(("small", bit + 1), small, smallR.at[bit + 2], grid.across[bit + 1])
            mark()
    input_end(0)
    input_end(1)
    put(igo, ig_h)
    put(small, small_h)
    for g in range(chunks):
        shares["po", g].wait()
    put(po, po_h)
    order = list(tail)
    while any(stream.pending is not None for stream in streams):
        index = order.pop(0) if order else [s.pending is not None for s in streams].index(True)
        advance(streams[index])
    for copy in outs:
        copy.wait()


def finish_kernel(
    plan, po_h, ig_h, g_h, small_h, po_o, ig_o, q_o, k_o, v_o, wo_o, up_o, dn_o, *rest
):
    tab_o, fg_o, fs_o, ub_o, db_o, sg_o, ss_o, po, ig, low, wide, small, tab, *vectors = rest
    *vectors, in_sems, out_sems = vectors
    targets = (dn_o, up_o, wo_o, q_o, k_o, v_o)
    get_small = pltpu.make_async_copy(small_h, small, in_sems.at[len(plan)])
    get_po = pltpu.make_async_copy(po_h, po, in_sems.at[len(plan) + 1])
    get_ig = pltpu.make_async_copy(ig_h, ig, in_sems.at[len(plan) + 2])
    gets = [
        pltpu.make_async_copy(
            g_h.at[pl.ds(row, rows)], low.at[pl.ds(row, rows)], in_sems.at[index]
        )
        for index, (row, rows, unused, unused_row) in enumerate(plan)
    ]
    for get in [get_small] + gets + [get_po, get_ig]:
        get.start()
    puts = []

    def put(source, target):
        copy = pltpu.make_async_copy(source, target, out_sems.at[len(puts)])
        copy.start()
        puts.append(copy)

    get_small.wait()
    for vector, row, out in zip(
        vectors,
        (FIRST_GAIN, FIRST_SHIFT, UP_ROW, DOWN_BIAS, SECOND_GAIN, SECOND_SHIFT),
        (fg_o, fs_o, ub_o, db_o, sg_o, ss_o),
    ):
        vector[...] = small[row, : vector.shape[0]]
        put(vector, out)
    tab[...] = small[TABLE_ROW : TABLE_ROW + tab.shape[0], : 2 * REL]
    put(tab, tab_o)
    for get, (row, rows, index, target_row) in zip(gets, plan):
        get.wait()

        def widen(here):
            where = pl.ds(pl.multiple_of(row + here, 32), 32)
            wide[where, :] = low[where, :].astype(F32)

        tiles(rows, 32, widen)
        put(wide.at[pl.ds(row, rows)], targets[index].at[pl.ds(target_row, rows)])
    get_po.wait()
    put(po, po_o)
    get_ig.wait()
    put(ig, ig_o)
    for copy in puts:
        copy.wait()


def finish(pooled_out, input_grad, grads, small, heads, ff, width):
    hw = heads * DH
    total = grads.shape[0]
    plan, row = [], 0
    for index, rows in enumerate((ff, width, hw, hw, hw, hw)):
        for start in range(0, rows, 384):
            size = min(384, rows - start)
            plan.append((row + start, size, index, start))
        row += rows
    vector = jax.ShapeDtypeStruct((width,), F32)
    any_spec = pl.BlockSpec(memory_space=pl.ANY)
    outs = pl.pallas_call(
        partial(finish_kernel, tuple(plan)),
        name="finish",
        out_shape=(
            jax.ShapeDtypeStruct(pooled_out.shape, BF16),
            jax.ShapeDtypeStruct(input_grad.shape, BF16),
            jax.ShapeDtypeStruct((hw, width), F32),
            jax.ShapeDtypeStruct((hw, width), F32),
            jax.ShapeDtypeStruct((hw, width), F32),
            jax.ShapeDtypeStruct((hw, width), F32),
            jax.ShapeDtypeStruct((width, ff), F32),
            jax.ShapeDtypeStruct((ff, width), F32),
            jax.ShapeDtypeStruct((heads, 2 * REL), F32),
            vector,
            vector,
            jax.ShapeDtypeStruct((ff,), F32),
            vector,
            vector,
            vector,
        ),
        in_specs=[any_spec] * 4,
        out_specs=(any_spec,) * 15,
        scratch_shapes=[
            pltpu.VMEM(pooled_out.shape, BF16),
            pltpu.VMEM(input_grad.shape, BF16),
            pltpu.VMEM((total, width), BF16),
            pltpu.VMEM((total, width), F32),
            pltpu.VMEM((SMALL_ROWS, width), F32),
            pltpu.VMEM((heads, 2 * REL), F32),
            pltpu.VMEM((width,), F32),
            pltpu.VMEM((width,), F32),
            pltpu.VMEM((ff,), F32),
            pltpu.VMEM((width,), F32),
            pltpu.VMEM((width,), F32),
            pltpu.VMEM((width,), F32),
            pltpu.SemaphoreType.DMA((len(plan) + 3,)),
            pltpu.SemaphoreType.DMA((len(plan) + 9,)),
        ],
        compiler_params=pltpu.CompilerParams(vmem_limit_bytes=64_000_000),
    )(pooled_out, input_grad, grads, small)
    po, ig, qg, kg, vg, wo, up, dn, tab, fg, fs, ub, db, sg, ss = outs
    return po, ig.T, qg.T, kg.T, vg.T, wo, tab, fg, fs, up, ub, dn, db, sg, ss


def local(n_dp, *args):
    (
        hidden_in,
        segment_ids,
        query_weight,
        key_weight,
        value_weight,
        output_weight,
        position_table,
        first_gain,
        first_shift,
        up_weight,
        up_bias,
        down_weight,
        down_bias,
        second_gain,
        second_shift,
        cotangent,
    ) = args
    tokens, width = hidden_in.shape
    chunks = tokens // TOK_ROW
    pooled = tokens // 2
    half = HALF_ROW // 2
    heads = position_table.shape[0]
    hw = heads * DH
    ff = up_weight.shape[1]
    share = width // 4
    specs, row = [], 0
    for pieces, opens in GROUPS:
        for order, rows in pieces:
            specs.append((row, rows, order, opens))
            row += rows
    plan = (tuple(specs), TURNS, TAIL)
    bits = n_dp.bit_length() - 1
    links = 5 if n_dp == 8 else bits + 3
    total = ff + width + 4 * hw
    cfg = (n_dp, heads, HALF_ROW, chunks, width, ff, share, plan)
    vmem = lambda *shape: pltpu.VMEM(shape, BF16)
    wide = lambda *shape: pltpu.VMEM(shape, F32)
    slots = 3 * chunks
    inbox_rows = total * 7 // 4 + max(bits - 3, 0) * total // 8
    any_spec = pl.BlockSpec(memory_space=pl.ANY)
    scratch = [
        pltpu.VMEM((tokens,), jnp.int32),
        wide(width),
        wide(width),
        wide(ff),
        wide(width),
        wide(width),
        wide(width),
        wide(heads, 2 * REL),
        vmem(tokens, width),
        vmem(width, hw),
        vmem(width, hw),
        vmem(width, hw),
        vmem(hw, width),
        vmem(width, ff),
        vmem(ff, width),
        vmem(pooled, width),
        vmem(hw, width),
        vmem(hw, width),
        vmem(hw, width),
        vmem(HALF_ROW, TOK_ROW),
        wide(pooled, 1),
        wide(heads, 64, BAND),
        wide(heads, 64, BAND),
        vmem(pooled, width),
        wide(pooled // 2, width),
        vmem(pooled, hw),
        vmem(hw, pooled),
        vmem(hw, tokens),
        vmem(hw, tokens),
        wide(HALF_ROW, TOK_ROW),
        wide(chunks * heads, HALF_ROW, TOK_ROW),
        vmem(chunks * heads, HALF_ROW, TOK_ROW),
        vmem(HALF_ROW, TOK_ROW),
        vmem(pooled, hw),
        vmem(slots, HALF_ROW, width),
        vmem(slots, half, width),
        vmem(slots, half, width),
        vmem(slots, half, width),
        vmem(pooled, width),
        vmem(pooled, width),
        vmem(pooled, width),
        wide(pooled // 2, width),
        wide(pooled // 2, width),
        wide(pooled // 2, 1),
        wide(HALF_ROW, ff),
        vmem(pooled, ff),
        wide(pooled, ff),
        vmem(pooled, ff),
        wide(pooled // 2, width),
        vmem(pooled, width),
        vmem(pooled, hw),
        vmem(hw, pooled),
        vmem(hw, pooled),
        vmem(hw, tokens),
        vmem(hw, tokens),
        vmem(width, TOK_ROW),
        vmem(chunks, 4, share, TOK_ROW),
        vmem(chunks, 2, share, TOK_ROW),
        vmem(chunks, share, TOK_ROW),
        vmem(chunks, share, TOK_ROW),
        vmem(share, tokens),
        vmem(total, width),
        vmem(total, width),
        vmem(inbox_rows, width),
        wide(6, 8, width),
        wide(SMALL_ROWS, width),
        wide(bits + 1, SMALL_ROWS, width),
        pltpu.SemaphoreType.DMA((16,)),
        pltpu.SemaphoreType.DMA((len(specs) + 3,)),
        pltpu.SemaphoreType.DMA((SENDS,)),
        pltpu.SemaphoreType.DMA((links * len(specs) + RECEIVES,)),
    ]
    pooled_out, input_grad, grads, small = pl.pallas_call(
        partial(fused, cfg),
        name="layer",
        out_shape=(
            jax.ShapeDtypeStruct((pooled, width), BF16),
            jax.ShapeDtypeStruct((share, tokens), BF16),
            jax.ShapeDtypeStruct((total, width), BF16),
            jax.ShapeDtypeStruct((SMALL_ROWS, width), F32),
        ),
        in_specs=[any_spec] * 16,
        out_specs=(any_spec,) * 4,
        scratch_shapes=scratch,
        compiler_params=pltpu.CompilerParams(
            collective_id=0, has_side_effects=True, vmem_limit_bytes=64_000_000
        ),
    )(
        segment_ids,
        first_gain,
        first_shift,
        up_bias,
        down_bias,
        second_gain,
        second_shift,
        position_table,
        hidden_in,
        query_weight.T,
        key_weight.T,
        value_weight.T,
        output_weight,
        up_weight,
        down_weight,
        cotangent,
    )
    return finish(pooled_out, input_grad, grads, small, heads, ff, width)


def solution(mesh):
    return jax.shard_map(
        partial(local, mesh.shape["dp"]),
        mesh=mesh,
        in_specs=(
            P("dp", None),
            P("dp"),
            P(None, "tensor"),
            P(None, "tensor"),
            P(None, "tensor"),
            P("tensor", None),
            P("tensor", None),
            P(),
            P(),
            P(None, "tensor"),
            P("tensor"),
            P("tensor", None),
            P(),
            P(),
            P(),
            P("dp", None),
        ),
        out_specs=(
            P("dp", None),
            P("dp", "tensor"),
            P(None, "tensor"),
            P(None, "tensor"),
            P(None, "tensor"),
            P("tensor", None),
            P("tensor", None),
            P(),
            P(),
            P(None, "tensor"),
            P("tensor"),
            P("tensor", None),
            P(),
            P(),
            P(),
        ),
        check_vma=False,
    )
```

```python
import math
from functools import partial

import jax
import jax.numpy as jnp
from jax import lax
from jax.experimental import pallas as pl
from jax.experimental.pallas import tpu as pltpu
from jax.sharding import PartitionSpec as P

DH = 64
TOK_ROW = 512
HALF_ROW = TOK_ROW // 2
REL = 64
EPSILON = 1e-06
NEGATIVE = -1e30
MESH = pl.DeviceIdType.MESH
F32 = jnp.float32
BF16 = jnp.bfloat16

FIRST_GAIN, FIRST_SHIFT, DOWN_BIAS, SECOND_GAIN, SECOND_SHIFT, UP_BIAS = range(6)
UP_ROW, TABLE_ROW, SMALL_ROWS = 8, 9, 16
BAND = 1024
ROLL = 1152
SENDS = 28
RECEIVES = 24
PIECES = (('Y', 192), ('Z', 128), ('Z', 64), ('Y', 128), ('Y', 128), ('Z', 64), ('Y', 64), ('Z', 64), ('Y', 128), ('Y', 192), ('Z', 128), ('Y', 128), ('Y', 128), ('Z', 128), ('Y', 64), ('Y', 192), ('Y', 128), ('Y', 128), ('Y', 128))
TURNS = [[2, 3, 1, 4], [12], [], [2, 3, 9], [4], [2, 10, 0], [1, 12], [3, 6], [9, 2, 1, 4], [3, 11], [], [], [0, 15, 4], [6, 10, 3, 2], [1], [4, 12, 11, 17]]
TAIL = [10, 3, 9, 2, -1, 12, 15, 4, 1, -1, 0, 9, 2, 6, -1, 12, 17, 10, 11, -1, 1, 3, 0, 12, -1, 7, 18, 15, 9, -1, 13, 4, 6, 10, -1, 11, 17, 8, 1, -1, 0, 14, 12, 7, -1, 15, 6, 5, 16, -1, 18, 9, 10, 8, -1, 13, 11, 14, 0, -1, 17, 6, 5, 7, -1, 16, 15, 18, 9, -1, 13, 10, 8, 17, -1, 14, 5, 11, 0, -1, 18, 16, 6, 8, -1, 7, 14, 13, 15, -1, 18, 5, 16, 17, -1, 8, 11, 14, 7, -1, 16, 13, 18, 7, -1, 8, 15, 14, 13, -1, 5, 16, 17, 5, -1, 7, 18, 8, 14, -1, 13, 16, 5]
U_SOFT, U_SBACK, U_NORM, U_GELU = 2, 2, 4, 2


def dot(left, right, left_dim=1, right_dim=0):
    return lax.dot_general(
        left, right, (((left_dim,), (right_dim,)), ((), ())), preferred_element_type=F32
    )


def tiles(count, step, body, unroll=1):
    unroll = math.gcd(unroll, count // step)
    stride = step * unroll

    def one(index, unused):
        for part in range(unroll):
            body(pl.multiple_of(index * stride + part * step, step))
        return unused

    if count == stride:
        one(0, 0)
    else:
        lax.fori_loop(0, count // stride, one, 0)


def fold(value):
    total = value[0:8]
    for start in range(8, value.shape[0], 8):
        total = total + value[start : start + 8]
    return total


class Copy:
    def __init__(self, copy, send, recv, free):
        self.copy, self.send, self.recv, self.free = copy, send, recv, free

    def start(self):
        if self.send is None:
            self.copy.start()
        else:
            pl.when(self.send)(self.copy.start)

    def wait(self):
        if self.send is None:
            self.copy.wait()
        else:
            pl.when(self.send)(self.copy.wait_send)
            pl.when(self.recv)(self.copy.wait_recv)
        self.free()


class Copies:
    def __init__(self, send_sems, recv_sems):
        self.send_sems, self.recv_sems = send_sems, recv_sems
        self.idle, self.keys = list(range(SENDS)), {}

    def start(self, key, source, target, device, send=None, recv=None):
        index = self.idle.pop(0)
        copy = Copy(
            pltpu.make_async_remote_copy(
                src_ref=source,
                dst_ref=target,
                send_sem=self.send_sems.at[index],
                recv_sem=self.recv_sems.at[self.keys.setdefault(key, len(self.keys))],
                device_id=device,
                device_id_type=MESH,
            ),
            send,
            recv,
            lambda: self.idle.append(index),
        )
        copy.start()
        return copy


class Grid:
    def __init__(self, n_dp, d, t):
        self.bits = n_dp.bit_length() - 1
        self.mine = [lax.rem(d // (1 << bit), 2) for bit in range(self.bits)]
        self.across = [(d + (1 - 2 * self.mine[b]) * (1 << b), t) for b in range(self.bits)]
        self.peers = list(self.across)
        self.plans = {}
        if n_dp == 8:
            z = d // 2
            middle = jnp.logical_or(z == 1, z == 2)
            end = jnp.logical_not(middle)
            upper = z // 2
            facing = (d + (3 - 2 * z) * 2, t)
            self.peers.append(facing)
            everyone = (None, None, None, "y")
            inner = (middle, middle, middle)
            y = ("half", self.across[0], self.mine[0])
            y_back = ("back", self.across[0], self.mine[0])
            gather = ("whole", self.across[1], 0, end, middle, middle, "z")
            spread = ("same", self.across[1], 0, middle, end, middle, "z")
            mid = ("half", facing, upper) + inner + ("mid",)
            mid_back = ("back", facing, upper) + inner + ("mid_back",)
            y_inner = inner + ("y",)
            y_out = ("y_back",)
            self.plans["Y"] = (
                y + everyone,
                gather,
                mid,
                mid_back,
                spread,
                y_back + everyone[:3] + y_out,
            )
            self.plans["Z"] = (gather, mid, y + y_inner, y_back + inner + y_out, mid_back, spread)
        else:
            everyone = (None, None, None)
            halving = list(range(min(3, self.bits)))
            plan = [("half", self.across[b], self.mine[b]) + everyone + (b,) for b in halving]
            plan += [
                ("whole", self.across[b], 0) + everyone + (b,)
                for b in range(len(halving), self.bits)
            ]
            plan += [
                ("back", self.across[b], self.mine[b]) + everyone + (self.bits + b,)
                for b in reversed(halving)
            ]
            self.plans["Y"] = self.plans["Z"] = tuple(plan)

    def inbox_rows(self, order, rows):
        total = 0
        for kind, *unused in self.plans[order]:
            if kind == "half":
                rows //= 2
            if kind in ("half", "whole"):
                total += rows
        return total


class Stream:
    def __init__(self, copies, buffers, inbox_row, row, rows, plan):
        self.copies, self.plan = copies, plan
        self.grads, self.summed, self.inbox = buffers
        self.inbox_row, self.rows, self.pos = inbox_row, rows, row
        self.first, self.count = row, rows
        self.step, self.pending = 0, None

    def begin(self):
        kind, device, mine, send, recv, unused, link = self.plan[self.step]
        size = self.rows
        at = self.pos
        if kind == "half":
            size //= 2
            self.keep = pl.multiple_of(self.pos + mine * size, 16)
            at = pl.multiple_of(self.pos + (1 - mine) * size, 16)
        if kind in ("half", "whole"):
            source = self.grads.at[pl.ds(at, size)]
            target = self.inbox.at[pl.ds(self.inbox_row, size)]
        else:
            source = target = self.summed.at[pl.ds(at, size)]
        self.pending = self.copies.start((self.first, link), source, target, device, send, recv)
        self.size = size

    def finish(self):
        kind, device, mine, send, recv, adds, link = self.plan[self.step]
        self.pending.wait()
        self.step += 1
        if kind == "back":
            self.pos = pl.multiple_of(self.pos - mine * self.size, 16)
            self.rows = 2 * self.size
        elif kind != "same":
            if kind == "half":
                self.pos, self.rows = self.keep, self.size
            base, inbox_row, grads, inbox = self.pos, self.inbox_row, self.grads, self.inbox
            result = self.summed if self.plan[self.step][0] == "back" else grads
            step = 32 if self.size % 32 == 0 else 16

            def add(row):
                rows = pl.ds(pl.multiple_of(base + row, 16), step)
                arrived = inbox[pl.ds(pl.multiple_of(inbox_row + row, 16), step), :]
                result[rows, :] = (grads[rows, :].astype(F32) + arrived.astype(F32)).astype(BF16)

            def add_all():
                tiles(self.size, step, add, 2)

            if adds is None:
                add_all()
            else:
                pl.when(adds)(add_all)
            self.inbox_row += self.size

    def done(self):
        return self.step == len(self.plan)

    def turn(self):
        if self.pending is not None:
            self.finish()
            self.pending = None
        if not self.done():
            self.begin()


def fused(
    cfg,
    seg_h,
    first_gain_h,
    first_shift_h,
    up_bias_h,
    down_bias_h,
    second_gain_h,
    second_shift_h,
    tab_h,
    hid_h,
    wq_h,
    wk_h,
    wv_h,
    wo_h,
    up_h,
    dn_h,
    cot_h,
    po_h,
    ig_h,
    g_h,
    small_h,
    seg_ref,
    first_gain,
    first_shift,
    up_bias_in,
    down_bias_in,
    second_gain,
    second_shift,
    tab_ref,
    hid,
    wq,
    wk,
    wv,
    wo,
    up,
    dn,
    cot,
    wqT,
    wkT,
    wvT,
    dup,
    segq,
    bias,
    tacc,
    plow,
    pown,
    q,
    qT,
    kT,
    vT,
    score,
    probs,
    problow,
    ds,
    ctx,
    arA,
    arR1,
    arB,
    arR2,
    f1,
    f2,
    f3,
    first_out,
    normed1,
    inv1,
    pre,
    act,
    gp,
    preg,
    sgrad,
    po,
    cg,
    cgT,
    dqT,
    kgT,
    vgT,
    f3dT,
    tp,
    inR1,
    inB,
    inR2,
    igo,
    grads,
    summed,
    inbox,
    acc,
    small,
    smallR,
    in_sems,
    out_sems,
    send_sems,
    recv_sems,
):
    n_dp, heads, rows_per, chunks, width, ff, share, stream_plan = cfg
    half = HALF_ROW // 2
    d = lax.axis_index("dp")
    t = lax.axis_index("tensor")
    core = lax.rem(t, 2)
    side = t // 2
    sib_id = (d, t + 1 - 2 * core)
    cross_id = (d, t + 2 - 4 * side)
    grid = Grid(n_dp, d, t)
    bits = grid.bits
    own = pl.multiple_of(core * half, half)
    away = pl.multiple_of((1 - core) * half, half)

    loads = [
        pltpu.make_async_copy(source, target, in_sems.at[index])
        for index, (source, target) in enumerate(
            [
                (hid_h, hid),
                (wk_h, wkT),
                (wv_h, wvT),
                (wq_h, wqT),
                (wo_h, wo),
                (up_h, up),
                (dn_h, dn),
                (cot_h, cot),
                (seg_h, seg_ref),
                (tab_h, tab_ref),
                (first_gain_h, first_gain),
                (first_shift_h, first_shift),
                (up_bias_h, up_bias_in),
                (down_bias_h, down_bias_in),
                (second_gain_h, second_gain),
                (second_shift_h, second_shift),
            ]
        )
    ]
    early, vectors, late = loads[:5], loads[8:], loads[5:8]
    for load in vectors[:2] + early:
        load.start()
    barrier = pltpu.get_barrier_semaphore()
    for device in [sib_id, cross_id] + grid.peers:
        pl.semaphore_signal(barrier, inc=1, device_id=device, device_id_type=MESH)

    row_i = lax.broadcasted_iota(jnp.int32, (HALF_ROW, TOK_ROW), 0)
    col_i = lax.broadcasted_iota(jnp.int32, (HALF_ROW, TOK_ROW), 1)
    dup[...] = jnp.where(col_i // 2 == row_i, 1.0, 0.0).astype(BF16)
    evens = jnp.where(col_i == 2 * row_i, 1.0, 0.0).astype(BF16)
    vectors[0].wait()
    segk = [
        seg_ref[g * TOK_ROW : (g + 1) * TOK_ROW].astype(F32).reshape(1, TOK_ROW)
        for g in range(chunks)
    ]
    for g in range(chunks):
        rows = jnp.broadcast_to(segk[g], (8, TOK_ROW)).astype(BF16)
        segq[g * HALF_ROW : (g + 1) * HALF_ROW, :] = dot(evens, rows, 1, 1)[:, 0:1]
    vectors[1].wait()
    for h in range(heads):
        table = jnp.concatenate(
            [
                jnp.broadcast_to(tab_ref[h : h + 1, 0:1], (REL, 512)),
                jnp.broadcast_to(tab_ref[h : h + 1, :], (REL, 2 * REL)),
                jnp.broadcast_to(tab_ref[h : h + 1, 2 * REL - 1 : 2 * REL], (REL, 512)),
            ],
            axis=1,
        )
        bias[h] = pltpu.roll(table, ROLL - 64, 1, stride=2, stride_axis=0)[:, :BAND]
    tacc[...] = jnp.zeros_like(tacc)
    acc[...] = jnp.zeros_like(acc)
    small[...] = jnp.zeros_like(small)

    copies = Copies(send_sems, recv_sems)

    reduce_one, reduce_two = {}, {}

    def reduce_start(which, g):
        slot = which * chunks + g
        reduce_one[slot] = copies.start(("one", g), arA.at[slot, pl.ds(away, half)], arR1.at[slot], sib_id)

    def reduce_middle(which, g):
        slot = which * chunks + g
        reduce_one[slot].wait()

        def add(row):
            mine = arA[slot, pl.ds(pl.multiple_of(own + row, 32), 32), :].astype(F32)
            arB[slot, pl.ds(row, 32), :] = (
                mine + arR1[slot, pl.ds(row, 32), :].astype(F32)
            ).astype(BF16)

        tiles(half, 32, add, 2)
        reduce_two[slot] = copies.start(("two", g, which % 2), arB.at[slot], arR2.at[slot], cross_id)

    def reduced(which, g, row):
        slot = which * chunks + g
        return arB[slot, pl.ds(row, 16), :].astype(F32) + arR2[slot, pl.ds(row, 16), :].astype(F32)

    shares = {}

    def share_start(name, buffer, g):
        rows = buffer.at[pl.ds(pl.multiple_of(g * HALF_ROW + own, half), half)]
        key = ("po" if name == "po" else "share", g)
        shares[name, g] = copies.start(key, rows, rows, sib_id)

    def qkv(g):
        tokens = hid[g * TOK_ROW : (g + 1) * TOK_ROW, :]
        pooled = slice(g * HALF_ROW, (g + 1) * HALF_ROW)
        cols = slice(g * TOK_ROW, (g + 1) * TOK_ROW)
        plow[pooled, :] = (dot(dup[...], tokens) * 0.5).astype(BF16)
        mine = hid[pl.ds(pl.multiple_of(g * TOK_ROW + core * HALF_ROW, HALF_ROW), HALF_ROW), :]
        pown[g * half : (g + 1) * half, :] = dot(dup[0:half, 0:HALF_ROW], mine) * 0.5
        kT[:, cols] = dot(wkT[...], tokens, 1, 1).astype(BF16)
        vT[:, cols] = dot(wvT[...], tokens, 1, 1).astype(BF16)
        scale = 1.0 / math.sqrt(DH)
        q[pooled, :] = (dot(plow[pooled, :], wqT[...], 1, 1) * scale).astype(BF16)
        qT[:, pooled] = (dot(wqT[...], plow[pooled, :], 1, 1) * scale).astype(BF16)

    def attend(g):
        pooled = slice(g * HALF_ROW, (g + 1) * HALF_ROW)
        cols = slice(g * TOK_ROW, (g + 1) * TOK_ROW)
        for h in range(heads):
            lanes = slice(h * DH, (h + 1) * DH)
            slot = g * heads + h
            score[...] = dot(q[pooled, lanes], kT[lanes, cols])

            def one(row):
                block = row // 64
                part = pl.multiple_of(lax.rem(row, 64), 32)
                band = pl.ds(pl.multiple_of(512 - 128 * block, 128), TOK_ROW)
                raw = score[pl.ds(row, 32), :] + bias[h, pl.ds(part, 32), band]
                column = segq[pl.ds(pl.multiple_of(g * HALF_ROW + row, 32), 32), :]
                raw = jnp.where(column == segk[g], raw, NEGATIVE)
                weights = jnp.exp(raw - jnp.max(raw, axis=-1, keepdims=True))
                prob = weights * (1.0 / jnp.sum(weights, axis=-1, keepdims=True))
                probs[slot, pl.ds(row, 32), :] = prob
                problow[slot, pl.ds(row, 32), :] = prob.astype(BF16)

            tiles(HALF_ROW, 32, one, U_SOFT)
            ctx[pooled, lanes] = dot(problow[slot], vT[lanes, cols], 1, 1).astype(BF16)
        arA[g] = dot(ctx[pooled, :], wo[...]).astype(BF16)

    def first_norm(g):
        reduce_two[g].wait()
        gain, shift = first_gain[...].reshape(1, width), first_shift[...].reshape(1, width)

        def one(row):
            here = pl.ds(pl.multiple_of(g * half + row, 16), 16)
            value = pown[here, :] + reduced(0, g, row)
            centred = value - jnp.mean(value, axis=-1, keepdims=True)
            inverse = lax.rsqrt(jnp.mean(centred * centred, axis=-1, keepdims=True) + EPSILON)
            normed = centred * inverse
            out = normed * gain + shift
            normed1[here, :] = normed
            inv1[here, :] = inverse
            first_out[here, :] = out
            f1[pl.ds(pl.multiple_of(g * HALF_ROW + own + row, 16), 16), :] = out.astype(BF16)

        tiles(half, 16, one, U_NORM)
        share_start("f1", f1, g)

    def feed_forward(g):
        shares["f1", g].wait()
        pooled = slice(g * HALF_ROW, (g + 1) * HALF_ROW)
        pre[...] = dot(f1[pooled, :], up[...])
        up_bias = up_bias_in[...].reshape(1, ff)

        def one(row):
            value = pre[pl.ds(row, 16), :] + up_bias
            cdf = 0.5 * (1.0 + lax.erf(value * (1.0 / math.sqrt(2.0))))
            density = jnp.exp(-0.5 * value * value) * (1.0 / math.sqrt(2.0 * math.pi))
            here = pl.ds(pl.multiple_of(g * HALF_ROW + row, 16), 16)
            act[here, :] = (value * cdf).astype(BF16)
            gp[here, :] = cdf + value * density

        tiles(HALF_ROW, 16, one, U_GELU)
        arA[chunks + g] = dot(act[pooled, :], dn[...]).astype(BF16)

    def second_norm(g):
        reduce_two[chunks + g].wait()
        gain, shift = second_gain[...].reshape(1, width), second_shift[...].reshape(1, width)
        down_bias = down_bias_in[...].reshape(1, width)

        def one(row):
            here = pl.ds(pl.multiple_of(g * half + row, 16), 16)
            full = pl.ds(pl.multiple_of(g * HALF_ROW + own + row, 16), 16)
            value = first_out[here, :] + reduced(1, g, row) + down_bias
            centred = value - jnp.mean(value, axis=-1, keepdims=True)
            inverse = lax.rsqrt(jnp.mean(centred * centred, axis=-1, keepdims=True) + EPSILON)
            normed = centred * inverse
            po[full, :] = (normed * gain + shift).astype(BF16)
            upstream = cot[full, :].astype(F32)
            scaled = upstream * gain
            grad = inverse * (
                scaled
                - jnp.mean(scaled, axis=-1, keepdims=True)
                - normed * jnp.mean(scaled * normed, axis=-1, keepdims=True)
            )
            sgrad[here, :] = grad
            f2[full, :] = grad.astype(BF16)
            acc[SECOND_GAIN] += fold(upstream * normed)
            acc[SECOND_SHIFT] += fold(upstream)
            acc[DOWN_BIAS] += fold(grad)

        tiles(half, 16, one, U_NORM)
        share_start("f2", f2, g)
        share_start("po", po, g)

    def feed_back(g):
        shares["f2", g].wait()
        pooled = slice(g * HALF_ROW, (g + 1) * HALF_ROW)
        pre[...] = dot(f2[pooled, :], dn[...], 1, 1)

        def one(row):
            here = pl.ds(pl.multiple_of(g * HALF_ROW + row, 16), 16)
            low = (gp[here, :] * pre[pl.ds(row, 16), :]).astype(BF16)
            preg[here, :] = low
            acc[UP_BIAS, :, :ff] += fold(low.astype(F32))

        tiles(HALF_ROW, 16, one, U_GELU)
        arA[2 * chunks + g] = dot(preg[pooled, :], up[...], 1, 1).astype(BF16)

    def first_back(g):
        reduce_two[2 * chunks + g].wait()
        gain = first_gain[...].reshape(1, width)

        def one(row):
            here = pl.ds(pl.multiple_of(g * half + row, 16), 16)
            full = pl.ds(pl.multiple_of(g * HALF_ROW + own + row, 16), 16)
            upstream = reduced(2, g, row) + sgrad[here, :]
            normed = normed1[here, :]
            scaled = upstream * gain
            grad = inv1[here, :] * (
                scaled
                - jnp.mean(scaled, axis=-1, keepdims=True)
                - normed * jnp.mean(scaled * normed, axis=-1, keepdims=True)
            )
            f3[full, :] = grad.astype(BF16)
            acc[FIRST_GAIN] += fold(upstream * normed)
            acc[FIRST_SHIFT] += fold(upstream)

        tiles(half, 16, one, U_NORM)
        share_start("f3", f3, g)

    def attend_back(g, after):
        shares["f3", g].wait()
        pooled = slice(g * HALF_ROW, (g + 1) * HALF_ROW)
        cols = slice(g * TOK_ROW, (g + 1) * TOK_ROW)
        cg[pooled, :] = dot(f3[pooled, :], wo[...], 1, 1).astype(BF16)
        cgT[:, pooled] = dot(wo[...], f3[pooled, :], 1, 1).astype(BF16)
        for h in range(heads):
            lanes = slice(h * DH, (h + 1) * DH)
            slot = g * heads + h
            score[...] = dot(cg[pooled, lanes], vT[lanes, cols])

            def one(row):
                block = row // 64
                part = pl.multiple_of(lax.rem(row, 64), 32)
                band = pl.ds(pl.multiple_of(512 - 128 * block, 128), TOK_ROW)
                prob = probs[slot, pl.ds(row, 32), :]
                prob_grad = score[pl.ds(row, 32), :]
                inner = jnp.sum(prob * prob_grad, axis=-1, keepdims=True)
                grad = prob * (prob_grad - inner)
                ds[pl.ds(row, 32), :] = grad.astype(BF16)
                tacc[h, pl.ds(part, 32), band] += grad

            tiles(HALF_ROW, 32, one, U_SBACK)
            scale = 1.0 / math.sqrt(DH)
            dqT[lanes, pooled] = (dot(kT[lanes, cols], ds[...], 1, 1) * scale).astype(BF16)
            kgT[lanes, cols] = dot(qT[lanes, pooled], ds[...]).astype(BF16)
            vgT[lanes, cols] = dot(cgT[lanes, pooled], problow[slot]).astype(BF16)
            after()

    in_one, in_two = {}, {}

    def input_part(g):
        pooled = slice(g * HALF_ROW, (g + 1) * HALF_ROW)
        cols = slice(g * TOK_ROW, (g + 1) * TOK_ROW)
        doubled = (dot(dqT[:, pooled], dup[...]) * 0.5).astype(BF16)
        f3dT[...] = (dot(f3[pooled, :], dup[...], 0, 0) * 0.125).astype(BF16)
        for b in range(4):
            rows = slice(b * share, (b + 1) * share)
            total = dot(wk[rows, :], kgT[:, cols]) + dot(wv[rows, :], vgT[:, cols])
            total = total + dot(wq[rows, :], doubled) + f3dT[rows, :].astype(F32)
            tp[g, b] = total.astype(BF16)
        for index, block in enumerate((1 - core + 2 * (1 - side), 1 - core + 2 * side)):
            in_one[g, index] = copies.start(("in", g, index), tp.at[g, block], inR1.at[g, index], sib_id)

    def input_middle(g):
        far = core + 2 * (1 - side)
        in_one[g, 0].wait()

        def add(row):
            here = pl.ds(row, 32)
            inB[g, here, :] = (
                tp[g, far, here, :].astype(F32) + inR1[g, 0, here, :].astype(F32)
            ).astype(BF16)

        tiles(share, 32, add, 2)
        in_two[g] = copies.start(("in two", g), inB.at[g], inR2.at[g], cross_id)

    def input_end(g):
        in_one[g, 1].wait()
        in_two[g].wait()

        def add(row):
            here = pl.ds(row, 32)
            igo[here, g * TOK_ROW : (g + 1) * TOK_ROW] = (
                tp[g, t, here, :].astype(F32)
                + inR1[g, 1, here, :].astype(F32)
                + inR2[g, here, :].astype(F32)
            ).astype(BF16)

        tiles(share, 32, add, 2)

    def small_sums():
        for index in range(5):
            small[index : index + 1, :] = jnp.sum(acc[index], axis=0, keepdims=True)
        small[UP_ROW : UP_ROW + 1, :] = jnp.sum(acc[UP_BIAS], axis=0, keepdims=True)
        lane = lax.broadcasted_iota(jnp.int32, (1, BAND), 1)
        lane_out = lax.broadcasted_iota(jnp.int32, (1, 2 * REL), 1)
        sub = lax.broadcasted_iota(jnp.int32, (8, BAND), 0)
        for h in range(heads):
            part = tacc[h]
            for size in (32, 16, 8):
                part = part[0:size] + pltpu.roll(part[size : 2 * size], BAND - 2 * size, 1)
            for size in (4, 2, 1):
                part = jnp.where(
                    lax.rem(sub // size, 2) == 1, pltpu.roll(part, BAND - 2 * size, 1), part
                )
            part = jnp.sum(part, axis=0, keepdims=True)
            low = jnp.sum(jnp.where(lane <= 448, part, 0.0), axis=1, keepdims=True)
            high = jnp.sum(jnp.where(lane >= 575, part, 0.0), axis=1, keepdims=True)
            middle = pltpu.roll(part, BAND - 448, 1)[:, 0 : 2 * REL]
            middle = jnp.where(
                lane_out == 0, low, jnp.where(lane_out == 2 * REL - 1, high, middle)
            )
            small[TABLE_ROW + h : TABLE_ROW + h + 1, 0 : 2 * REL] = middle

    for load in early[:4]:
        load.wait()
    for load in vectors[2:] + late:
        load.start()
    qkv(0)
    early[4].wait()
    attend(0)
    pl.semaphore_wait(barrier, 2 + len(grid.peers))
    reduce_start(0, 0)
    qkv(1)
    reduce_middle(0, 0)
    attend(1)
    reduce_start(0, 1)
    for load in vectors[2:]:
        load.wait()
    first_norm(0)
    reduce_middle(0, 1)
    for load in late:
        load.wait()
    feed_forward(0)
    reduce_start(1, 0)
    first_norm(1)
    reduce_middle(1, 0)
    feed_forward(1)
    reduce_start(1, 1)
    second_norm(0)
    reduce_middle(1, 1)
    feed_back(0)
    reduce_start(2, 0)
    second_norm(1)
    reduce_middle(2, 0)
    feed_back(1)
    reduce_start(2, 1)

    outs = []

    def put(source, target):
        copy = pltpu.make_async_copy(source, target, out_sems.at[len(outs)])
        copy.start()
        outs.append(copy)

    specs, turns, tail = stream_plan
    streams, inbox_row = [], 0
    for row, rows, order in specs:
        streams.append(
            Stream(copies, (grads, summed, inbox), inbox_row, row, rows, grid.plans[order])
        )
        inbox_row += grid.inbox_rows(order, rows)
    turns, chores = list(turns), []

    def advance(index):
        if index < 0:
            if chores:
                chores.pop(0)()
            return
        stream = streams[index]
        if not stream.done():
            stream.turn()
            if stream.done():
                rows = pl.ds(stream.first, stream.count)
                put(summed.at[rows], g_h.at[rows])

    def mark():
        for index in turns.pop(0) if turns else ():
            advance(index)

    grads[0:ff, :] = dot(act[...], f2[...], 0, 0).astype(BF16)
    mark()
    reduce_middle(2, 1)
    grads[ff : ff + width, :] = dot(f1[...], preg[...], 0, 0).astype(BF16)
    mark()
    first_back(0)
    wk[...] = wkT[...].T
    wv[...] = wvT[...].T
    wq[...] = wqT[...].T
    mark()
    attend_back(0, mark)
    first_back(1)
    mark()
    attend_back(1, mark)
    base = ff + width
    hw = heads * DH
    grads[base : base + hw, :] = dot(ctx[...], f3[...], 0, 0).astype(BF16)
    mark()
    grads[base + hw : base + 2 * hw, :] = dot(dqT[...], plow[...]).astype(BF16)
    mark()
    grads[base + 2 * hw : base + 3 * hw, :] = dot(kgT[...], hid[...]).astype(BF16)
    grads[base + 3 * hw : base + 4 * hw, :] = dot(vgT[...], hid[...]).astype(BF16)
    mark()
    small_sums()
    waiting = [copies.start("small", small.at[pl.ds(0, 8)], smallR.at[0, pl.ds(0, 8)], sib_id)]
    mark()
    input_part(0)
    mark()
    input_part(1)
    mark()

    def small_next(bit):
        waiting.pop().wait()
        if bit == 0:
            small[0:8, :] = small[0:8, :] + smallR[0, 0:8, :]
        else:
            small[...] = small[...] + smallR[bit]
        if bit < bits:
            waiting.append(
                copies.start(("small", bit), small, smallR.at[bit + 1], grid.across[bit])
            )
        else:
            put(small, small_h)

    def input_done(g):
        input_end(g)
        if g == chunks - 1:
            put(igo, ig_h)

    def pooled_done():
        for g in range(chunks):
            shares["po", g].wait()
        put(po, po_h)

    chores += [partial(input_middle, 0), partial(small_next, 0), partial(input_middle, 1)]
    chores += [pooled_done] + [partial(small_next, bit) for bit in range(1, bits + 1)]
    chores += [partial(input_done, g) for g in range(chunks)]
    for index in tail:
        advance(index)
    while chores:
        advance(-1)
    while not all(stream.done() for stream in streams):
        advance([stream.done() for stream in streams].index(False))
    for copy in outs:
        copy.wait()


def finish_kernel(
    plan, po_h, ig_h, g_h, small_h, po_o, ig_o, q_o, k_o, v_o, wo_o, up_o, dn_o, *rest
):
    tab_o, fg_o, fs_o, ub_o, db_o, sg_o, ss_o, po, ig, low, wide, small, tab, *vectors = rest
    *vectors, in_sems, out_sems = vectors
    targets = (dn_o, up_o, wo_o, q_o, k_o, v_o)
    get_small = pltpu.make_async_copy(small_h, small, in_sems.at[len(plan)])
    get_po = pltpu.make_async_copy(po_h, po, in_sems.at[len(plan) + 1])
    get_ig = pltpu.make_async_copy(ig_h, ig, in_sems.at[len(plan) + 2])
    gets = [
        pltpu.make_async_copy(
            g_h.at[pl.ds(row, rows)], low.at[pl.ds(row, rows)], in_sems.at[index]
        )
        for index, (row, rows, unused, unused_row) in enumerate(plan)
    ]
    for get in [get_small] + gets + [get_po, get_ig]:
        get.start()
    puts = []

    def put(source, target):
        copy = pltpu.make_async_copy(source, target, out_sems.at[len(puts)])
        copy.start()
        puts.append(copy)

    get_small.wait()
    for vector, row, out in zip(
        vectors,
        (FIRST_GAIN, FIRST_SHIFT, UP_ROW, DOWN_BIAS, SECOND_GAIN, SECOND_SHIFT),
        (fg_o, fs_o, ub_o, db_o, sg_o, ss_o),
    ):
        vector[...] = small[row, : vector.shape[0]]
        put(vector, out)
    tab[...] = small[TABLE_ROW : TABLE_ROW + tab.shape[0], : 2 * REL]
    put(tab, tab_o)
    for get, (row, rows, index, target_row) in zip(gets, plan):
        get.wait()

        def widen(here):
            where = pl.ds(pl.multiple_of(row + here, 32), 32)
            wide[where, :] = low[where, :].astype(F32)

        tiles(rows, 32, widen)
        put(wide.at[pl.ds(row, rows)], targets[index].at[pl.ds(target_row, rows)])
    get_po.wait()
    put(po, po_o)
    get_ig.wait()
    put(ig, ig_o)
    for copy in puts:
        copy.wait()


def finish(pooled_out, input_grad, grads, small, heads, ff, width):
    hw = heads * DH
    total = grads.shape[0]
    plan, row = [], 0
    for index, rows in enumerate((ff, width, hw, hw, hw, hw)):
        for start in range(0, rows, 384):
            size = min(384, rows - start)
            plan.append((row + start, size, index, start))
        row += rows
    vector = jax.ShapeDtypeStruct((width,), F32)
    any_spec = pl.BlockSpec(memory_space=pl.ANY)
    outs = pl.pallas_call(
        partial(finish_kernel, tuple(plan)),
        name="finish",
        out_shape=(
            jax.ShapeDtypeStruct(pooled_out.shape, BF16),
            jax.ShapeDtypeStruct(input_grad.shape, BF16),
            jax.ShapeDtypeStruct((hw, width), F32),
            jax.ShapeDtypeStruct((hw, width), F32),
            jax.ShapeDtypeStruct((hw, width), F32),
            jax.ShapeDtypeStruct((hw, width), F32),
            jax.ShapeDtypeStruct((width, ff), F32),
            jax.ShapeDtypeStruct((ff, width), F32),
            jax.ShapeDtypeStruct((heads, 2 * REL), F32),
            vector,
            vector,
            jax.ShapeDtypeStruct((ff,), F32),
            vector,
            vector,
            vector,
        ),
        in_specs=[any_spec] * 4,
        out_specs=(any_spec,) * 15,
        scratch_shapes=[
            pltpu.VMEM(pooled_out.shape, BF16),
            pltpu.VMEM(input_grad.shape, BF16),
            pltpu.VMEM((total, width), BF16),
            pltpu.VMEM((total, width), F32),
            pltpu.VMEM((SMALL_ROWS, width), F32),
            pltpu.VMEM((heads, 2 * REL), F32),
            pltpu.VMEM((width,), F32),
            pltpu.VMEM((width,), F32),
            pltpu.VMEM((ff,), F32),
            pltpu.VMEM((width,), F32),
            pltpu.VMEM((width,), F32),
            pltpu.VMEM((width,), F32),
            pltpu.SemaphoreType.DMA((len(plan) + 3,)),
            pltpu.SemaphoreType.DMA((len(plan) + 9,)),
        ],
        compiler_params=pltpu.CompilerParams(vmem_limit_bytes=64_000_000),
    )(pooled_out, input_grad, grads, small)
    po, ig, qg, kg, vg, wo, up, dn, tab, fg, fs, ub, db, sg, ss = outs
    return po, ig.T, qg.T, kg.T, vg.T, wo, tab, fg, fs, up, ub, dn, db, sg, ss


def local(n_dp, *args):
    (
        hidden_in,
        segment_ids,
        query_weight,
        key_weight,
        value_weight,
        output_weight,
        position_table,
        first_gain,
        first_shift,
        up_weight,
        up_bias,
        down_weight,
        down_bias,
        second_gain,
        second_shift,
        cotangent,
    ) = args
    tokens, width = hidden_in.shape
    chunks = tokens // TOK_ROW
    pooled = tokens // 2
    half = HALF_ROW // 2
    heads = position_table.shape[0]
    hw = heads * DH
    ff = up_weight.shape[1]
    share = width // 4
    specs, row = [], 0
    for order, rows in PIECES:
        specs.append((row, rows, order))
        row += rows
    plan = (tuple(specs), TURNS, TAIL)
    bits = n_dp.bit_length() - 1
    links = 5 if n_dp == 8 else bits + 3
    total = ff + width + 4 * hw
    cfg = (n_dp, heads, HALF_ROW, chunks, width, ff, share, plan)
    vmem = lambda *shape: pltpu.VMEM(shape, BF16)
    wide = lambda *shape: pltpu.VMEM(shape, F32)
    slots = 3 * chunks
    inbox_rows = total * 7 // 4 + max(bits - 3, 0) * total // 8
    any_spec = pl.BlockSpec(memory_space=pl.ANY)
    scratch = [
        pltpu.VMEM((tokens,), jnp.int32),
        wide(width),
        wide(width),
        wide(ff),
        wide(width),
        wide(width),
        wide(width),
        wide(heads, 2 * REL),
        vmem(tokens, width),
        vmem(width, hw),
        vmem(width, hw),
        vmem(width, hw),
        vmem(hw, width),
        vmem(width, ff),
        vmem(ff, width),
        vmem(pooled, width),
        vmem(hw, width),
        vmem(hw, width),
        vmem(hw, width),
        vmem(HALF_ROW, TOK_ROW),
        wide(pooled, 1),
        wide(heads, 64, BAND),
        wide(heads, 64, BAND),
        vmem(pooled, width),
        wide(pooled // 2, width),
        vmem(pooled, hw),
        vmem(hw, pooled),
        vmem(hw, tokens),
        vmem(hw, tokens),
        wide(HALF_ROW, TOK_ROW),
        wide(chunks * heads, HALF_ROW, TOK_ROW),
        vmem(chunks * heads, HALF_ROW, TOK_ROW),
        vmem(HALF_ROW, TOK_ROW),
        vmem(pooled, hw),
        vmem(slots, HALF_ROW, width),
        vmem(slots, half, width),
        vmem(slots, half, width),
        vmem(slots, half, width),
        vmem(pooled, width),
        vmem(pooled, width),
        vmem(pooled, width),
        wide(pooled // 2, width),
        wide(pooled // 2, width),
        wide(pooled // 2, 1),
        wide(HALF_ROW, ff),
        vmem(pooled, ff),
        wide(pooled, ff),
        vmem(pooled, ff),
        wide(pooled // 2, width),
        vmem(pooled, width),
        vmem(pooled, hw),
        vmem(hw, pooled),
        vmem(hw, pooled),
        vmem(hw, tokens),
        vmem(hw, tokens),
        vmem(width, TOK_ROW),
        vmem(chunks, 4, share, TOK_ROW),
        vmem(chunks, 2, share, TOK_ROW),
        vmem(chunks, share, TOK_ROW),
        vmem(chunks, share, TOK_ROW),
        vmem(share, tokens),
        vmem(total, width),
        vmem(total, width),
        vmem(inbox_rows, width),
        wide(6, 8, width),
        wide(SMALL_ROWS, width),
        wide(bits + 1, SMALL_ROWS, width),
        pltpu.SemaphoreType.DMA((16,)),
        pltpu.SemaphoreType.DMA((len(specs) + 3,)),
        pltpu.SemaphoreType.DMA((SENDS,)),
        pltpu.SemaphoreType.DMA((links * len(specs) + RECEIVES,)),
    ]
    pooled_out, input_grad, grads, small = pl.pallas_call(
        partial(fused, cfg),
        name="layer",
        out_shape=(
            jax.ShapeDtypeStruct((pooled, width), BF16),
            jax.ShapeDtypeStruct((share, tokens), BF16),
            jax.ShapeDtypeStruct((total, width), BF16),
            jax.ShapeDtypeStruct((SMALL_ROWS, width), F32),
        ),
        in_specs=[any_spec] * 16,
        out_specs=(any_spec,) * 4,
        scratch_shapes=scratch,
        compiler_params=pltpu.CompilerParams(
            collective_id=0, has_side_effects=True, vmem_limit_bytes=64_000_000
        ),
    )(
        segment_ids,
        first_gain,
        first_shift,
        up_bias,
        down_bias,
        second_gain,
        second_shift,
        position_table,
        hidden_in,
        query_weight.T,
        key_weight.T,
        value_weight.T,
        output_weight,
        up_weight,
        down_weight,
        cotangent,
    )
    return finish(pooled_out, input_grad, grads, small, heads, ff, width)


def solution(mesh):
    return jax.shard_map(
        partial(local, mesh.shape["dp"]),
        mesh=mesh,
        in_specs=(
            P("dp", None),
            P("dp"),
            P(None, "tensor"),
            P(None, "tensor"),
            P(None, "tensor"),
            P("tensor", None),
            P("tensor", None),
            P(),
            P(),
            P(None, "tensor"),
            P("tensor"),
            P("tensor", None),
            P(),
            P(),
            P(),
            P("dp", None),
        ),
        out_specs=(
            P("dp", None),
            P("dp", "tensor"),
            P(None, "tensor"),
            P(None, "tensor"),
            P(None, "tensor"),
            P("tensor", None),
            P("tensor", None),
            P(),
            P(),
            P(None, "tensor"),
            P("tensor"),
            P("tensor", None),
            P(),
            P(),
            P(),
        ),
        check_vma=False,
    )
```

```python
import math
from functools import partial

import jax
import jax.numpy as jnp
from jax import lax
from jax.experimental import pallas as pl
from jax.experimental.pallas import tpu as pltpu
from jax.sharding import PartitionSpec as P

DH = 64
TOK_ROW = 512
LANES = 128
HALF_ROW = TOK_ROW // 2
REL = 64
EPSILON = 1e-06
NEGATIVE = -1e30
MESH = pl.DeviceIdType.MESH
F32 = jnp.float32
BF16 = jnp.bfloat16

FIRST_GAIN, FIRST_SHIFT, DOWN_BIAS, SECOND_GAIN, SECOND_SHIFT, UP_BIAS = range(6)
UP_ROW, TABLE_ROW, SMALL_ROWS = 8, 9, 16
BAND = 1024
ROLL = 1152
SENDS = 28
RECEIVES = 24
PIECES = (('Y', 192), ('Z', 128), ('Z', 64), ('Y', 128), ('Y', 128), ('Z', 64), ('Y', 64), ('Z', 64), ('Y', 128), ('Y', 192), ('Z', 128), ('Y', 128), ('Y', 128), ('Z', 128), ('Y', 64), ('Y', 192), ('Y', 128), ('Y', 128), ('Y', 128))
TURNS = [[2, 3, 1, 4], [12], [], [2, 3, 9], [4], [2, 10, 0], [1, 12], [3, 6], [9, 2, 1, 4], [3, 11], [], [], [0, 15, 4], [6, 10, 3, 2], [1], [4, 12, 11, 17]]
TAIL = [10, 3, 9, 2, -1, 12, 15, 4, 1, -1, 0, 9, 2, 6, -1, 12, 17, 10, 11, -1, 1, 3, 0, 12, -1, 7, 18, 15, 9, -1, 13, 4, 6, 10, -1, 11, 17, 8, 1, -1, 0, 14, 12, 7, -1, 15, 6, 5, 16, -1, 18, 9, 10, 8, -1, 13, 11, 14, 0, -1, 17, 6, 5, 7, -1, 16, 15, 18, 9, -1, 13, 10, 8, 17, -1, 14, 5, 11, 0, -1, 18, 16, 6, 8, -1, 7, 14, 13, 15, -1, 18, 5, 16, 17, -1, 8, 11, 14, 7, -1, 16, 13, 18, 7, -1, 8, 15, 14, 13, -1, 5, 16, 17, 5, -1, 7, 18, 8, 14, -1, 13, 16, 5]
U_SOFT, U_SBACK, U_NORM, U_GELU = 8, 2, 4, 2


def dot(left, right, left_dim=1, right_dim=0):
    return lax.dot_general(
        left, right, (((left_dim,), (right_dim,)), ((), ())), preferred_element_type=F32
    )


def tiles(count, step, body, unroll=1):
    unroll = math.gcd(unroll, count // step)
    stride = step * unroll

    def one(index, unused):
        for part in range(unroll):
            body(pl.multiple_of(index * stride + part * step, step))
        return unused

    if count == stride:
        for row in range(0, count, step):
            body(row)
    else:
        lax.fori_loop(0, count // stride, one, 0)


def across_row(column):
    return jnp.concatenate([column] * (TOK_ROW // LANES), axis=1)


def fold(value):
    total = value[0:8]
    for start in range(8, value.shape[0], 8):
        total = total + value[start : start + 8]
    return total


class Copy:
    def __init__(self, copy, send, recv, free):
        self.copy, self.send, self.recv, self.free = copy, send, recv, free

    def start(self):
        if self.send is None:
            self.copy.start()
        else:
            pl.when(self.send)(self.copy.start)

    def wait(self):
        if self.send is None:
            self.copy.wait()
        else:
            pl.when(self.send)(self.copy.wait_send)
            pl.when(self.recv)(self.copy.wait_recv)
        self.free()


class Copies:
    def __init__(self, send_sems, recv_sems):
        self.send_sems, self.recv_sems = send_sems, recv_sems
        self.idle, self.keys = list(range(SENDS)), {}

    def start(self, key, source, target, device, send=None, recv=None):
        index = self.idle.pop(0)
        copy = Copy(
            pltpu.make_async_remote_copy(
                src_ref=source,
                dst_ref=target,
                send_sem=self.send_sems.at[index],
                recv_sem=self.recv_sems.at[self.keys.setdefault(key, len(self.keys))],
                device_id=device,
                device_id_type=MESH,
            ),
            send,
            recv,
            lambda: self.idle.append(index),
        )
        copy.start()
        return copy


class Grid:
    def __init__(self, n_dp, d, t):
        self.bits = n_dp.bit_length() - 1
        self.mine = [lax.rem(d // (1 << bit), 2) for bit in range(self.bits)]
        self.across = [(d + (1 - 2 * self.mine[b]) * (1 << b), t) for b in range(self.bits)]
        self.peers = list(self.across)
        self.plans = {}
        if n_dp == 8:
            z = d // 2
            middle = jnp.logical_or(z == 1, z == 2)
            end = jnp.logical_not(middle)
            upper = z // 2
            facing = (d + (3 - 2 * z) * 2, t)
            self.peers.append(facing)
            everyone = (None, None, None, "y")
            inner = (middle, middle, middle)
            y = ("half", self.across[0], self.mine[0])
            y_back = ("back", self.across[0], self.mine[0])
            gather = ("whole", self.across[1], 0, end, middle, middle, "z")
            spread = ("same", self.across[1], 0, middle, end, middle, "z")
            mid = ("half", facing, upper) + inner + ("mid",)
            mid_back = ("back", facing, upper) + inner + ("mid_back",)
            y_inner = inner + ("y",)
            y_out = ("y_back",)
            self.plans["Y"] = (
                y + everyone,
                gather,
                mid,
                mid_back,
                spread,
                y_back + everyone[:3] + y_out,
            )
            self.plans["Z"] = (gather, mid, y + y_inner, y_back + inner + y_out, mid_back, spread)
        else:
            everyone = (None, None, None)
            halving = list(range(min(3, self.bits)))
            plan = [("half", self.across[b], self.mine[b]) + everyone + (b,) for b in halving]
            plan += [
                ("whole", self.across[b], 0) + everyone + (b,)
                for b in range(len(halving), self.bits)
            ]
            plan += [
                ("back", self.across[b], self.mine[b]) + everyone + (self.bits + b,)
                for b in reversed(halving)
            ]
            self.plans["Y"] = self.plans["Z"] = tuple(plan)

    def inbox_rows(self, order, rows):
        total = 0
        for kind, *unused in self.plans[order]:
            if kind == "half":
                rows //= 2
            if kind in ("half", "whole"):
                total += rows
        return total


class Stream:
    def __init__(self, copies, buffers, inbox_row, row, rows, plan):
        self.copies, self.plan = copies, plan
        self.grads, self.summed, self.inbox = buffers
        self.inbox_row, self.rows, self.pos = inbox_row, rows, row
        self.first, self.count = row, rows
        self.step, self.pending = 0, None

    def begin(self):
        kind, device, mine, send, recv, unused, link = self.plan[self.step]
        size = self.rows
        at = self.pos
        if kind == "half":
            size //= 2
            self.keep = pl.multiple_of(self.pos + mine * size, 16)
            at = pl.multiple_of(self.pos + (1 - mine) * size, 16)
        if kind in ("half", "whole"):
            source = self.grads.at[pl.ds(at, size)]
            target = self.inbox.at[pl.ds(self.inbox_row, size)]
        else:
            source = target = self.summed.at[pl.ds(at, size)]
        self.pending = self.copies.start((self.first, link), source, target, device, send, recv)
        self.size = size

    def finish(self):
        kind, device, mine, send, recv, adds, link = self.plan[self.step]
        self.pending.wait()
        self.step += 1
        if kind == "back":
            self.pos = pl.multiple_of(self.pos - mine * self.size, 16)
            self.rows = 2 * self.size
        elif kind != "same":
            if kind == "half":
                self.pos, self.rows = self.keep, self.size
            base, inbox_row, grads, inbox = self.pos, self.inbox_row, self.grads, self.inbox
            result = self.summed if self.plan[self.step][0] == "back" else grads
            step = 32 if self.size % 32 == 0 else 16

            def add(row):
                rows = pl.ds(pl.multiple_of(base + row, 16), step)
                arrived = inbox[pl.ds(pl.multiple_of(inbox_row + row, 16), step), :]
                result[rows, :] = (grads[rows, :].astype(F32) + arrived.astype(F32)).astype(BF16)

            def add_all():
                tiles(self.size, step, add, 2)

            if adds is None:
                add_all()
            else:
                pl.when(adds)(add_all)
            self.inbox_row += self.size

    def done(self):
        return self.step == len(self.plan)

    def turn(self):
        if self.pending is not None:
            self.finish()
            self.pending = None
        if not self.done():
            self.begin()


def fused(
    cfg,
    seg_h,
    first_gain_h,
    first_shift_h,
    up_bias_h,
    down_bias_h,
    second_gain_h,
    second_shift_h,
    tab_h,
    hid_h,
    wq_h,
    wk_h,
    wv_h,
    wo_h,
    up_h,
    dn_h,
    cot_h,
    po_h,
    ig_h,
    g_h,
    small_h,
    seg_ref,
    first_gain,
    first_shift,
    up_bias_in,
    down_bias_in,
    second_gain,
    second_shift,
    tab_ref,
    hid,
    wq,
    wk,
    wv,
    wo,
    up,
    dn,
    cot,
    wqT,
    wkT,
    wvT,
    dup,
    mask,
    stat,
    bias,
    tacc,
    plow,
    pown,
    q,
    qT,
    kT,
    vT,
    score,
    probs,
    problow,
    ds,
    ctx,
    arA,
    arR1,
    arB,
    arR2,
    f1,
    f2,
    f3,
    first_out,
    normed1,
    inv1,
    pre,
    act,
    gp,
    preg,
    sgrad,
    po,
    cg,
    cgT,
    dqT,
    kgT,
    vgT,
    f3dT,
    tp,
    inR1,
    inB,
    inR2,
    igo,
    grads,
    summed,
    inbox,
    acc,
    small,
    smallR,
    in_sems,
    out_sems,
    send_sems,
    recv_sems,
):
    n_dp, heads, rows_per, chunks, width, ff, share, stream_plan = cfg
    half = HALF_ROW // 2
    d = lax.axis_index("dp")
    t = lax.axis_index("tensor")
    core = lax.rem(t, 2)
    side = t // 2
    sib_id = (d, t + 1 - 2 * core)
    cross_id = (d, t + 2 - 4 * side)
    grid = Grid(n_dp, d, t)
    bits = grid.bits
    own = pl.multiple_of(core * half, half)
    away = pl.multiple_of((1 - core) * half, half)

    loads = [
        pltpu.make_async_copy(source, target, in_sems.at[index])
        for index, (source, target) in enumerate(
            [
                (hid_h, hid),
                (wk_h, wkT),
                (wv_h, wvT),
                (wq_h, wqT),
                (wo_h, wo),
                (up_h, up),
                (dn_h, dn),
                (cot_h, cot),
                (seg_h, seg_ref),
                (tab_h, tab_ref),
                (first_gain_h, first_gain),
                (first_shift_h, first_shift),
                (up_bias_h, up_bias_in),
                (down_bias_h, down_bias_in),
                (second_gain_h, second_gain),
                (second_shift_h, second_shift),
            ]
        )
    ]
    early, vectors, late = loads[:5], loads[8:], loads[5:8]
    for load in vectors[:2] + early:
        load.start()
    barrier = pltpu.get_barrier_semaphore()
    for device in [sib_id, cross_id] + grid.peers:
        pl.semaphore_signal(barrier, inc=1, device_id=device, device_id_type=MESH)

    row_i = lax.broadcasted_iota(jnp.int32, (HALF_ROW, TOK_ROW), 0)
    col_i = lax.broadcasted_iota(jnp.int32, (HALF_ROW, TOK_ROW), 1)
    dup[...] = jnp.where(col_i // 2 == row_i, 1.0, 0.0).astype(BF16)
    evens = jnp.where(col_i == 2 * row_i, 1.0, 0.0).astype(BF16)
    vectors[0].wait()
    segk = [
        seg_ref[g * TOK_ROW : (g + 1) * TOK_ROW].astype(F32).reshape(1, TOK_ROW)
        for g in range(chunks)
    ]
    for g in range(chunks):
        rows = jnp.broadcast_to(segk[g], (LANES, TOK_ROW)).astype(BF16)
        column = across_row(dot(evens, rows, 1, 1))
        mask[g] = jnp.where(column == segk[g], 0.0, NEGATIVE)
    vectors[1].wait()
    for h in range(heads):
        table = jnp.concatenate(
            [
                jnp.broadcast_to(tab_ref[h : h + 1, 0:1], (REL, 512)),
                jnp.broadcast_to(tab_ref[h : h + 1, :], (REL, 2 * REL)),
                jnp.broadcast_to(tab_ref[h : h + 1, 2 * REL - 1 : 2 * REL], (REL, 512)),
            ],
            axis=1,
        )
        bias[h] = pltpu.roll(table, ROLL - 64, 1, stride=2, stride_axis=0)[:, :BAND]
    tacc[...] = jnp.zeros_like(tacc)
    acc[...] = jnp.zeros_like(acc)
    small[...] = jnp.zeros_like(small)

    copies = Copies(send_sems, recv_sems)

    reduce_one, reduce_two = {}, {}

    def reduce_start(which, g):
        slot = which * chunks + g
        reduce_one[slot] = copies.start(("one", g), arA.at[slot, pl.ds(away, half)], arR1.at[slot], sib_id)

    def reduce_middle(which, g):
        slot = which * chunks + g
        reduce_one[slot].wait()

        def add(row):
            mine = arA[slot, pl.ds(pl.multiple_of(own + row, 32), 32), :].astype(F32)
            arB[slot, pl.ds(row, 32), :] = (
                mine + arR1[slot, pl.ds(row, 32), :].astype(F32)
            ).astype(BF16)

        tiles(half, 32, add, 2)
        reduce_two[slot] = copies.start(("two", g, which % 2), arB.at[slot], arR2.at[slot], cross_id)

    def reduced(which, g, row):
        slot = which * chunks + g
        return arB[slot, pl.ds(row, 16), :].astype(F32) + arR2[slot, pl.ds(row, 16), :].astype(F32)

    shares = {}

    def share_start(name, buffer, g):
        rows = buffer.at[pl.ds(pl.multiple_of(g * HALF_ROW + own, half), half)]
        key = ("po" if name == "po" else "share", g)
        shares[name, g] = copies.start(key, rows, rows, sib_id)

    def qkv(g):
        tokens = hid[g * TOK_ROW : (g + 1) * TOK_ROW, :]
        pooled = slice(g * HALF_ROW, (g + 1) * HALF_ROW)
        cols = slice(g * TOK_ROW, (g + 1) * TOK_ROW)
        plow[pooled, :] = (dot(dup[...], tokens) * 0.5).astype(BF16)
        mine = hid[pl.ds(pl.multiple_of(g * TOK_ROW + core * HALF_ROW, HALF_ROW), HALF_ROW), :]
        pown[g * half : (g + 1) * half, :] = dot(dup[0:half, 0:HALF_ROW], mine) * 0.5
        kT[:, cols] = dot(wkT[...], tokens, 1, 1).astype(BF16)
        vT[:, cols] = dot(wvT[...], tokens, 1, 1).astype(BF16)
        scale = 1.0 / math.sqrt(DH)
        q[pooled, :] = (dot(plow[pooled, :], wqT[...], 1, 1) * scale).astype(BF16)
        qT[:, pooled] = (dot(wqT[...], plow[pooled, :], 1, 1) * scale).astype(BF16)

    def attend(g):
        pooled = slice(g * HALF_ROW, (g + 1) * HALF_ROW)
        cols = slice(g * TOK_ROW, (g + 1) * TOK_ROW)
        for h in range(heads):
            lanes = slice(h * DH, (h + 1) * DH)
            slot = g * heads + h
            score[...] = dot(q[pooled, lanes], kT[lanes, cols])

            def add_bias(row):
                here = pl.ds(row, 32)
                band, part = 512 - 128 * (row // 64), row % 64
                if not isinstance(row, int):
                    part = pl.multiple_of(lax.rem(row, 64), 32)
                    band = pl.multiple_of(band, 128)
                raw = score[here, :] + bias[h, pl.ds(part, 32), pl.ds(band, TOK_ROW)]
                raw = raw + mask[g, here, :]
                score[here, :] = raw
                peak = jnp.max(raw, axis=-1, keepdims=True)
                stat[0, here, :] = jnp.broadcast_to(peak, (32, LANES))

            def weigh(row):
                here = pl.ds(row, 32)
                weights = jnp.exp(score[here, :] - across_row(stat[0, here, :]))
                score[here, :] = weights
                total = jnp.sum(weights, axis=-1, keepdims=True)
                stat[1, here, :] = jnp.broadcast_to(total, (32, LANES))

            def divide(row):
                here = pl.ds(row, 32)
                prob = score[here, :] * across_row(1.0 / stat[1, here, :])
                probs[slot, here, :] = prob
                problow[slot, here, :] = prob.astype(BF16)

            for step in (add_bias, weigh, divide):
                tiles(HALF_ROW, 32, step, U_SOFT)
            ctx[pooled, lanes] = dot(problow[slot], vT[lanes, cols], 1, 1).astype(BF16)
        arA[g] = dot(ctx[pooled, :], wo[...]).astype(BF16)

    def first_norm(g):
        reduce_two[g].wait()
        gain, shift = first_gain[...].reshape(1, width), first_shift[...].reshape(1, width)

        def one(row):
            here = pl.ds(pl.multiple_of(g * half + row, 16), 16)
            value = pown[here, :] + reduced(0, g, row)
            centred = value - jnp.mean(value, axis=-1, keepdims=True)
            inverse = lax.rsqrt(jnp.mean(centred * centred, axis=-1, keepdims=True) + EPSILON)
            normed = centred * inverse
            out = normed * gain + shift
            normed1[here, :] = normed
            inv1[here, :] = inverse
            first_out[here, :] = out
            f1[pl.ds(pl.multiple_of(g * HALF_ROW + own + row, 16), 16), :] = out.astype(BF16)

        tiles(half, 16, one, U_NORM)
        share_start("f1", f1, g)

    def feed_forward(g):
        shares["f1", g].wait()
        pooled = slice(g * HALF_ROW, (g + 1) * HALF_ROW)
        pre[...] = dot(f1[pooled, :], up[...])
        up_bias = up_bias_in[...].reshape(1, ff)

        def one(row):
            value = pre[pl.ds(row, 16), :] + up_bias
            cdf = 0.5 * (1.0 + lax.erf(value * (1.0 / math.sqrt(2.0))))
            density = jnp.exp(-0.5 * value * value) * (1.0 / math.sqrt(2.0 * math.pi))
            here = pl.ds(pl.multiple_of(g * HALF_ROW + row, 16), 16)
            act[here, :] = (value * cdf).astype(BF16)
            gp[here, :] = cdf + value * density

        tiles(HALF_ROW, 16, one, U_GELU)
        arA[chunks + g] = dot(act[pooled, :], dn[...]).astype(BF16)

    def second_norm(g):
        reduce_two[chunks + g].wait()
        gain, shift = second_gain[...].reshape(1, width), second_shift[...].reshape(1, width)
        down_bias = down_bias_in[...].reshape(1, width)

        def one(row):
            here = pl.ds(pl.multiple_of(g * half + row, 16), 16)
            full = pl.ds(pl.multiple_of(g * HALF_ROW + own + row, 16), 16)
            value = first_out[here, :] + reduced(1, g, row) + down_bias
            centred = value - jnp.mean(value, axis=-1, keepdims=True)
            inverse = lax.rsqrt(jnp.mean(centred * centred, axis=-1, keepdims=True) + EPSILON)
            normed = centred * inverse
            po[full, :] = (normed * gain + shift).astype(BF16)
            upstream = cot[full, :].astype(F32)
            scaled = upstream * gain
            grad = inverse * (
                scaled
                - jnp.mean(scaled, axis=-1, keepdims=True)
                - normed * jnp.mean(scaled * normed, axis=-1, keepdims=True)
            )
            sgrad[here, :] = grad
            f2[full, :] = grad.astype(BF16)
            acc[SECOND_GAIN] += fold(upstream * normed)
            acc[SECOND_SHIFT] += fold(upstream)
            acc[DOWN_BIAS] += fold(grad)

        tiles(half, 16, one, U_NORM)
        share_start("f2", f2, g)
        share_start("po", po, g)

    def feed_back(g):
        shares["f2", g].wait()
        pooled = slice(g * HALF_ROW, (g + 1) * HALF_ROW)
        pre[...] = dot(f2[pooled, :], dn[...], 1, 1)

        def one(row):
            here = pl.ds(pl.multiple_of(g * HALF_ROW + row, 16), 16)
            low = (gp[here, :] * pre[pl.ds(row, 16), :]).astype(BF16)
            preg[here, :] = low
            acc[UP_BIAS, :, :ff] += fold(low.astype(F32))

        tiles(HALF_ROW, 16, one, U_GELU)
        arA[2 * chunks + g] = dot(preg[pooled, :], up[...], 1, 1).astype(BF16)

    def first_back(g):
        reduce_two[2 * chunks + g].wait()
        gain = first_gain[...].reshape(1, width)

        def one(row):
            here = pl.ds(pl.multiple_of(g * half + row, 16), 16)
            full = pl.ds(pl.multiple_of(g * HALF_ROW + own + row, 16), 16)
            upstream = reduced(2, g, row) + sgrad[here, :]
            normed = normed1[here, :]
            scaled = upstream * gain
            grad = inv1[here, :] * (
                scaled
                - jnp.mean(scaled, axis=-1, keepdims=True)
                - normed * jnp.mean(scaled * normed, axis=-1, keepdims=True)
            )
            f3[full, :] = grad.astype(BF16)
            acc[FIRST_GAIN] += fold(upstream * normed)
            acc[FIRST_SHIFT] += fold(upstream)

        tiles(half, 16, one, U_NORM)
        share_start("f3", f3, g)

    def attend_back(g, after):
        shares["f3", g].wait()
        pooled = slice(g * HALF_ROW, (g + 1) * HALF_ROW)
        cols = slice(g * TOK_ROW, (g + 1) * TOK_ROW)
        cg[pooled, :] = dot(f3[pooled, :], wo[...], 1, 1).astype(BF16)
        cgT[:, pooled] = dot(wo[...], f3[pooled, :], 1, 1).astype(BF16)
        for h in range(heads):
            lanes = slice(h * DH, (h + 1) * DH)
            slot = g * heads + h
            score[...] = dot(cg[pooled, lanes], vT[lanes, cols])

            def one(row):
                block = row // 64
                part = pl.multiple_of(lax.rem(row, 64), 32)
                band = pl.ds(pl.multiple_of(512 - 128 * block, 128), TOK_ROW)
                prob = probs[slot, pl.ds(row, 32), :]
                prob_grad = score[pl.ds(row, 32), :]
                inner = jnp.sum(prob * prob_grad, axis=-1, keepdims=True)
                grad = prob * (prob_grad - inner)
                ds[pl.ds(row, 32), :] = grad.astype(BF16)
                tacc[h, pl.ds(part, 32), band] += grad

            tiles(HALF_ROW, 32, one, U_SBACK)
            scale = 1.0 / math.sqrt(DH)
            dqT[lanes, pooled] = (dot(kT[lanes, cols], ds[...], 1, 1) * scale).astype(BF16)
            kgT[lanes, cols] = dot(qT[lanes, pooled], ds[...]).astype(BF16)
            vgT[lanes, cols] = dot(cgT[lanes, pooled], problow[slot]).astype(BF16)
            after()

    in_one, in_two = {}, {}

    def input_part(g):
        pooled = slice(g * HALF_ROW, (g + 1) * HALF_ROW)
        cols = slice(g * TOK_ROW, (g + 1) * TOK_ROW)
        doubled = (dot(dqT[:, pooled], dup[...]) * 0.5).astype(BF16)
        f3dT[...] = (dot(f3[pooled, :], dup[...], 0, 0) * 0.125).astype(BF16)
        for b in range(4):
            rows = slice(b * share, (b + 1) * share)
            total = dot(wk[rows, :], kgT[:, cols]) + dot(wv[rows, :], vgT[:, cols])
            total = total + dot(wq[rows, :], doubled) + f3dT[rows, :].astype(F32)
            tp[g, b] = total.astype(BF16)
        for index, block in enumerate((1 - core + 2 * (1 - side), 1 - core + 2 * side)):
            in_one[g, index] = copies.start(("in", g, index), tp.at[g, block], inR1.at[g, index], sib_id)

    def input_middle(g):
        far = core + 2 * (1 - side)
        in_one[g, 0].wait()

        def add(row):
            here = pl.ds(row, 32)
            inB[g, here, :] = (
                tp[g, far, here, :].astype(F32) + inR1[g, 0, here, :].astype(F32)
            ).astype(BF16)

        tiles(share, 32, add, 2)
        in_two[g] = copies.start(("in two", g), inB.at[g], inR2.at[g], cross_id)

    def input_end(g):
        in_one[g, 1].wait()
        in_two[g].wait()

        def add(row):
            here = pl.ds(row, 32)
            igo[here, g * TOK_ROW : (g + 1) * TOK_ROW] = (
                tp[g, t, here, :].astype(F32)
                + inR1[g, 1, here, :].astype(F32)
                + inR2[g, here, :].astype(F32)
            ).astype(BF16)

        tiles(share, 32, add, 2)

    def small_sums():
        for index in range(5):
            small[index : index + 1, :] = jnp.sum(acc[index], axis=0, keepdims=True)
        small[UP_ROW : UP_ROW + 1, :] = jnp.sum(acc[UP_BIAS], axis=0, keepdims=True)
        lane = lax.broadcasted_iota(jnp.int32, (1, BAND), 1)
        lane_out = lax.broadcasted_iota(jnp.int32, (1, 2 * REL), 1)
        sub = lax.broadcasted_iota(jnp.int32, (8, BAND), 0)
        for h in range(heads):
            part = tacc[h]
            for size in (32, 16, 8):
                part = part[0:size] + pltpu.roll(part[size : 2 * size], BAND - 2 * size, 1)
            for size in (4, 2, 1):
                part = jnp.where(
                    lax.rem(sub // size, 2) == 1, pltpu.roll(part, BAND - 2 * size, 1), part
                )
            part = jnp.sum(part, axis=0, keepdims=True)
            low = jnp.sum(jnp.where(lane <= 448, part, 0.0), axis=1, keepdims=True)
            high = jnp.sum(jnp.where(lane >= 575, part, 0.0), axis=1, keepdims=True)
            middle = pltpu.roll(part, BAND - 448, 1)[:, 0 : 2 * REL]
            middle = jnp.where(
                lane_out == 0, low, jnp.where(lane_out == 2 * REL - 1, high, middle)
            )
            small[TABLE_ROW + h : TABLE_ROW + h + 1, 0 : 2 * REL] = middle

    for load in early[:4]:
        load.wait()
    for load in vectors[2:] + late:
        load.start()
    qkv(0)
    early[4].wait()
    attend(0)
    pl.semaphore_wait(barrier, 2 + len(grid.peers))
    reduce_start(0, 0)
    qkv(1)
    reduce_middle(0, 0)
    attend(1)
    reduce_start(0, 1)
    for load in vectors[2:]:
        load.wait()
    first_norm(0)
    reduce_middle(0, 1)
    for load in late:
        load.wait()
    feed_forward(0)
    reduce_start(1, 0)
    first_norm(1)
    reduce_middle(1, 0)
    feed_forward(1)
    reduce_start(1, 1)
    second_norm(0)
    reduce_middle(1, 1)
    feed_back(0)
    reduce_start(2, 0)
    second_norm(1)
    reduce_middle(2, 0)
    feed_back(1)
    reduce_start(2, 1)

    outs = []

    def put(source, target):
        copy = pltpu.make_async_copy(source, target, out_sems.at[len(outs)])
        copy.start()
        outs.append(copy)

    specs, turns, tail = stream_plan
    streams, inbox_row = [], 0
    for row, rows, order in specs:
        streams.append(
            Stream(copies, (grads, summed, inbox), inbox_row, row, rows, grid.plans[order])
        )
        inbox_row += grid.inbox_rows(order, rows)
    turns, chores = list(turns), []

    def advance(index):
        if index < 0:
            if chores:
                chores.pop(0)()
            return
        stream = streams[index]
        if not stream.done():
            stream.turn()
            if stream.done():
                rows = pl.ds(stream.first, stream.count)
                put(summed.at[rows], g_h.at[rows])

    def mark():
        for index in turns.pop(0) if turns else ():
            advance(index)

    grads[0:ff, :] = dot(act[...], f2[...], 0, 0).astype(BF16)
    mark()
    reduce_middle(2, 1)
    grads[ff : ff + width, :] = dot(f1[...], preg[...], 0, 0).astype(BF16)
    mark()
    first_back(0)
    wk[...] = wkT[...].T
    wv[...] = wvT[...].T
    wq[...] = wqT[...].T
    mark()
    attend_back(0, mark)
    first_back(1)
    mark()
    attend_back(1, mark)
    base = ff + width
    hw = heads * DH
    grads[base : base + hw, :] = dot(ctx[...], f3[...], 0, 0).astype(BF16)
    mark()
    grads[base + hw : base + 2 * hw, :] = dot(dqT[...], plow[...]).astype(BF16)
    mark()
    grads[base + 2 * hw : base + 3 * hw, :] = dot(kgT[...], hid[...]).astype(BF16)
    grads[base + 3 * hw : base + 4 * hw, :] = dot(vgT[...], hid[...]).astype(BF16)
    mark()
    small_sums()
    waiting = [copies.start("small", small.at[pl.ds(0, 8)], smallR.at[0, pl.ds(0, 8)], sib_id)]
    mark()
    input_part(0)
    mark()
    input_part(1)
    mark()

    def small_next(bit):
        waiting.pop().wait()
        if bit == 0:
            small[0:8, :] = small[0:8, :] + smallR[0, 0:8, :]
        else:
            small[...] = small[...] + smallR[bit]
        if bit < bits:
            waiting.append(
                copies.start(("small", bit), small, smallR.at[bit + 1], grid.across[bit])
            )
        else:
            put(small, small_h)

    def input_done(g):
        input_end(g)
        if g == chunks - 1:
            put(igo, ig_h)

    def pooled_done():
        for g in range(chunks):
            shares["po", g].wait()
        put(po, po_h)

    chores += [partial(input_middle, 0), partial(small_next, 0), partial(input_middle, 1)]
    chores += [pooled_done] + [partial(small_next, bit) for bit in range(1, bits + 1)]
    chores += [partial(input_done, g) for g in range(chunks)]
    for index in tail:
        advance(index)
    while chores:
        advance(-1)
    while not all(stream.done() for stream in streams):
        advance([stream.done() for stream in streams].index(False))
    for copy in outs:
        copy.wait()


def finish_kernel(
    plan, po_h, ig_h, g_h, small_h, po_o, ig_o, q_o, k_o, v_o, wo_o, up_o, dn_o, *rest
):
    tab_o, fg_o, fs_o, ub_o, db_o, sg_o, ss_o, po, ig, low, wide, small, tab, *vectors = rest
    *vectors, in_sems, out_sems = vectors
    targets = (dn_o, up_o, wo_o, q_o, k_o, v_o)
    get_small = pltpu.make_async_copy(small_h, small, in_sems.at[len(plan)])
    get_po = pltpu.make_async_copy(po_h, po, in_sems.at[len(plan) + 1])
    get_ig = pltpu.make_async_copy(ig_h, ig, in_sems.at[len(plan) + 2])
    gets = [
        pltpu.make_async_copy(
            g_h.at[pl.ds(row, rows)], low.at[pl.ds(row, rows)], in_sems.at[index]
        )
        for index, (row, rows, unused, unused_row) in enumerate(plan)
    ]
    for get in [get_small] + gets + [get_po, get_ig]:
        get.start()
    puts = []

    def put(source, target):
        copy = pltpu.make_async_copy(source, target, out_sems.at[len(puts)])
        copy.start()
        puts.append(copy)

    get_small.wait()
    for vector, row, out in zip(
        vectors,
        (FIRST_GAIN, FIRST_SHIFT, UP_ROW, DOWN_BIAS, SECOND_GAIN, SECOND_SHIFT),
        (fg_o, fs_o, ub_o, db_o, sg_o, ss_o),
    ):
        vector[...] = small[row, : vector.shape[0]]
        put(vector, out)
    tab[...] = small[TABLE_ROW : TABLE_ROW + tab.shape[0], : 2 * REL]
    put(tab, tab_o)
    for get, (row, rows, index, target_row) in zip(gets, plan):
        get.wait()

        def widen(here):
            where = pl.ds(pl.multiple_of(row + here, 32), 32)
            wide[where, :] = low[where, :].astype(F32)

        tiles(rows, 32, widen)
        put(wide.at[pl.ds(row, rows)], targets[index].at[pl.ds(target_row, rows)])
    get_po.wait()
    put(po, po_o)
    get_ig.wait()
    put(ig, ig_o)
    for copy in puts:
        copy.wait()


def finish(pooled_out, input_grad, grads, small, heads, ff, width):
    hw = heads * DH
    total = grads.shape[0]
    plan, row = [], 0
    for index, rows in enumerate((ff, width, hw, hw, hw, hw)):
        for start in range(0, rows, 384):
            size = min(384, rows - start)
            plan.append((row + start, size, index, start))
        row += rows
    vector = jax.ShapeDtypeStruct((width,), F32)
    any_spec = pl.BlockSpec(memory_space=pl.ANY)
    outs = pl.pallas_call(
        partial(finish_kernel, tuple(plan)),
        name="finish",
        out_shape=(
            jax.ShapeDtypeStruct(pooled_out.shape, BF16),
            jax.ShapeDtypeStruct(input_grad.shape, BF16),
            jax.ShapeDtypeStruct((hw, width), F32),
            jax.ShapeDtypeStruct((hw, width), F32),
            jax.ShapeDtypeStruct((hw, width), F32),
            jax.ShapeDtypeStruct((hw, width), F32),
            jax.ShapeDtypeStruct((width, ff), F32),
            jax.ShapeDtypeStruct((ff, width), F32),
            jax.ShapeDtypeStruct((heads, 2 * REL), F32),
            vector,
            vector,
            jax.ShapeDtypeStruct((ff,), F32),
            vector,
            vector,
            vector,
        ),
        in_specs=[any_spec] * 4,
        out_specs=(any_spec,) * 15,
        scratch_shapes=[
            pltpu.VMEM(pooled_out.shape, BF16),
            pltpu.VMEM(input_grad.shape, BF16),
            pltpu.VMEM((total, width), BF16),
            pltpu.VMEM((total, width), F32),
            pltpu.VMEM((SMALL_ROWS, width), F32),
            pltpu.VMEM((heads, 2 * REL), F32),
            pltpu.VMEM((width,), F32),
            pltpu.VMEM((width,), F32),
            pltpu.VMEM((ff,), F32),
            pltpu.VMEM((width,), F32),
            pltpu.VMEM((width,), F32),
            pltpu.VMEM((width,), F32),
            pltpu.SemaphoreType.DMA((len(plan) + 3,)),
            pltpu.SemaphoreType.DMA((len(plan) + 9,)),
        ],
        compiler_params=pltpu.CompilerParams(vmem_limit_bytes=64_000_000),
    )(pooled_out, input_grad, grads, small)
    po, ig, qg, kg, vg, wo, up, dn, tab, fg, fs, ub, db, sg, ss = outs
    return po, ig.T, qg.T, kg.T, vg.T, wo, tab, fg, fs, up, ub, dn, db, sg, ss


def local(n_dp, *args):
    (
        hidden_in,
        segment_ids,
        query_weight,
        key_weight,
        value_weight,
        output_weight,
        position_table,
        first_gain,
        first_shift,
        up_weight,
        up_bias,
        down_weight,
        down_bias,
        second_gain,
        second_shift,
        cotangent,
    ) = args
    tokens, width = hidden_in.shape
    chunks = tokens // TOK_ROW
    pooled = tokens // 2
    half = HALF_ROW // 2
    heads = position_table.shape[0]
    hw = heads * DH
    ff = up_weight.shape[1]
    share = width // 4
    specs, row = [], 0
    for order, rows in PIECES:
        specs.append((row, rows, order))
        row += rows
    plan = (tuple(specs), TURNS, TAIL)
    bits = n_dp.bit_length() - 1
    links = 5 if n_dp == 8 else bits + 3
    total = ff + width + 4 * hw
    cfg = (n_dp, heads, HALF_ROW, chunks, width, ff, share, plan)
    vmem = lambda *shape: pltpu.VMEM(shape, BF16)
    wide = lambda *shape: pltpu.VMEM(shape, F32)
    slots = 3 * chunks
    inbox_rows = total * 7 // 4 + max(bits - 3, 0) * total // 8
    any_spec = pl.BlockSpec(memory_space=pl.ANY)
    scratch = [
        pltpu.VMEM((tokens,), jnp.int32),
        wide(width),
        wide(width),
        wide(ff),
        wide(width),
        wide(width),
        wide(width),
        wide(heads, 2 * REL),
        vmem(tokens, width),
        vmem(width, hw),
        vmem(width, hw),
        vmem(width, hw),
        vmem(hw, width),
        vmem(width, ff),
        vmem(ff, width),
        vmem(pooled, width),
        vmem(hw, width),
        vmem(hw, width),
        vmem(hw, width),
        vmem(HALF_ROW, TOK_ROW),
        wide(chunks, HALF_ROW, TOK_ROW),
        wide(2, HALF_ROW, LANES),
        wide(heads, 64, BAND),
        wide(heads, 64, BAND),
        vmem(pooled, width),
        wide(pooled // 2, width),
        vmem(pooled, hw),
        vmem(hw, pooled),
        vmem(hw, tokens),
        vmem(hw, tokens),
        wide(HALF_ROW, TOK_ROW),
        wide(chunks * heads, HALF_ROW, TOK_ROW),
        vmem(chunks * heads, HALF_ROW, TOK_ROW),
        vmem(HALF_ROW, TOK_ROW),
        vmem(pooled, hw),
        vmem(slots, HALF_ROW, width),
        vmem(slots, half, width),
        vmem(slots, half, width),
        vmem(slots, half, width),
        vmem(pooled, width),
        vmem(pooled, width),
        vmem(pooled, width),
        wide(pooled // 2, width),
        wide(pooled // 2, width),
        wide(pooled // 2, 1),
        wide(HALF_ROW, ff),
        vmem(pooled, ff),
        wide(pooled, ff),
        vmem(pooled, ff),
        wide(pooled // 2, width),
        vmem(pooled, width),
        vmem(pooled, hw),
        vmem(hw, pooled),
        vmem(hw, pooled),
        vmem(hw, tokens),
        vmem(hw, tokens),
        vmem(width, TOK_ROW),
        vmem(chunks, 4, share, TOK_ROW),
        vmem(chunks, 2, share, TOK_ROW),
        vmem(chunks, share, TOK_ROW),
        vmem(chunks, share, TOK_ROW),
        vmem(share, tokens),
        vmem(total, width),
        vmem(total, width),
        vmem(inbox_rows, width),
        wide(6, 8, width),
        wide(SMALL_ROWS, width),
        wide(bits + 1, SMALL_ROWS, width),
        pltpu.SemaphoreType.DMA((16,)),
        pltpu.SemaphoreType.DMA((len(specs) + 3,)),
        pltpu.SemaphoreType.DMA((SENDS,)),
        pltpu.SemaphoreType.DMA((links * len(specs) + RECEIVES,)),
    ]
    pooled_out, input_grad, grads, small = pl.pallas_call(
        partial(fused, cfg),
        name="layer",
        out_shape=(
            jax.ShapeDtypeStruct((pooled, width), BF16),
            jax.ShapeDtypeStruct((share, tokens), BF16),
            jax.ShapeDtypeStruct((total, width), BF16),
            jax.ShapeDtypeStruct((SMALL_ROWS, width), F32),
        ),
        in_specs=[any_spec] * 16,
        out_specs=(any_spec,) * 4,
        scratch_shapes=scratch,
        compiler_params=pltpu.CompilerParams(
            collective_id=0, has_side_effects=True, vmem_limit_bytes=64_000_000
        ),
    )(
        segment_ids,
        first_gain,
        first_shift,
        up_bias,
        down_bias,
        second_gain,
        second_shift,
        position_table,
        hidden_in,
        query_weight.T,
        key_weight.T,
        value_weight.T,
        output_weight,
        up_weight,
        down_weight,
        cotangent,
    )
    return finish(pooled_out, input_grad, grads, small, heads, ff, width)


def solution(mesh):
    return jax.shard_map(
        partial(local, mesh.shape["dp"]),
        mesh=mesh,
        in_specs=(
            P("dp", None),
            P("dp"),
            P(None, "tensor"),
            P(None, "tensor"),
            P(None, "tensor"),
            P("tensor", None),
            P("tensor", None),
            P(),
            P(),
            P(None, "tensor"),
            P("tensor"),
            P("tensor", None),
            P(),
            P(),
            P(),
            P("dp", None),
        ),
        out_specs=(
            P("dp", None),
            P("dp", "tensor"),
            P(None, "tensor"),
            P(None, "tensor"),
            P(None, "tensor"),
            P("tensor", None),
            P("tensor", None),
            P(),
            P(),
            P(None, "tensor"),
            P("tensor"),
            P("tensor", None),
            P(),
            P(),
            P(),
        ),
        check_vma=False,
    )
```

```python
import math
from functools import partial

import jax
import jax.numpy as jnp
from jax import lax
from jax.experimental import pallas as pl
from jax.experimental.pallas import tpu as pltpu
from jax.sharding import PartitionSpec as P

DH = 64
TOK_ROW = 512
LANES = 128
HALF_ROW = TOK_ROW // 2
REL = 64
EPSILON = 1e-06
NEGATIVE = -1e30
MESH = pl.DeviceIdType.MESH
F32 = jnp.float32
BF16 = jnp.bfloat16

FIRST_GAIN, FIRST_SHIFT, DOWN_BIAS, SECOND_GAIN, SECOND_SHIFT, UP_BIAS = range(6)
UP_ROW, TABLE_ROW, SMALL_ROWS = 8, 9, 16
BAND = 1024
ROLL = 1152
SENDS = 28
RECEIVES = 24
PIECES = (('Y', 192), ('Z', 128), ('Z', 64), ('Y', 128), ('Y', 128), ('Z', 64), ('Y', 64), ('Z', 64), ('Y', 128), ('Y', 192), ('Z', 128), ('Y', 128), ('Y', 128), ('Z', 128), ('Y', 64), ('Y', 192), ('Y', 128), ('Y', 128), ('Y', 128))
TURNS = [[2, 3, 1, 4], [12], [], [2, 3, 9], [4], [2, 10, 0], [1, 12], [3, 6], [9, 2, 1, 4], [3, 11], [], [], [0, 15, 4], [6, 10, 3, 2], [1], [4, 12, 11, 17]]
TAIL = [10, 3, 9, 2, -1, 12, 15, 4, 1, -1, 0, 9, 2, 6, -1, 12, 17, 10, 11, -1, 1, 3, 0, 12, -1, 7, 18, 15, 9, -1, 13, 4, 6, 10, -1, 11, 17, 8, 1, -1, 0, 14, 12, 7, -1, 15, 6, 5, 16, -1, 18, 9, 10, 8, -1, 13, 11, 14, 0, -1, 17, 6, 5, 7, -1, 16, 15, 18, 9, -1, 13, 10, 8, 17, -1, 14, 5, 11, 0, -1, 18, 16, 6, 8, -1, 7, 14, 13, 15, -1, 18, 5, 16, 17, -1, 8, 11, 14, 7, -1, 16, 13, 18, 7, -1, 8, 15, 14, 13, -1, 5, 16, 17, 5, -1, 7, 18, 8, 14, -1, 13, 16, 5]
U_SOFT, U_SBACK, U_NORM, U_GELU = 8, 2, 8, 4


def dot(left, right, left_dim=1, right_dim=0):
    return lax.dot_general(
        left, right, (((left_dim,), (right_dim,)), ((), ())), preferred_element_type=F32
    )


def tiles(count, step, body, unroll=1):
    unroll = math.gcd(unroll, count // step)
    stride = step * unroll

    def one(index, unused):
        for part in range(unroll):
            body(pl.multiple_of(index * stride + part * step, step))
        return unused

    if count == stride:
        for row in range(0, count, step):
            body(row)
    else:
        lax.fori_loop(0, count // stride, one, 0)


def across_row(column):
    return jnp.concatenate([column] * (TOK_ROW // LANES), axis=1)


def fold(value):
    total = value[0:8]
    for start in range(8, value.shape[0], 8):
        total = total + value[start : start + 8]
    return total


class Copy:
    def __init__(self, copy, send, recv, free):
        self.copy, self.send, self.recv, self.free = copy, send, recv, free

    def start(self):
        if self.send is None:
            self.copy.start()
        else:
            pl.when(self.send)(self.copy.start)

    def wait(self):
        if self.send is None:
            self.copy.wait()
        else:
            pl.when(self.send)(self.copy.wait_send)
            pl.when(self.recv)(self.copy.wait_recv)
        self.free()


class Copies:
    def __init__(self, send_sems, recv_sems):
        self.send_sems, self.recv_sems = send_sems, recv_sems
        self.idle, self.keys = list(range(SENDS)), {}

    def start(self, key, source, target, device, send=None, recv=None):
        index = self.idle.pop(0)
        copy = Copy(
            pltpu.make_async_remote_copy(
                src_ref=source,
                dst_ref=target,
                send_sem=self.send_sems.at[index],
                recv_sem=self.recv_sems.at[self.keys.setdefault(key, len(self.keys))],
                device_id=device,
                device_id_type=MESH,
            ),
            send,
            recv,
            lambda: self.idle.append(index),
        )
        copy.start()
        return copy


class Grid:
    def __init__(self, n_dp, d, t):
        self.bits = n_dp.bit_length() - 1
        self.mine = [lax.rem(d // (1 << bit), 2) for bit in range(self.bits)]
        self.across = [(d + (1 - 2 * self.mine[b]) * (1 << b), t) for b in range(self.bits)]
        self.peers = list(self.across)
        self.plans = {}
        if n_dp == 8:
            z = d // 2
            middle = jnp.logical_or(z == 1, z == 2)
            end = jnp.logical_not(middle)
            upper = z // 2
            facing = (d + (3 - 2 * z) * 2, t)
            self.peers.append(facing)
            everyone = (None, None, None, "y")
            inner = (middle, middle, middle)
            y = ("half", self.across[0], self.mine[0])
            y_back = ("back", self.across[0], self.mine[0])
            gather = ("whole", self.across[1], 0, end, middle, middle, "z")
            spread = ("same", self.across[1], 0, middle, end, middle, "z")
            mid = ("half", facing, upper) + inner + ("mid",)
            mid_back = ("back", facing, upper) + inner + ("mid_back",)
            y_inner = inner + ("y",)
            y_out = ("y_back",)
            self.plans["Y"] = (
                y + everyone,
                gather,
                mid,
                mid_back,
                spread,
                y_back + everyone[:3] + y_out,
            )
            self.plans["Z"] = (gather, mid, y + y_inner, y_back + inner + y_out, mid_back, spread)
        else:
            everyone = (None, None, None)
            halving = list(range(min(3, self.bits)))
            plan = [("half", self.across[b], self.mine[b]) + everyone + (b,) for b in halving]
            plan += [
                ("whole", self.across[b], 0) + everyone + (b,)
                for b in range(len(halving), self.bits)
            ]
            plan += [
                ("back", self.across[b], self.mine[b]) + everyone + (self.bits + b,)
                for b in reversed(halving)
            ]
            self.plans["Y"] = self.plans["Z"] = tuple(plan)

    def inbox_rows(self, order, rows):
        total = 0
        for kind, *unused in self.plans[order]:
            if kind == "half":
                rows //= 2
            if kind in ("half", "whole"):
                total += rows
        return total


class Stream:
    def __init__(self, copies, buffers, inbox_row, row, rows, plan):
        self.copies, self.plan = copies, plan
        self.grads, self.summed, self.inbox = buffers
        self.inbox_row, self.rows, self.pos = inbox_row, rows, row
        self.first, self.count = row, rows
        self.step, self.pending = 0, None

    def begin(self):
        kind, device, mine, send, recv, unused, link = self.plan[self.step]
        size = self.rows
        at = self.pos
        if kind == "half":
            size //= 2
            self.keep = pl.multiple_of(self.pos + mine * size, 16)
            at = pl.multiple_of(self.pos + (1 - mine) * size, 16)
        if kind in ("half", "whole"):
            source = self.grads.at[pl.ds(at, size)]
            target = self.inbox.at[pl.ds(self.inbox_row, size)]
        else:
            source = target = self.summed.at[pl.ds(at, size)]
        self.pending = self.copies.start((self.first, link), source, target, device, send, recv)
        self.size = size

    def finish(self):
        kind, device, mine, send, recv, adds, link = self.plan[self.step]
        self.pending.wait()
        self.step += 1
        if kind == "back":
            self.pos = pl.multiple_of(self.pos - mine * self.size, 16)
            self.rows = 2 * self.size
        elif kind != "same":
            if kind == "half":
                self.pos, self.rows = self.keep, self.size
            base, inbox_row, grads, inbox = self.pos, self.inbox_row, self.grads, self.inbox
            result = self.summed if self.plan[self.step][0] == "back" else grads
            step = 32 if self.size % 32 == 0 else 16

            def add(row):
                rows = pl.ds(pl.multiple_of(base + row, 16), step)
                arrived = inbox[pl.ds(pl.multiple_of(inbox_row + row, 16), step), :]
                result[rows, :] = (grads[rows, :].astype(F32) + arrived.astype(F32)).astype(BF16)

            def add_all():
                tiles(self.size, step, add, 2)

            if adds is None:
                add_all()
            else:
                pl.when(adds)(add_all)
            self.inbox_row += self.size

    def done(self):
        return self.step == len(self.plan)

    def turn(self):
        if self.pending is not None:
            self.finish()
            self.pending = None
        if not self.done():
            self.begin()


def fused(
    cfg,
    seg_h,
    first_gain_h,
    first_shift_h,
    up_bias_h,
    down_bias_h,
    second_gain_h,
    second_shift_h,
    tab_h,
    hid_h,
    wq_h,
    wk_h,
    wv_h,
    wo_h,
    up_h,
    dn_h,
    cot_h,
    po_h,
    ig_h,
    g_h,
    small_h,
    seg_ref,
    first_gain,
    first_shift,
    up_bias_in,
    down_bias_in,
    second_gain,
    second_shift,
    tab_ref,
    hid,
    wq,
    wk,
    wv,
    wo,
    up,
    dn,
    cot,
    wqT,
    wkT,
    wvT,
    dup,
    mask,
    stat,
    bias,
    tacc,
    plow,
    pown,
    q,
    qT,
    kT,
    vT,
    score,
    probs,
    problow,
    ds,
    ctx,
    arA,
    arR1,
    arB,
    arR2,
    f1,
    f2,
    f3,
    first_out,
    normed1,
    inv1,
    pre,
    act,
    gp,
    preg,
    sgrad,
    po,
    cg,
    cgT,
    dqT,
    kgT,
    vgT,
    f3dT,
    tp,
    inR1,
    inB,
    inR2,
    igo,
    grads,
    summed,
    inbox,
    acc,
    small,
    smallR,
    in_sems,
    out_sems,
    send_sems,
    recv_sems,
):
    n_dp, heads, rows_per, chunks, width, ff, share, stream_plan = cfg
    half = HALF_ROW // 2
    d = lax.axis_index("dp")
    t = lax.axis_index("tensor")
    core = lax.rem(t, 2)
    side = t // 2
    sib_id = (d, t + 1 - 2 * core)
    cross_id = (d, t + 2 - 4 * side)
    grid = Grid(n_dp, d, t)
    bits = grid.bits
    own = pl.multiple_of(core * half, half)
    away = pl.multiple_of((1 - core) * half, half)

    loads = [
        pltpu.make_async_copy(source, target, in_sems.at[index])
        for index, (source, target) in enumerate(
            [
                (hid_h, hid),
                (wk_h, wkT),
                (wv_h, wvT),
                (wq_h, wqT),
                (wo_h, wo),
                (up_h, up),
                (dn_h, dn),
                (cot_h, cot),
                (seg_h, seg_ref),
                (tab_h, tab_ref),
                (first_gain_h, first_gain),
                (first_shift_h, first_shift),
                (up_bias_h, up_bias_in),
                (down_bias_h, down_bias_in),
                (second_gain_h, second_gain),
                (second_shift_h, second_shift),
            ]
        )
    ]
    early, vectors, late = loads[:5], loads[8:], loads[5:8]
    for load in vectors[:2] + early:
        load.start()
    barrier = pltpu.get_barrier_semaphore()
    for device in [sib_id, cross_id] + grid.peers:
        pl.semaphore_signal(barrier, inc=1, device_id=device, device_id_type=MESH)

    row_i = lax.broadcasted_iota(jnp.int32, (HALF_ROW, TOK_ROW), 0)
    col_i = lax.broadcasted_iota(jnp.int32, (HALF_ROW, TOK_ROW), 1)
    dup[...] = jnp.where(col_i // 2 == row_i, 1.0, 0.0).astype(BF16)
    evens = jnp.where(col_i == 2 * row_i, 1.0, 0.0).astype(BF16)
    vectors[0].wait()
    segk = [
        seg_ref[g * TOK_ROW : (g + 1) * TOK_ROW].astype(F32).reshape(1, TOK_ROW)
        for g in range(chunks)
    ]
    for g in range(chunks):
        rows = jnp.broadcast_to(segk[g], (LANES, TOK_ROW)).astype(BF16)
        column = across_row(dot(evens, rows, 1, 1))
        mask[g] = jnp.where(column == segk[g], 0.0, NEGATIVE)
    vectors[1].wait()
    for h in range(heads):
        table = jnp.concatenate(
            [
                jnp.broadcast_to(tab_ref[h : h + 1, 0:1], (REL, 512)),
                jnp.broadcast_to(tab_ref[h : h + 1, :], (REL, 2 * REL)),
                jnp.broadcast_to(tab_ref[h : h + 1, 2 * REL - 1 : 2 * REL], (REL, 512)),
            ],
            axis=1,
        )
        bias[h] = pltpu.roll(table, ROLL - 64, 1, stride=2, stride_axis=0)[:, :BAND]
    tacc[...] = jnp.zeros_like(tacc)
    acc[...] = jnp.zeros_like(acc)
    small[...] = jnp.zeros_like(small)

    copies = Copies(send_sems, recv_sems)

    reduce_one, reduce_two = {}, {}

    def reduce_start(which, g):
        slot = which * chunks + g
        reduce_one[slot] = copies.start(("one", g), arA.at[slot, pl.ds(away, half)], arR1.at[slot], sib_id)

    def reduce_middle(which, g):
        slot = which * chunks + g
        reduce_one[slot].wait()

        def add(row):
            mine = arA[slot, pl.ds(pl.multiple_of(own + row, 32), 32), :].astype(F32)
            arB[slot, pl.ds(row, 32), :] = (
                mine + arR1[slot, pl.ds(row, 32), :].astype(F32)
            ).astype(BF16)

        tiles(half, 32, add, 2)
        reduce_two[slot] = copies.start(("two", g, which % 2), arB.at[slot], arR2.at[slot], cross_id)

    def reduced(which, g, row):
        slot = which * chunks + g
        return arB[slot, pl.ds(row, 16), :].astype(F32) + arR2[slot, pl.ds(row, 16), :].astype(F32)

    shares = {}

    def share_start(name, buffer, g):
        rows = buffer.at[pl.ds(pl.multiple_of(g * HALF_ROW + own, half), half)]
        key = ("po" if name == "po" else "share", g)
        shares[name, g] = copies.start(key, rows, rows, sib_id)

    def qkv(g):
        tokens = hid[g * TOK_ROW : (g + 1) * TOK_ROW, :]
        pooled = slice(g * HALF_ROW, (g + 1) * HALF_ROW)
        cols = slice(g * TOK_ROW, (g + 1) * TOK_ROW)
        plow[pooled, :] = (dot(dup[...], tokens) * 0.5).astype(BF16)
        mine = hid[pl.ds(pl.multiple_of(g * TOK_ROW + core * HALF_ROW, HALF_ROW), HALF_ROW), :]
        pown[g * half : (g + 1) * half, :] = dot(dup[0:half, 0:HALF_ROW], mine) * 0.5
        kT[:, cols] = dot(wkT[...], tokens, 1, 1).astype(BF16)
        vT[:, cols] = dot(wvT[...], tokens, 1, 1).astype(BF16)
        scale = 1.0 / math.sqrt(DH)
        q[pooled, :] = (dot(plow[pooled, :], wqT[...], 1, 1) * scale).astype(BF16)
        qT[:, pooled] = (dot(wqT[...], plow[pooled, :], 1, 1) * scale).astype(BF16)

    def attend(g):
        pooled = slice(g * HALF_ROW, (g + 1) * HALF_ROW)
        cols = slice(g * TOK_ROW, (g + 1) * TOK_ROW)
        for h in range(heads):
            lanes = slice(h * DH, (h + 1) * DH)
            slot = g * heads + h
            score[...] = dot(q[pooled, lanes], kT[lanes, cols])

            def add_bias(row):
                here = pl.ds(row, 32)
                band, part = 512 - 128 * (row // 64), row % 64
                if not isinstance(row, int):
                    part = pl.multiple_of(lax.rem(row, 64), 32)
                    band = pl.multiple_of(band, 128)
                raw = score[here, :] + bias[h, pl.ds(part, 32), pl.ds(band, TOK_ROW)]
                raw = raw + mask[g, here, :]
                score[here, :] = raw
                peak = jnp.max(raw, axis=-1, keepdims=True)
                stat[0, here, :] = jnp.broadcast_to(peak, (32, LANES))

            def weigh(row):
                here = pl.ds(row, 32)
                weights = jnp.exp(score[here, :] - across_row(stat[0, here, :]))
                score[here, :] = weights
                total = jnp.sum(weights, axis=-1, keepdims=True)
                stat[1, here, :] = jnp.broadcast_to(total, (32, LANES))

            def divide(row):
                here = pl.ds(row, 32)
                prob = score[here, :] * across_row(1.0 / stat[1, here, :])
                probs[slot, here, :] = prob
                problow[slot, here, :] = prob.astype(BF16)

            for step in (add_bias, weigh, divide):
                tiles(HALF_ROW, 32, step, U_SOFT)
            ctx[pooled, lanes] = dot(problow[slot], vT[lanes, cols], 1, 1).astype(BF16)
        arA[g] = dot(ctx[pooled, :], wo[...]).astype(BF16)

    def first_norm(g):
        reduce_two[g].wait()
        gain, shift = first_gain[...].reshape(1, width), first_shift[...].reshape(1, width)

        def one(row):
            here = pl.ds(pl.multiple_of(g * half + row, 16), 16)
            value = pown[here, :] + reduced(0, g, row)
            centred = value - jnp.mean(value, axis=-1, keepdims=True)
            inverse = lax.rsqrt(jnp.mean(centred * centred, axis=-1, keepdims=True) + EPSILON)
            normed = centred * inverse
            out = normed * gain + shift
            normed1[here, :] = normed
            inv1[here, :] = inverse
            first_out[here, :] = out
            f1[pl.ds(pl.multiple_of(g * HALF_ROW + own + row, 16), 16), :] = out.astype(BF16)

        tiles(half, 16, one, U_NORM)
        share_start("f1", f1, g)

    def feed_forward(g):
        shares["f1", g].wait()
        pooled = slice(g * HALF_ROW, (g + 1) * HALF_ROW)
        pre[...] = dot(f1[pooled, :], up[...])
        up_bias = up_bias_in[...].reshape(1, ff)

        def one(row):
            value = pre[pl.ds(row, 16), :] + up_bias
            cdf = 0.5 * (1.0 + lax.erf(value * (1.0 / math.sqrt(2.0))))
            density = jnp.exp(-0.5 * value * value) * (1.0 / math.sqrt(2.0 * math.pi))
            here = pl.ds(pl.multiple_of(g * HALF_ROW + row, 16), 16)
            act[here, :] = (value * cdf).astype(BF16)
            gp[here, :] = cdf + value * density

        tiles(HALF_ROW, 16, one, U_GELU)
        arA[chunks + g] = dot(act[pooled, :], dn[...]).astype(BF16)

    def second_norm(g):
        reduce_two[chunks + g].wait()
        gain, shift = second_gain[...].reshape(1, width), second_shift[...].reshape(1, width)
        down_bias = down_bias_in[...].reshape(1, width)

        def one(row):
            here = pl.ds(pl.multiple_of(g * half + row, 16), 16)
            full = pl.ds(pl.multiple_of(g * HALF_ROW + own + row, 16), 16)
            value = first_out[here, :] + reduced(1, g, row) + down_bias
            centred = value - jnp.mean(value, axis=-1, keepdims=True)
            inverse = lax.rsqrt(jnp.mean(centred * centred, axis=-1, keepdims=True) + EPSILON)
            normed = centred * inverse
            po[full, :] = (normed * gain + shift).astype(BF16)
            upstream = cot[full, :].astype(F32)
            scaled = upstream * gain
            grad = inverse * (
                scaled
                - jnp.mean(scaled, axis=-1, keepdims=True)
                - normed * jnp.mean(scaled * normed, axis=-1, keepdims=True)
            )
            sgrad[here, :] = grad
            f2[full, :] = grad.astype(BF16)
            acc[SECOND_GAIN] += fold(upstream * normed)
            acc[SECOND_SHIFT] += fold(upstream)
            acc[DOWN_BIAS] += fold(grad)

        tiles(half, 16, one, U_NORM)
        share_start("f2", f2, g)
        share_start("po", po, g)

    def feed_back(g):
        shares["f2", g].wait()
        pooled = slice(g * HALF_ROW, (g + 1) * HALF_ROW)
        pre[...] = dot(f2[pooled, :], dn[...], 1, 1)

        def one(row):
            here = pl.ds(pl.multiple_of(g * HALF_ROW + row, 16), 16)
            low = (gp[here, :] * pre[pl.ds(row, 16), :]).astype(BF16)
            preg[here, :] = low
            acc[UP_BIAS, :, :ff] += fold(low.astype(F32))

        tiles(HALF_ROW, 16, one, U_GELU)
        arA[2 * chunks + g] = dot(preg[pooled, :], up[...], 1, 1).astype(BF16)

    def first_back(g):
        reduce_two[2 * chunks + g].wait()
        gain = first_gain[...].reshape(1, width)

        def one(row):
            here = pl.ds(pl.multiple_of(g * half + row, 16), 16)
            full = pl.ds(pl.multiple_of(g * HALF_ROW + own + row, 16), 16)
            upstream = reduced(2, g, row) + sgrad[here, :]
            normed = normed1[here, :]
            scaled = upstream * gain
            grad = inv1[here, :] * (
                scaled
                - jnp.mean(scaled, axis=-1, keepdims=True)
                - normed * jnp.mean(scaled * normed, axis=-1, keepdims=True)
            )
            f3[full, :] = grad.astype(BF16)
            acc[FIRST_GAIN] += fold(upstream * normed)
            acc[FIRST_SHIFT] += fold(upstream)

        tiles(half, 16, one, U_NORM)
        share_start("f3", f3, g)

    def attend_back(g, after):
        shares["f3", g].wait()
        pooled = slice(g * HALF_ROW, (g + 1) * HALF_ROW)
        cols = slice(g * TOK_ROW, (g + 1) * TOK_ROW)
        cg[pooled, :] = dot(f3[pooled, :], wo[...], 1, 1).astype(BF16)
        cgT[:, pooled] = dot(wo[...], f3[pooled, :], 1, 1).astype(BF16)
        for h in range(heads):
            lanes = slice(h * DH, (h + 1) * DH)
            slot = g * heads + h
            score[...] = dot(cg[pooled, lanes], vT[lanes, cols])

            def one(row):
                block = row // 64
                part = pl.multiple_of(lax.rem(row, 64), 32)
                band = pl.ds(pl.multiple_of(512 - 128 * block, 128), TOK_ROW)
                prob = probs[slot, pl.ds(row, 32), :]
                prob_grad = score[pl.ds(row, 32), :]
                inner = jnp.sum(prob * prob_grad, axis=-1, keepdims=True)
                grad = prob * (prob_grad - inner)
                ds[pl.ds(row, 32), :] = grad.astype(BF16)
                tacc[h, pl.ds(part, 32), band] += grad

            tiles(HALF_ROW, 32, one, U_SBACK)
            scale = 1.0 / math.sqrt(DH)
            dqT[lanes, pooled] = (dot(kT[lanes, cols], ds[...], 1, 1) * scale).astype(BF16)
            kgT[lanes, cols] = dot(qT[lanes, pooled], ds[...]).astype(BF16)
            vgT[lanes, cols] = dot(cgT[lanes, pooled], problow[slot]).astype(BF16)
            after()

    in_one, in_two = {}, {}

    def input_part(g):
        pooled = slice(g * HALF_ROW, (g + 1) * HALF_ROW)
        cols = slice(g * TOK_ROW, (g + 1) * TOK_ROW)
        doubled = (dot(dqT[:, pooled], dup[...]) * 0.5).astype(BF16)
        f3dT[...] = (dot(f3[pooled, :], dup[...], 0, 0) * 0.125).astype(BF16)
        for b in range(4):
            rows = slice(b * share, (b + 1) * share)
            total = dot(wk[rows, :], kgT[:, cols]) + dot(wv[rows, :], vgT[:, cols])
            total = total + dot(wq[rows, :], doubled) + f3dT[rows, :].astype(F32)
            tp[g, b] = total.astype(BF16)
        for index, block in enumerate((1 - core + 2 * (1 - side), 1 - core + 2 * side)):
            in_one[g, index] = copies.start(("in", g, index), tp.at[g, block], inR1.at[g, index], sib_id)

    def input_middle(g):
        far = core + 2 * (1 - side)
        in_one[g, 0].wait()

        def add(row):
            here = pl.ds(row, 32)
            inB[g, here, :] = (
                tp[g, far, here, :].astype(F32) + inR1[g, 0, here, :].astype(F32)
            ).astype(BF16)

        tiles(share, 32, add, 2)
        in_two[g] = copies.start(("in two", g), inB.at[g], inR2.at[g], cross_id)

    def input_end(g):
        in_one[g, 1].wait()
        in_two[g].wait()

        def add(row):
            here = pl.ds(row, 32)
            igo[here, g * TOK_ROW : (g + 1) * TOK_ROW] = (
                tp[g, t, here, :].astype(F32)
                + inR1[g, 1, here, :].astype(F32)
                + inR2[g, here, :].astype(F32)
            ).astype(BF16)

        tiles(share, 32, add, 2)

    def small_sums():
        for index in range(5):
            small[index : index + 1, :] = jnp.sum(acc[index], axis=0, keepdims=True)
        small[UP_ROW : UP_ROW + 1, :] = jnp.sum(acc[UP_BIAS], axis=0, keepdims=True)
        lane = lax.broadcasted_iota(jnp.int32, (1, BAND), 1)
        lane_out = lax.broadcasted_iota(jnp.int32, (1, 2 * REL), 1)
        sub = lax.broadcasted_iota(jnp.int32, (8, BAND), 0)
        for h in range(heads):
            part = tacc[h]
            for size in (32, 16, 8):
                part = part[0:size] + pltpu.roll(part[size : 2 * size], BAND - 2 * size, 1)
            for size in (4, 2, 1):
                part = jnp.where(
                    lax.rem(sub // size, 2) == 1, pltpu.roll(part, BAND - 2 * size, 1), part
                )
            part = jnp.sum(part, axis=0, keepdims=True)
            low = jnp.sum(jnp.where(lane <= 448, part, 0.0), axis=1, keepdims=True)
            high = jnp.sum(jnp.where(lane >= 575, part, 0.0), axis=1, keepdims=True)
            middle = pltpu.roll(part, BAND - 448, 1)[:, 0 : 2 * REL]
            middle = jnp.where(
                lane_out == 0, low, jnp.where(lane_out == 2 * REL - 1, high, middle)
            )
            small[TABLE_ROW + h : TABLE_ROW + h + 1, 0 : 2 * REL] = middle

    for load in early[:4]:
        load.wait()
    for load in vectors[2:] + late:
        load.start()
    qkv(0)
    early[4].wait()
    attend(0)
    pl.semaphore_wait(barrier, 2 + len(grid.peers))
    reduce_start(0, 0)
    qkv(1)
    reduce_middle(0, 0)
    attend(1)
    reduce_start(0, 1)
    for load in vectors[2:]:
        load.wait()
    first_norm(0)
    reduce_middle(0, 1)
    for load in late:
        load.wait()
    feed_forward(0)
    reduce_start(1, 0)
    first_norm(1)
    reduce_middle(1, 0)
    feed_forward(1)
    reduce_start(1, 1)
    second_norm(0)
    reduce_middle(1, 1)
    feed_back(0)
    reduce_start(2, 0)
    second_norm(1)
    reduce_middle(2, 0)
    feed_back(1)
    reduce_start(2, 1)

    outs = []

    def put(source, target):
        copy = pltpu.make_async_copy(source, target, out_sems.at[len(outs)])
        copy.start()
        outs.append(copy)

    specs, turns, tail = stream_plan
    streams, inbox_row = [], 0
    for row, rows, order in specs:
        streams.append(
            Stream(copies, (grads, summed, inbox), inbox_row, row, rows, grid.plans[order])
        )
        inbox_row += grid.inbox_rows(order, rows)
    turns, chores = list(turns), []

    def advance(index):
        if index < 0:
            if chores:
                chores.pop(0)()
            return
        stream = streams[index]
        if not stream.done():
            stream.turn()
            if stream.done():
                rows = pl.ds(stream.first, stream.count)
                put(summed.at[rows], g_h.at[rows])

    def mark():
        for index in turns.pop(0) if turns else ():
            advance(index)

    grads[0:ff, :] = dot(act[...], f2[...], 0, 0).astype(BF16)
    mark()
    reduce_middle(2, 1)
    grads[ff : ff + width, :] = dot(f1[...], preg[...], 0, 0).astype(BF16)
    mark()
    first_back(0)
    wk[...] = wkT[...].T
    wv[...] = wvT[...].T
    wq[...] = wqT[...].T
    mark()
    attend_back(0, mark)
    first_back(1)
    mark()
    attend_back(1, mark)
    base = ff + width
    hw = heads * DH
    grads[base : base + hw, :] = dot(ctx[...], f3[...], 0, 0).astype(BF16)
    mark()
    grads[base + hw : base + 2 * hw, :] = dot(dqT[...], plow[...]).astype(BF16)
    mark()
    grads[base + 2 * hw : base + 3 * hw, :] = dot(kgT[...], hid[...]).astype(BF16)
    grads[base + 3 * hw : base + 4 * hw, :] = dot(vgT[...], hid[...]).astype(BF16)
    mark()
    small_sums()
    waiting = [copies.start("small", small.at[pl.ds(0, 8)], smallR.at[0, pl.ds(0, 8)], sib_id)]
    mark()
    input_part(0)
    mark()
    input_part(1)
    mark()

    def small_next(bit):
        waiting.pop().wait()
        if bit == 0:
            small[0:8, :] = small[0:8, :] + smallR[0, 0:8, :]
        else:
            small[...] = small[...] + smallR[bit]
        if bit < bits:
            waiting.append(
                copies.start(("small", bit), small, smallR.at[bit + 1], grid.across[bit])
            )
        else:
            put(small, small_h)

    def input_done(g):
        input_end(g)
        if g == chunks - 1:
            put(igo, ig_h)

    def pooled_done():
        for g in range(chunks):
            shares["po", g].wait()
        put(po, po_h)

    chores += [partial(input_middle, 0), partial(small_next, 0), partial(input_middle, 1)]
    chores += [pooled_done] + [partial(small_next, bit) for bit in range(1, bits + 1)]
    chores += [partial(input_done, g) for g in range(chunks)]
    for index in tail:
        advance(index)
    while chores:
        advance(-1)
    while not all(stream.done() for stream in streams):
        advance([stream.done() for stream in streams].index(False))
    for copy in outs:
        copy.wait()


def finish_kernel(
    plan, po_h, ig_h, g_h, small_h, po_o, ig_o, q_o, k_o, v_o, wo_o, up_o, dn_o, *rest
):
    tab_o, fg_o, fs_o, ub_o, db_o, sg_o, ss_o, po, ig, low, wide, small, tab, *vectors = rest
    *vectors, in_sems, out_sems = vectors
    targets = (dn_o, up_o, wo_o, q_o, k_o, v_o)
    get_small = pltpu.make_async_copy(small_h, small, in_sems.at[len(plan)])
    get_po = pltpu.make_async_copy(po_h, po, in_sems.at[len(plan) + 1])
    get_ig = pltpu.make_async_copy(ig_h, ig, in_sems.at[len(plan) + 2])
    gets = [
        pltpu.make_async_copy(
            g_h.at[pl.ds(row, rows)], low.at[pl.ds(row, rows)], in_sems.at[index]
        )
        for index, (row, rows, unused, unused_row) in enumerate(plan)
    ]
    for get in [get_small] + gets + [get_po, get_ig]:
        get.start()
    puts = []

    def put(source, target):
        copy = pltpu.make_async_copy(source, target, out_sems.at[len(puts)])
        copy.start()
        puts.append(copy)

    get_small.wait()
    for vector, row, out in zip(
        vectors,
        (FIRST_GAIN, FIRST_SHIFT, UP_ROW, DOWN_BIAS, SECOND_GAIN, SECOND_SHIFT),
        (fg_o, fs_o, ub_o, db_o, sg_o, ss_o),
    ):
        vector[...] = small[row, : vector.shape[0]]
        put(vector, out)
    tab[...] = small[TABLE_ROW : TABLE_ROW + tab.shape[0], : 2 * REL]
    put(tab, tab_o)
    for get, (row, rows, index, target_row) in zip(gets, plan):
        get.wait()

        def widen(here):
            where = pl.ds(pl.multiple_of(row + here, 32), 32)
            wide[where, :] = low[where, :].astype(F32)

        tiles(rows, 32, widen)
        put(wide.at[pl.ds(row, rows)], targets[index].at[pl.ds(target_row, rows)])
    get_po.wait()
    put(po, po_o)
    get_ig.wait()
    put(ig, ig_o)
    for copy in puts:
        copy.wait()


def finish(pooled_out, input_grad, grads, small, heads, ff, width):
    hw = heads * DH
    total = grads.shape[0]
    plan, row = [], 0
    for index, rows in enumerate((ff, width, hw, hw, hw, hw)):
        for start in range(0, rows, 384):
            size = min(384, rows - start)
            plan.append((row + start, size, index, start))
        row += rows
    vector = jax.ShapeDtypeStruct((width,), F32)
    any_spec = pl.BlockSpec(memory_space=pl.ANY)
    outs = pl.pallas_call(
        partial(finish_kernel, tuple(plan)),
        name="finish",
        out_shape=(
            jax.ShapeDtypeStruct(pooled_out.shape, BF16),
            jax.ShapeDtypeStruct(input_grad.shape, BF16),
            jax.ShapeDtypeStruct((hw, width), F32),
            jax.ShapeDtypeStruct((hw, width), F32),
            jax.ShapeDtypeStruct((hw, width), F32),
            jax.ShapeDtypeStruct((hw, width), F32),
            jax.ShapeDtypeStruct((width, ff), F32),
            jax.ShapeDtypeStruct((ff, width), F32),
            jax.ShapeDtypeStruct((heads, 2 * REL), F32),
            vector,
            vector,
            jax.ShapeDtypeStruct((ff,), F32),
            vector,
            vector,
            vector,
        ),
        in_specs=[any_spec] * 4,
        out_specs=(any_spec,) * 15,
        scratch_shapes=[
            pltpu.VMEM(pooled_out.shape, BF16),
            pltpu.VMEM(input_grad.shape, BF16),
            pltpu.VMEM((total, width), BF16),
            pltpu.VMEM((total, width), F32),
            pltpu.VMEM((SMALL_ROWS, width), F32),
            pltpu.VMEM((heads, 2 * REL), F32),
            pltpu.VMEM((width,), F32),
            pltpu.VMEM((width,), F32),
            pltpu.VMEM((ff,), F32),
            pltpu.VMEM((width,), F32),
            pltpu.VMEM((width,), F32),
            pltpu.VMEM((width,), F32),
            pltpu.SemaphoreType.DMA((len(plan) + 3,)),
            pltpu.SemaphoreType.DMA((len(plan) + 9,)),
        ],
        compiler_params=pltpu.CompilerParams(vmem_limit_bytes=64_000_000),
    )(pooled_out, input_grad, grads, small)
    po, ig, qg, kg, vg, wo, up, dn, tab, fg, fs, ub, db, sg, ss = outs
    return po, ig.T, qg.T, kg.T, vg.T, wo, tab, fg, fs, up, ub, dn, db, sg, ss


def local(n_dp, *args):
    (
        hidden_in,
        segment_ids,
        query_weight,
        key_weight,
        value_weight,
        output_weight,
        position_table,
        first_gain,
        first_shift,
        up_weight,
        up_bias,
        down_weight,
        down_bias,
        second_gain,
        second_shift,
        cotangent,
    ) = args
    tokens, width = hidden_in.shape
    chunks = tokens // TOK_ROW
    pooled = tokens // 2
    half = HALF_ROW // 2
    heads = position_table.shape[0]
    hw = heads * DH
    ff = up_weight.shape[1]
    share = width // 4
    specs, row = [], 0
    for order, rows in PIECES:
        specs.append((row, rows, order))
        row += rows
    plan = (tuple(specs), TURNS, TAIL)
    bits = n_dp.bit_length() - 1
    links = 5 if n_dp == 8 else bits + 3
    total = ff + width + 4 * hw
    cfg = (n_dp, heads, HALF_ROW, chunks, width, ff, share, plan)
    vmem = lambda *shape: pltpu.VMEM(shape, BF16)
    wide = lambda *shape: pltpu.VMEM(shape, F32)
    slots = 3 * chunks
    inbox_rows = total * 7 // 4 + max(bits - 3, 0) * total // 8
    any_spec = pl.BlockSpec(memory_space=pl.ANY)
    scratch = [
        pltpu.VMEM((tokens,), jnp.int32),
        wide(width),
        wide(width),
        wide(ff),
        wide(width),
        wide(width),
        wide(width),
        wide(heads, 2 * REL),
        vmem(tokens, width),
        vmem(width, hw),
        vmem(width, hw),
        vmem(width, hw),
        vmem(hw, width),
        vmem(width, ff),
        vmem(ff, width),
        vmem(pooled, width),
        vmem(hw, width),
        vmem(hw, width),
        vmem(hw, width),
        vmem(HALF_ROW, TOK_ROW),
        wide(chunks, HALF_ROW, TOK_ROW),
        wide(2, HALF_ROW, LANES),
        wide(heads, 64, BAND),
        wide(heads, 64, BAND),
        vmem(pooled, width),
        wide(pooled // 2, width),
        vmem(pooled, hw),
        vmem(hw, pooled),
        vmem(hw, tokens),
        vmem(hw, tokens),
        wide(HALF_ROW, TOK_ROW),
        wide(chunks * heads, HALF_ROW, TOK_ROW),
        vmem(chunks * heads, HALF_ROW, TOK_ROW),
        vmem(HALF_ROW, TOK_ROW),
        vmem(pooled, hw),
        vmem(slots, HALF_ROW, width),
        vmem(slots, half, width),
        vmem(slots, half, width),
        vmem(slots, half, width),
        vmem(pooled, width),
        vmem(pooled, width),
        vmem(pooled, width),
        wide(pooled // 2, width),
        wide(pooled // 2, width),
        wide(pooled // 2, 1),
        wide(HALF_ROW, ff),
        vmem(pooled, ff),
        wide(pooled, ff),
        vmem(pooled, ff),
        wide(pooled // 2, width),
        vmem(pooled, width),
        vmem(pooled, hw),
        vmem(hw, pooled),
        vmem(hw, pooled),
        vmem(hw, tokens),
        vmem(hw, tokens),
        vmem(width, TOK_ROW),
        vmem(chunks, 4, share, TOK_ROW),
        vmem(chunks, 2, share, TOK_ROW),
        vmem(chunks, share, TOK_ROW),
        vmem(chunks, share, TOK_ROW),
        vmem(share, tokens),
        vmem(total, width),
        vmem(total, width),
        vmem(inbox_rows, width),
        wide(6, 8, width),
        wide(SMALL_ROWS, width),
        wide(bits + 1, SMALL_ROWS, width),
        pltpu.SemaphoreType.DMA((16,)),
        pltpu.SemaphoreType.DMA((len(specs) + 3,)),
        pltpu.SemaphoreType.DMA((SENDS,)),
        pltpu.SemaphoreType.DMA((links * len(specs) + RECEIVES,)),
    ]
    pooled_out, input_grad, grads, small = pl.pallas_call(
        partial(fused, cfg),
        name="layer",
        out_shape=(
            jax.ShapeDtypeStruct((pooled, width), BF16),
            jax.ShapeDtypeStruct((share, tokens), BF16),
            jax.ShapeDtypeStruct((total, width), BF16),
            jax.ShapeDtypeStruct((SMALL_ROWS, width), F32),
        ),
        in_specs=[any_spec] * 16,
        out_specs=(any_spec,) * 4,
        scratch_shapes=scratch,
        compiler_params=pltpu.CompilerParams(
            collective_id=0, has_side_effects=True, vmem_limit_bytes=64_000_000
        ),
    )(
        segment_ids,
        first_gain,
        first_shift,
        up_bias,
        down_bias,
        second_gain,
        second_shift,
        position_table,
        hidden_in,
        query_weight.T,
        key_weight.T,
        value_weight.T,
        output_weight,
        up_weight,
        down_weight,
        cotangent,
    )
    return finish(pooled_out, input_grad, grads, small, heads, ff, width)


def solution(mesh):
    return jax.shard_map(
        partial(local, mesh.shape["dp"]),
        mesh=mesh,
        in_specs=(
            P("dp", None),
            P("dp"),
            P(None, "tensor"),
            P(None, "tensor"),
            P(None, "tensor"),
            P("tensor", None),
            P("tensor", None),
            P(),
            P(),
            P(None, "tensor"),
            P("tensor"),
            P("tensor", None),
            P(),
            P(),
            P(),
            P("dp", None),
        ),
        out_specs=(
            P("dp", None),
            P("dp", "tensor"),
            P(None, "tensor"),
            P(None, "tensor"),
            P(None, "tensor"),
            P("tensor", None),
            P("tensor", None),
            P(),
            P(),
            P(None, "tensor"),
            P("tensor"),
            P("tensor", None),
            P(),
            P(),
            P(),
        ),
        check_vma=False,
    )
```

```python
import math
from functools import partial

import jax
import jax.numpy as jnp
from jax import lax
from jax.experimental import pallas as pl
from jax.experimental.pallas import tpu as pltpu
from jax.sharding import PartitionSpec as P

DH = 64
TOK_ROW = 512
LANES = 128
HALF_ROW = TOK_ROW // 2
REL = 64
EPSILON = 1e-06
NEGATIVE = -1e30
MESH = pl.DeviceIdType.MESH
F32 = jnp.float32
BF16 = jnp.bfloat16

FIRST_GAIN, FIRST_SHIFT, DOWN_BIAS, SECOND_GAIN, SECOND_SHIFT, UP_BIAS = range(6)
UP_ROW, TABLE_ROW, SMALL_ROWS = 8, 9, 16
BAND = 1024
ROLL = 1152
SENDS = 28
RECEIVES = 24
PIECES = (('Y', 192), ('Z', 128), ('Z', 64), ('Y', 128), ('Y', 128), ('Z', 64), ('Y', 64), ('Z', 64), ('Y', 128), ('Y', 192), ('Z', 128), ('Y', 128), ('Y', 128), ('Z', 128), ('Y', 64), ('Y', 192), ('Y', 128), ('Y', 128), ('Y', 128))
TURNS = [[2, 3, 1, 4], [12], [], [2, 3, 9], [4], [2, 10, 0], [1, 12], [3, 6], [9, 2, 1, 4], [3, 11], [], [], [0, 15, 4], [6, 10, 3, 2], [1], [4, 12, 11, 17]]
TAIL = [10, 3, 9, -1, 2, 12, 15, -1, 4, 1, 0, -1, 9, 2, 6, -1, 12, 17, 10, -1, 11, 1, 3, -1, 0, 12, 7, -1, 18, 15, 9, -1, 13, 4, 6, -1, 10, 11, 17, -1, 8, 1, 0, -1, 14, 12, 7, -1, 15, 6, 5, -1, 16, 18, 9, -1, 10, 8, 13, -1, 11, 14, 0, -1, 17, 6, 5, -1, 7, 16, 15, -1, 18, 9, 13, -1, 10, 8, 17, -1, 14, 5, 11, -1, 0, 18, 16, -1, 6, 8, 7, -1, 14, 13, 15, -1, 18, 5, 16, -1, 17, 8, 11, -1, 14, 7, 16, -1, 13, 18, 7, -1, 8, 15, 14, -1, 13, 5, 16, -1, 17, 5, 7, -1, 18, 8, 14, -1, 13, 16, 5, -1]
U_SOFT, U_SBACK, U_NORM, U_GELU = 8, 2, 8, 4


def dot(left, right, left_dim=1, right_dim=0):
    return lax.dot_general(
        left, right, (((left_dim,), (right_dim,)), ((), ())), preferred_element_type=F32
    )


def tiles(count, step, body, unroll=1):
    unroll = math.gcd(unroll, count // step)
    stride = step * unroll

    def one(index, unused):
        for part in range(unroll):
            body(pl.multiple_of(index * stride + part * step, step))
        return unused

    if count == stride:
        for row in range(0, count, step):
            body(row)
    else:
        lax.fori_loop(0, count // stride, one, 0)


def across_row(column):
    return jnp.concatenate([column] * (TOK_ROW // LANES), axis=1)


def fold(value):
    total = value[0:8]
    for start in range(8, value.shape[0], 8):
        total = total + value[start : start + 8]
    return total


class Copy:
    def __init__(self, copy, send, recv, free):
        self.copy, self.send, self.recv, self.free = copy, send, recv, free

    def start(self):
        if self.send is None:
            self.copy.start()
        else:
            pl.when(self.send)(self.copy.start)

    def wait(self):
        if self.send is None:
            self.copy.wait()
        else:
            pl.when(self.send)(self.copy.wait_send)
            pl.when(self.recv)(self.copy.wait_recv)
        self.free()


class Copies:
    def __init__(self, send_sems, recv_sems):
        self.send_sems, self.recv_sems = send_sems, recv_sems
        self.idle, self.keys = list(range(SENDS)), {}

    def start(self, key, source, target, device, send=None, recv=None):
        index = self.idle.pop(0)
        copy = Copy(
            pltpu.make_async_remote_copy(
                src_ref=source,
                dst_ref=target,
                send_sem=self.send_sems.at[index],
                recv_sem=self.recv_sems.at[self.keys.setdefault(key, len(self.keys))],
                device_id=device,
                device_id_type=MESH,
            ),
            send,
            recv,
            lambda: self.idle.append(index),
        )
        copy.start()
        return copy


class Grid:
    def __init__(self, n_dp, d, t):
        self.bits = n_dp.bit_length() - 1
        self.mine = [lax.rem(d // (1 << bit), 2) for bit in range(self.bits)]
        self.across = [(d + (1 - 2 * self.mine[b]) * (1 << b), t) for b in range(self.bits)]
        self.peers = list(self.across)
        self.plans = {}
        if n_dp == 8:
            z = d // 2
            middle = jnp.logical_or(z == 1, z == 2)
            end = jnp.logical_not(middle)
            upper = z // 2
            facing = (d + (3 - 2 * z) * 2, t)
            self.peers.append(facing)
            everyone = (None, None, None, "y")
            inner = (middle, middle, middle)
            y = ("half", self.across[0], self.mine[0])
            y_back = ("back", self.across[0], self.mine[0])
            gather = ("whole", self.across[1], 0, end, middle, middle, "z")
            spread = ("same", self.across[1], 0, middle, end, middle, "z")
            mid = ("half", facing, upper) + inner + ("mid",)
            mid_back = ("back", facing, upper) + inner + ("mid_back",)
            y_inner = inner + ("y",)
            y_out = ("y_back",)
            self.plans["Y"] = (
                y + everyone,
                gather,
                mid,
                mid_back,
                spread,
                y_back + everyone[:3] + y_out,
            )
            self.plans["Z"] = (gather, mid, y + y_inner, y_back + inner + y_out, mid_back, spread)
        else:
            everyone = (None, None, None)
            halving = list(range(min(3, self.bits)))
            plan = [("half", self.across[b], self.mine[b]) + everyone + (b,) for b in halving]
            plan += [
                ("whole", self.across[b], 0) + everyone + (b,)
                for b in range(len(halving), self.bits)
            ]
            plan += [
                ("back", self.across[b], self.mine[b]) + everyone + (self.bits + b,)
                for b in reversed(halving)
            ]
            self.plans["Y"] = self.plans["Z"] = tuple(plan)

    def inbox_rows(self, order, rows):
        total = 0
        for kind, *unused in self.plans[order]:
            if kind == "half":
                rows //= 2
            if kind in ("half", "whole"):
                total += rows
        return total


class Stream:
    def __init__(self, copies, buffers, inbox_row, row, rows, plan):
        self.copies, self.plan = copies, plan
        self.grads, self.summed, self.inbox = buffers
        self.inbox_row, self.rows, self.pos = inbox_row, rows, row
        self.first, self.count = row, rows
        self.step, self.pending = 0, None

    def begin(self):
        kind, device, mine, send, recv, unused, link = self.plan[self.step]
        size = self.rows
        at = self.pos
        if kind == "half":
            size //= 2
            self.keep = pl.multiple_of(self.pos + mine * size, 16)
            at = pl.multiple_of(self.pos + (1 - mine) * size, 16)
        if kind in ("half", "whole"):
            source = self.grads.at[pl.ds(at, size)]
            target = self.inbox.at[pl.ds(self.inbox_row, size)]
        else:
            source = target = self.summed.at[pl.ds(at, size)]
        self.pending = self.copies.start((self.first, link), source, target, device, send, recv)
        self.size = size

    def finish(self):
        kind, device, mine, send, recv, adds, link = self.plan[self.step]
        self.pending.wait()
        self.step += 1
        if kind == "back":
            self.pos = pl.multiple_of(self.pos - mine * self.size, 16)
            self.rows = 2 * self.size
        elif kind != "same":
            if kind == "half":
                self.pos, self.rows = self.keep, self.size
            base, inbox_row, grads, inbox = self.pos, self.inbox_row, self.grads, self.inbox
            result = self.summed if self.plan[self.step][0] == "back" else grads
            step = 32 if self.size % 32 == 0 else 16

            def add(row):
                rows = pl.ds(pl.multiple_of(base + row, 16), step)
                arrived = inbox[pl.ds(pl.multiple_of(inbox_row + row, 16), step), :]
                result[rows, :] = (grads[rows, :].astype(F32) + arrived.astype(F32)).astype(BF16)

            def add_all():
                tiles(self.size, step, add, 2)

            if adds is None:
                add_all()
            else:
                pl.when(adds)(add_all)
            self.inbox_row += self.size

    def done(self):
        return self.step == len(self.plan)

    def turn(self):
        if self.pending is not None:
            self.finish()
            self.pending = None
        if not self.done():
            self.begin()


def fused(
    cfg,
    seg_h,
    first_gain_h,
    first_shift_h,
    up_bias_h,
    down_bias_h,
    second_gain_h,
    second_shift_h,
    tab_h,
    hid_h,
    wq_h,
    wk_h,
    wv_h,
    wo_h,
    up_h,
    dn_h,
    cot_h,
    po_h,
    ig_h,
    g_h,
    small_h,
    seg_ref,
    first_gain,
    first_shift,
    up_bias_in,
    down_bias_in,
    second_gain,
    second_shift,
    tab_ref,
    hid,
    wq,
    wk,
    wv,
    wo,
    up,
    dn,
    cot,
    wqT,
    wkT,
    wvT,
    dup,
    mask,
    stat,
    bias,
    tacc,
    plow,
    pown,
    q,
    qT,
    kT,
    vT,
    score,
    probs,
    problow,
    ds,
    ctx,
    arA,
    arR1,
    arB,
    arR2,
    f1,
    f2,
    f3,
    first_out,
    normed1,
    inv1,
    pre,
    act,
    gp,
    preg,
    sgrad,
    po,
    cg,
    cgT,
    dqT,
    kgT,
    vgT,
    f3dT,
    tp,
    inR1,
    inB,
    inR2,
    igo,
    grads,
    summed,
    inbox,
    acc,
    small,
    smallR,
    in_sems,
    out_sems,
    send_sems,
    recv_sems,
):
    n_dp, heads, rows_per, chunks, width, ff, share, stream_plan = cfg
    half = HALF_ROW // 2
    d = lax.axis_index("dp")
    t = lax.axis_index("tensor")
    core = lax.rem(t, 2)
    side = t // 2
    sib_id = (d, t + 1 - 2 * core)
    cross_id = (d, t + 2 - 4 * side)
    grid = Grid(n_dp, d, t)
    bits = grid.bits
    own = pl.multiple_of(core * half, half)
    away = pl.multiple_of((1 - core) * half, half)

    loads = [
        pltpu.make_async_copy(source, target, in_sems.at[index])
        for index, (source, target) in enumerate(
            [
                (hid_h, hid),
                (wk_h, wkT),
                (wv_h, wvT),
                (wq_h, wqT),
                (wo_h, wo),
                (up_h, up),
                (dn_h, dn),
                (cot_h, cot),
                (seg_h, seg_ref),
                (tab_h, tab_ref),
                (first_gain_h, first_gain),
                (first_shift_h, first_shift),
                (up_bias_h, up_bias_in),
                (down_bias_h, down_bias_in),
                (second_gain_h, second_gain),
                (second_shift_h, second_shift),
            ]
        )
    ]
    early, vectors, late = loads[:5], loads[8:], loads[5:8]
    for load in vectors[:2] + early:
        load.start()
    barrier = pltpu.get_barrier_semaphore()
    for device in [sib_id, cross_id] + grid.peers:
        pl.semaphore_signal(barrier, inc=1, device_id=device, device_id_type=MESH)

    row_i = lax.broadcasted_iota(jnp.int32, (HALF_ROW, TOK_ROW), 0)
    col_i = lax.broadcasted_iota(jnp.int32, (HALF_ROW, TOK_ROW), 1)
    dup[...] = jnp.where(col_i // 2 == row_i, 1.0, 0.0).astype(BF16)
    evens = jnp.where(col_i == 2 * row_i, 1.0, 0.0).astype(BF16)
    vectors[0].wait()
    segk = [
        seg_ref[g * TOK_ROW : (g + 1) * TOK_ROW].astype(F32).reshape(1, TOK_ROW)
        for g in range(chunks)
    ]
    for g in range(chunks):
        rows = jnp.broadcast_to(segk[g], (LANES, TOK_ROW)).astype(BF16)
        column = across_row(dot(evens, rows, 1, 1))
        mask[g] = jnp.where(column == segk[g], 0.0, NEGATIVE)
    vectors[1].wait()
    for h in range(heads):
        table = jnp.concatenate(
            [
                jnp.broadcast_to(tab_ref[h : h + 1, 0:1], (REL, 512)),
                jnp.broadcast_to(tab_ref[h : h + 1, :], (REL, 2 * REL)),
                jnp.broadcast_to(tab_ref[h : h + 1, 2 * REL - 1 : 2 * REL], (REL, 512)),
            ],
            axis=1,
        )
        bias[h] = pltpu.roll(table, ROLL - 64, 1, stride=2, stride_axis=0)[:, :BAND]
    tacc[...] = jnp.zeros_like(tacc)
    acc[...] = jnp.zeros_like(acc)
    small[...] = jnp.zeros_like(small)

    copies = Copies(send_sems, recv_sems)

    reduce_one, reduce_two = {}, {}

    def reduce_start(which, g):
        slot = which * chunks + g
        reduce_one[slot] = copies.start(("one", g), arA.at[slot, pl.ds(away, half)], arR1.at[slot], sib_id)

    def reduce_middle(which, g):
        slot = which * chunks + g
        reduce_one[slot].wait()

        def add(row):
            mine = arA[slot, pl.ds(pl.multiple_of(own + row, 32), 32), :].astype(F32)
            arB[slot, pl.ds(row, 32), :] = (
                mine + arR1[slot, pl.ds(row, 32), :].astype(F32)
            ).astype(BF16)

        tiles(half, 32, add, 2)
        reduce_two[slot] = copies.start(("two", g, which % 2), arB.at[slot], arR2.at[slot], cross_id)

    def reduced(which, g, row):
        slot = which * chunks + g
        return arB[slot, pl.ds(row, 16), :].astype(F32) + arR2[slot, pl.ds(row, 16), :].astype(F32)

    shares = {}

    def share_start(name, buffer, g):
        rows = buffer.at[pl.ds(pl.multiple_of(g * HALF_ROW + own, half), half)]
        key = ("po" if name == "po" else "share", g)
        shares[name, g] = copies.start(key, rows, rows, sib_id)

    def qkv(g):
        tokens = hid[g * TOK_ROW : (g + 1) * TOK_ROW, :]
        pooled = slice(g * HALF_ROW, (g + 1) * HALF_ROW)
        cols = slice(g * TOK_ROW, (g + 1) * TOK_ROW)
        plow[pooled, :] = (dot(dup[...], tokens) * 0.5).astype(BF16)
        mine = hid[pl.ds(pl.multiple_of(g * TOK_ROW + core * HALF_ROW, HALF_ROW), HALF_ROW), :]
        pown[g * half : (g + 1) * half, :] = dot(dup[0:half, 0:HALF_ROW], mine) * 0.5
        kT[:, cols] = dot(wkT[...], tokens, 1, 1).astype(BF16)
        vT[:, cols] = dot(wvT[...], tokens, 1, 1).astype(BF16)
        scale = 1.0 / math.sqrt(DH)
        q[pooled, :] = (dot(plow[pooled, :], wqT[...], 1, 1) * scale).astype(BF16)
        qT[:, pooled] = (dot(wqT[...], plow[pooled, :], 1, 1) * scale).astype(BF16)

    def attend(g):
        pooled = slice(g * HALF_ROW, (g + 1) * HALF_ROW)
        cols = slice(g * TOK_ROW, (g + 1) * TOK_ROW)
        for h in range(heads):
            lanes = slice(h * DH, (h + 1) * DH)
            slot = g * heads + h
            score[...] = dot(q[pooled, lanes], kT[lanes, cols])

            def add_bias(row):
                here = pl.ds(row, 32)
                band, part = 512 - 128 * (row // 64), row % 64
                if not isinstance(row, int):
                    part = pl.multiple_of(lax.rem(row, 64), 32)
                    band = pl.multiple_of(band, 128)
                raw = score[here, :] + bias[h, pl.ds(part, 32), pl.ds(band, TOK_ROW)]
                raw = raw + mask[g, here, :]
                score[here, :] = raw
                peak = jnp.max(raw, axis=-1, keepdims=True)
                stat[0, here, :] = jnp.broadcast_to(peak, (32, LANES))

            def weigh(row):
                here = pl.ds(row, 32)
                weights = jnp.exp(score[here, :] - across_row(stat[0, here, :]))
                score[here, :] = weights
                total = jnp.sum(weights, axis=-1, keepdims=True)
                stat[1, here, :] = jnp.broadcast_to(total, (32, LANES))

            def divide(row):
                here = pl.ds(row, 32)
                prob = score[here, :] * across_row(1.0 / stat[1, here, :])
                probs[slot, here, :] = prob
                problow[slot, here, :] = prob.astype(BF16)

            for step in (add_bias, weigh, divide):
                tiles(HALF_ROW, 32, step, U_SOFT)
            ctx[pooled, lanes] = dot(problow[slot], vT[lanes, cols], 1, 1).astype(BF16)
        arA[g] = dot(ctx[pooled, :], wo[...]).astype(BF16)

    def first_norm(g):
        reduce_two[g].wait()
        gain, shift = first_gain[...].reshape(1, width), first_shift[...].reshape(1, width)

        def one(row):
            here = pl.ds(pl.multiple_of(g * half + row, 16), 16)
            value = pown[here, :] + reduced(0, g, row)
            centred = value - jnp.mean(value, axis=-1, keepdims=True)
            inverse = lax.rsqrt(jnp.mean(centred * centred, axis=-1, keepdims=True) + EPSILON)
            normed = centred * inverse
            out = normed * gain + shift
            normed1[here, :] = normed
            inv1[here, :] = inverse
            first_out[here, :] = out
            f1[pl.ds(pl.multiple_of(g * HALF_ROW + own + row, 16), 16), :] = out.astype(BF16)

        tiles(half, 16, one, U_NORM)
        share_start("f1", f1, g)

    def feed_forward(g):
        shares["f1", g].wait()
        pooled = slice(g * HALF_ROW, (g + 1) * HALF_ROW)
        pre[...] = dot(f1[pooled, :], up[...])
        up_bias = up_bias_in[...].reshape(1, ff)

        def one(row):
            value = pre[pl.ds(row, 16), :] + up_bias
            cdf = 0.5 * (1.0 + lax.erf(value * (1.0 / math.sqrt(2.0))))
            density = jnp.exp(-0.5 * value * value) * (1.0 / math.sqrt(2.0 * math.pi))
            here = pl.ds(pl.multiple_of(g * HALF_ROW + row, 16), 16)
            act[here, :] = (value * cdf).astype(BF16)
            gp[here, :] = cdf + value * density

        tiles(HALF_ROW, 16, one, U_GELU)
        arA[chunks + g] = dot(act[pooled, :], dn[...]).astype(BF16)

    def second_norm(g):
        reduce_two[chunks + g].wait()
        gain, shift = second_gain[...].reshape(1, width), second_shift[...].reshape(1, width)
        down_bias = down_bias_in[...].reshape(1, width)

        def one(row):
            here = pl.ds(pl.multiple_of(g * half + row, 16), 16)
            full = pl.ds(pl.multiple_of(g * HALF_ROW + own + row, 16), 16)
            value = first_out[here, :] + reduced(1, g, row) + down_bias
            centred = value - jnp.mean(value, axis=-1, keepdims=True)
            inverse = lax.rsqrt(jnp.mean(centred * centred, axis=-1, keepdims=True) + EPSILON)
            normed = centred * inverse
            po[full, :] = (normed * gain + shift).astype(BF16)
            upstream = cot[full, :].astype(F32)
            scaled = upstream * gain
            grad = inverse * (
                scaled
                - jnp.mean(scaled, axis=-1, keepdims=True)
                - normed * jnp.mean(scaled * normed, axis=-1, keepdims=True)
            )
            sgrad[here, :] = grad
            f2[full, :] = grad.astype(BF16)
            acc[SECOND_GAIN] += fold(upstream * normed)
            acc[SECOND_SHIFT] += fold(upstream)
            acc[DOWN_BIAS] += fold(grad)

        tiles(half, 16, one, U_NORM)
        share_start("f2", f2, g)
        share_start("po", po, g)

    def feed_back(g):
        shares["f2", g].wait()
        pooled = slice(g * HALF_ROW, (g + 1) * HALF_ROW)
        pre[...] = dot(f2[pooled, :], dn[...], 1, 1)

        def one(row):
            here = pl.ds(pl.multiple_of(g * HALF_ROW + row, 16), 16)
            low = (gp[here, :] * pre[pl.ds(row, 16), :]).astype(BF16)
            preg[here, :] = low
            acc[UP_BIAS, :, :ff] += fold(low.astype(F32))

        tiles(HALF_ROW, 16, one, U_GELU)
        arA[2 * chunks + g] = dot(preg[pooled, :], up[...], 1, 1).astype(BF16)

    def first_back(g):
        reduce_two[2 * chunks + g].wait()
        gain = first_gain[...].reshape(1, width)

        def one(row):
            here = pl.ds(pl.multiple_of(g * half + row, 16), 16)
            full = pl.ds(pl.multiple_of(g * HALF_ROW + own + row, 16), 16)
            upstream = reduced(2, g, row) + sgrad[here, :]
            normed = normed1[here, :]
            scaled = upstream * gain
            grad = inv1[here, :] * (
                scaled
                - jnp.mean(scaled, axis=-1, keepdims=True)
                - normed * jnp.mean(scaled * normed, axis=-1, keepdims=True)
            )
            f3[full, :] = grad.astype(BF16)
            acc[FIRST_GAIN] += fold(upstream * normed)
            acc[FIRST_SHIFT] += fold(upstream)

        tiles(half, 16, one, U_NORM)
        share_start("f3", f3, g)

    def attend_back(g, after):
        shares["f3", g].wait()
        pooled = slice(g * HALF_ROW, (g + 1) * HALF_ROW)
        cols = slice(g * TOK_ROW, (g + 1) * TOK_ROW)
        cg[pooled, :] = dot(f3[pooled, :], wo[...], 1, 1).astype(BF16)
        cgT[:, pooled] = dot(wo[...], f3[pooled, :], 1, 1).astype(BF16)
        for h in range(heads):
            lanes = slice(h * DH, (h + 1) * DH)
            slot = g * heads + h
            score[...] = dot(cg[pooled, lanes], vT[lanes, cols])

            def one(row):
                block = row // 64
                part = pl.multiple_of(lax.rem(row, 64), 32)
                band = pl.ds(pl.multiple_of(512 - 128 * block, 128), TOK_ROW)
                prob = probs[slot, pl.ds(row, 32), :]
                prob_grad = score[pl.ds(row, 32), :]
                inner = jnp.sum(prob * prob_grad, axis=-1, keepdims=True)
                grad = prob * (prob_grad - inner)
                ds[pl.ds(row, 32), :] = grad.astype(BF16)
                tacc[h, pl.ds(part, 32), band] += grad

            tiles(HALF_ROW, 32, one, U_SBACK)
            scale = 1.0 / math.sqrt(DH)
            dqT[lanes, pooled] = (dot(kT[lanes, cols], ds[...], 1, 1) * scale).astype(BF16)
            kgT[lanes, cols] = dot(qT[lanes, pooled], ds[...]).astype(BF16)
            vgT[lanes, cols] = dot(cgT[lanes, pooled], problow[slot]).astype(BF16)
            after()

    in_one, in_two = {}, {}

    def input_part(g):
        pooled = slice(g * HALF_ROW, (g + 1) * HALF_ROW)
        cols = slice(g * TOK_ROW, (g + 1) * TOK_ROW)
        doubled = (dot(dqT[:, pooled], dup[...]) * 0.5).astype(BF16)
        f3dT[...] = (dot(f3[pooled, :], dup[...], 0, 0) * 0.125).astype(BF16)
        for b in range(4):
            rows = slice(b * share, (b + 1) * share)
            total = dot(wk[rows, :], kgT[:, cols]) + dot(wv[rows, :], vgT[:, cols])
            total = total + dot(wq[rows, :], doubled) + f3dT[rows, :].astype(F32)
            tp[g, b] = total.astype(BF16)
        for index, block in enumerate((1 - core + 2 * (1 - side), 1 - core + 2 * side)):
            in_one[g, index] = copies.start(("in", g, index), tp.at[g, block], inR1.at[g, index], sib_id)

    def input_middle(g):
        far = core + 2 * (1 - side)
        in_one[g, 0].wait()

        def add(row):
            here = pl.ds(row, 32)
            inB[g, here, :] = (
                tp[g, far, here, :].astype(F32) + inR1[g, 0, here, :].astype(F32)
            ).astype(BF16)

        tiles(share, 32, add, 2)
        in_two[g] = copies.start(("in two", g), inB.at[g], inR2.at[g], cross_id)

    def input_end(g):
        in_one[g, 1].wait()
        in_two[g].wait()

        def add(row):
            here = pl.ds(row, 32)
            igo[here, g * TOK_ROW : (g + 1) * TOK_ROW] = (
                tp[g, t, here, :].astype(F32)
                + inR1[g, 1, here, :].astype(F32)
                + inR2[g, here, :].astype(F32)
            ).astype(BF16)

        tiles(share, 32, add, 2)

    def small_sums():
        for index in range(5):
            small[index : index + 1, :] = jnp.sum(acc[index], axis=0, keepdims=True)
        small[UP_ROW : UP_ROW + 1, :] = jnp.sum(acc[UP_BIAS], axis=0, keepdims=True)
        lane = lax.broadcasted_iota(jnp.int32, (1, BAND), 1)
        lane_out = lax.broadcasted_iota(jnp.int32, (1, 2 * REL), 1)
        sub = lax.broadcasted_iota(jnp.int32, (8, BAND), 0)
        for h in range(heads):
            part = tacc[h]
            for size in (32, 16, 8):
                part = part[0:size] + pltpu.roll(part[size : 2 * size], BAND - 2 * size, 1)
            for size in (4, 2, 1):
                part = jnp.where(
                    lax.rem(sub // size, 2) == 1, pltpu.roll(part, BAND - 2 * size, 1), part
                )
            part = jnp.sum(part, axis=0, keepdims=True)
            low = jnp.sum(jnp.where(lane <= 448, part, 0.0), axis=1, keepdims=True)
            high = jnp.sum(jnp.where(lane >= 575, part, 0.0), axis=1, keepdims=True)
            middle = pltpu.roll(part, BAND - 448, 1)[:, 0 : 2 * REL]
            middle = jnp.where(
                lane_out == 0, low, jnp.where(lane_out == 2 * REL - 1, high, middle)
            )
            small[TABLE_ROW + h : TABLE_ROW + h + 1, 0 : 2 * REL] = middle

    for load in early[:4]:
        load.wait()
    for load in vectors[2:] + late:
        load.start()
    qkv(0)
    early[4].wait()
    attend(0)
    pl.semaphore_wait(barrier, 2 + len(grid.peers))
    reduce_start(0, 0)
    qkv(1)
    reduce_middle(0, 0)
    attend(1)
    reduce_start(0, 1)
    for load in vectors[2:]:
        load.wait()
    first_norm(0)
    reduce_middle(0, 1)
    for load in late:
        load.wait()
    feed_forward(0)
    reduce_start(1, 0)
    first_norm(1)
    reduce_middle(1, 0)
    feed_forward(1)
    reduce_start(1, 1)
    second_norm(0)
    reduce_middle(1, 1)
    feed_back(0)
    reduce_start(2, 0)
    second_norm(1)
    reduce_middle(2, 0)
    feed_back(1)
    reduce_start(2, 1)

    outs = []

    def put(source, target):
        copy = pltpu.make_async_copy(source, target, out_sems.at[len(outs)])
        copy.start()
        outs.append(copy)

    specs, turns, tail = stream_plan
    streams, inbox_row = [], 0
    for row, rows, order in specs:
        streams.append(
            Stream(copies, (grads, summed, inbox), inbox_row, row, rows, grid.plans[order])
        )
        inbox_row += grid.inbox_rows(order, rows)
    turns, chores = list(turns), []

    def advance(index):
        if index < 0:
            if chores:
                chores.pop(0)()
            return
        stream = streams[index]
        if not stream.done():
            stream.turn()
            if stream.done():
                rows = pl.ds(stream.first, stream.count)
                put(summed.at[rows], g_h.at[rows])

    def mark():
        for index in turns.pop(0) if turns else ():
            advance(index)

    grads[0:ff, :] = dot(act[...], f2[...], 0, 0).astype(BF16)
    mark()
    reduce_middle(2, 1)
    grads[ff : ff + width, :] = dot(f1[...], preg[...], 0, 0).astype(BF16)
    mark()
    first_back(0)
    wk[...] = wkT[...].T
    wv[...] = wvT[...].T
    wq[...] = wqT[...].T
    mark()
    attend_back(0, mark)
    first_back(1)
    mark()
    attend_back(1, mark)
    base = ff + width
    hw = heads * DH
    grads[base : base + hw, :] = dot(ctx[...], f3[...], 0, 0).astype(BF16)
    mark()
    grads[base + hw : base + 2 * hw, :] = dot(dqT[...], plow[...]).astype(BF16)
    mark()
    grads[base + 2 * hw : base + 3 * hw, :] = dot(kgT[...], hid[...]).astype(BF16)
    grads[base + 3 * hw : base + 4 * hw, :] = dot(vgT[...], hid[...]).astype(BF16)
    mark()
    small_sums()
    waiting = [copies.start("small", small.at[pl.ds(0, 8)], smallR.at[0, pl.ds(0, 8)], sib_id)]
    mark()
    input_part(0)
    mark()
    input_part(1)
    mark()

    def small_next(bit):
        waiting.pop().wait()
        if bit == 0:
            small[0:8, :] = small[0:8, :] + smallR[0, 0:8, :]
        else:
            small[...] = small[...] + smallR[bit]
        if bit < bits:
            waiting.append(
                copies.start(("small", bit), small, smallR.at[bit + 1], grid.across[bit])
            )
        else:
            put(small, small_h)

    def input_done(g):
        input_end(g)
        if g == chunks - 1:
            put(igo, ig_h)

    def pooled_done():
        for g in range(chunks):
            shares["po", g].wait()
        put(po, po_h)

    chores += [partial(input_middle, 0), partial(small_next, 0), partial(input_middle, 1)]
    chores += [pooled_done] + [partial(small_next, bit) for bit in range(1, bits + 1)]
    chores += [partial(input_done, g) for g in range(chunks)]
    for index in tail:
        advance(index)
    while chores:
        advance(-1)
    while not all(stream.done() for stream in streams):
        advance([stream.done() for stream in streams].index(False))
    for copy in outs:
        copy.wait()


def finish_kernel(
    plan, po_h, ig_h, g_h, small_h, po_o, ig_o, q_o, k_o, v_o, wo_o, up_o, dn_o, *rest
):
    tab_o, fg_o, fs_o, ub_o, db_o, sg_o, ss_o, po, ig, low, wide, small, tab, *vectors = rest
    *vectors, in_sems, out_sems = vectors
    targets = (dn_o, up_o, wo_o, q_o, k_o, v_o)
    get_small = pltpu.make_async_copy(small_h, small, in_sems.at[len(plan)])
    get_po = pltpu.make_async_copy(po_h, po, in_sems.at[len(plan) + 1])
    get_ig = pltpu.make_async_copy(ig_h, ig, in_sems.at[len(plan) + 2])
    gets = [
        pltpu.make_async_copy(
            g_h.at[pl.ds(row, rows)], low.at[pl.ds(row, rows)], in_sems.at[index]
        )
        for index, (row, rows, unused, unused_row) in enumerate(plan)
    ]
    for get in [get_small] + gets + [get_po, get_ig]:
        get.start()
    puts = []

    def put(source, target):
        copy = pltpu.make_async_copy(source, target, out_sems.at[len(puts)])
        copy.start()
        puts.append(copy)

    get_small.wait()
    for vector, row, out in zip(
        vectors,
        (FIRST_GAIN, FIRST_SHIFT, UP_ROW, DOWN_BIAS, SECOND_GAIN, SECOND_SHIFT),
        (fg_o, fs_o, ub_o, db_o, sg_o, ss_o),
    ):
        vector[...] = small[row, : vector.shape[0]]
        put(vector, out)
    tab[...] = small[TABLE_ROW : TABLE_ROW + tab.shape[0], : 2 * REL]
    put(tab, tab_o)
    for get, (row, rows, index, target_row) in zip(gets, plan):
        get.wait()

        def widen(here):
            where = pl.ds(pl.multiple_of(row + here, 32), 32)
            wide[where, :] = low[where, :].astype(F32)

        tiles(rows, 32, widen)
        put(wide.at[pl.ds(row, rows)], targets[index].at[pl.ds(target_row, rows)])
    get_po.wait()
    put(po, po_o)
    get_ig.wait()
    put(ig, ig_o)
    for copy in puts:
        copy.wait()


def finish(pooled_out, input_grad, grads, small, heads, ff, width):
    hw = heads * DH
    total = grads.shape[0]
    plan, row = [], 0
    for index, rows in enumerate((ff, width, hw, hw, hw, hw)):
        for start in range(0, rows, 384):
            size = min(384, rows - start)
            plan.append((row + start, size, index, start))
        row += rows
    vector = jax.ShapeDtypeStruct((width,), F32)
    any_spec = pl.BlockSpec(memory_space=pl.ANY)
    outs = pl.pallas_call(
        partial(finish_kernel, tuple(plan)),
        name="finish",
        out_shape=(
            jax.ShapeDtypeStruct(pooled_out.shape, BF16),
            jax.ShapeDtypeStruct(input_grad.shape, BF16),
            jax.ShapeDtypeStruct((hw, width), F32),
            jax.ShapeDtypeStruct((hw, width), F32),
            jax.ShapeDtypeStruct((hw, width), F32),
            jax.ShapeDtypeStruct((hw, width), F32),
            jax.ShapeDtypeStruct((width, ff), F32),
            jax.ShapeDtypeStruct((ff, width), F32),
            jax.ShapeDtypeStruct((heads, 2 * REL), F32),
            vector,
            vector,
            jax.ShapeDtypeStruct((ff,), F32),
            vector,
            vector,
            vector,
        ),
        in_specs=[any_spec] * 4,
        out_specs=(any_spec,) * 15,
        scratch_shapes=[
            pltpu.VMEM(pooled_out.shape, BF16),
            pltpu.VMEM(input_grad.shape, BF16),
            pltpu.VMEM((total, width), BF16),
            pltpu.VMEM((total, width), F32),
            pltpu.VMEM((SMALL_ROWS, width), F32),
            pltpu.VMEM((heads, 2 * REL), F32),
            pltpu.VMEM((width,), F32),
            pltpu.VMEM((width,), F32),
            pltpu.VMEM((ff,), F32),
            pltpu.VMEM((width,), F32),
            pltpu.VMEM((width,), F32),
            pltpu.VMEM((width,), F32),
            pltpu.SemaphoreType.DMA((len(plan) + 3,)),
            pltpu.SemaphoreType.DMA((len(plan) + 9,)),
        ],
        compiler_params=pltpu.CompilerParams(vmem_limit_bytes=64_000_000),
    )(pooled_out, input_grad, grads, small)
    po, ig, qg, kg, vg, wo, up, dn, tab, fg, fs, ub, db, sg, ss = outs
    return po, ig.T, qg.T, kg.T, vg.T, wo, tab, fg, fs, up, ub, dn, db, sg, ss


def local(n_dp, *args):
    (
        hidden_in,
        segment_ids,
        query_weight,
        key_weight,
        value_weight,
        output_weight,
        position_table,
        first_gain,
        first_shift,
        up_weight,
        up_bias,
        down_weight,
        down_bias,
        second_gain,
        second_shift,
        cotangent,
    ) = args
    tokens, width = hidden_in.shape
    chunks = tokens // TOK_ROW
    pooled = tokens // 2
    half = HALF_ROW // 2
    heads = position_table.shape[0]
    hw = heads * DH
    ff = up_weight.shape[1]
    share = width // 4
    specs, row = [], 0
    for order, rows in PIECES:
        specs.append((row, rows, order))
        row += rows
    plan = (tuple(specs), TURNS, TAIL)
    bits = n_dp.bit_length() - 1
    links = 5 if n_dp == 8 else bits + 3
    total = ff + width + 4 * hw
    cfg = (n_dp, heads, HALF_ROW, chunks, width, ff, share, plan)
    vmem = lambda *shape: pltpu.VMEM(shape, BF16)
    wide = lambda *shape: pltpu.VMEM(shape, F32)
    slots = 3 * chunks
    inbox_rows = total * 7 // 4 + max(bits - 3, 0) * total // 8
    any_spec = pl.BlockSpec(memory_space=pl.ANY)
    scratch = [
        pltpu.VMEM((tokens,), jnp.int32),
        wide(width),
        wide(width),
        wide(ff),
        wide(width),
        wide(width),
        wide(width),
        wide(heads, 2 * REL),
        vmem(tokens, width),
        vmem(width, hw),
        vmem(width, hw),
        vmem(width, hw),
        vmem(hw, width),
        vmem(width, ff),
        vmem(ff, width),
        vmem(pooled, width),
        vmem(hw, width),
        vmem(hw, width),
        vmem(hw, width),
        vmem(HALF_ROW, TOK_ROW),
        wide(chunks, HALF_ROW, TOK_ROW),
        wide(2, HALF_ROW, LANES),
        wide(heads, 64, BAND),
        wide(heads, 64, BAND),
        vmem(pooled, width),
        wide(pooled // 2, width),
        vmem(pooled, hw),
        vmem(hw, pooled),
        vmem(hw, tokens),
        vmem(hw, tokens),
        wide(HALF_ROW, TOK_ROW),
        wide(chunks * heads, HALF_ROW, TOK_ROW),
        vmem(chunks * heads, HALF_ROW, TOK_ROW),
        vmem(HALF_ROW, TOK_ROW),
        vmem(pooled, hw),
        vmem(slots, HALF_ROW, width),
        vmem(slots, half, width),
        vmem(slots, half, width),
        vmem(slots, half, width),
        vmem(pooled, width),
        vmem(pooled, width),
        vmem(pooled, width),
        wide(pooled // 2, width),
        wide(pooled // 2, width),
        wide(pooled // 2, 1),
        wide(HALF_ROW, ff),
        vmem(pooled, ff),
        wide(pooled, ff),
        vmem(pooled, ff),
        wide(pooled // 2, width),
        vmem(pooled, width),
        vmem(pooled, hw),
        vmem(hw, pooled),
        vmem(hw, pooled),
        vmem(hw, tokens),
        vmem(hw, tokens),
        vmem(width, TOK_ROW),
        vmem(chunks, 4, share, TOK_ROW),
        vmem(chunks, 2, share, TOK_ROW),
        vmem(chunks, share, TOK_ROW),
        vmem(chunks, share, TOK_ROW),
        vmem(share, tokens),
        vmem(total, width),
        vmem(total, width),
        vmem(inbox_rows, width),
        wide(6, 8, width),
        wide(SMALL_ROWS, width),
        wide(bits + 1, SMALL_ROWS, width),
        pltpu.SemaphoreType.DMA((16,)),
        pltpu.SemaphoreType.DMA((len(specs) + 3,)),
        pltpu.SemaphoreType.DMA((SENDS,)),
        pltpu.SemaphoreType.DMA((links * len(specs) + RECEIVES,)),
    ]
    pooled_out, input_grad, grads, small = pl.pallas_call(
        partial(fused, cfg),
        name="layer",
        out_shape=(
            jax.ShapeDtypeStruct((pooled, width), BF16),
            jax.ShapeDtypeStruct((share, tokens), BF16),
            jax.ShapeDtypeStruct((total, width), BF16),
            jax.ShapeDtypeStruct((SMALL_ROWS, width), F32),
        ),
        in_specs=[any_spec] * 16,
        out_specs=(any_spec,) * 4,
        scratch_shapes=scratch,
        compiler_params=pltpu.CompilerParams(
            collective_id=0, has_side_effects=True, vmem_limit_bytes=64_000_000
        ),
    )(
        segment_ids,
        first_gain,
        first_shift,
        up_bias,
        down_bias,
        second_gain,
        second_shift,
        position_table,
        hidden_in,
        query_weight.T,
        key_weight.T,
        value_weight.T,
        output_weight,
        up_weight,
        down_weight,
        cotangent,
    )
    return finish(pooled_out, input_grad, grads, small, heads, ff, width)


def solution(mesh):
    return jax.shard_map(
        partial(local, mesh.shape["dp"]),
        mesh=mesh,
        in_specs=(
            P("dp", None),
            P("dp"),
            P(None, "tensor"),
            P(None, "tensor"),
            P(None, "tensor"),
            P("tensor", None),
            P("tensor", None),
            P(),
            P(),
            P(None, "tensor"),
            P("tensor"),
            P("tensor", None),
            P(),
            P(),
            P(),
            P("dp", None),
        ),
        out_specs=(
            P("dp", None),
            P("dp", "tensor"),
            P(None, "tensor"),
            P(None, "tensor"),
            P(None, "tensor"),
            P("tensor", None),
            P("tensor", None),
            P(),
            P(),
            P(None, "tensor"),
            P("tensor"),
            P("tensor", None),
            P(),
            P(),
            P(),
        ),
        check_vma=False,
    )
```
